32 devices in a mesh: dp: 8 (over z, core), blk: 4 (over y, x).
Axes of the slice: x: 2, y: 2, z: 4, core: 2. Of those that a mesh axis runs over, the one named last changes fastest.
Arguments:
- block_in: bfloat16 [8, 1024, 1024], P('dp', 'blk'), may hold values from -6 to 6
- memory: bfloat16 [8, 512, 1024], P('dp', 'blk'), may hold values from -6 to 6
- memory_len: int32 [8], P('dp'), may hold values from 64 to 512, as said below
- cross_mask: int32 [8, 512], P('dp'), may hold values 0 or 1
- buckets: int32 [1024], replicated, may hold values from 0 to 31, never falling along the last dimension, each value on 1 to 256 neighbouring positions
- bias_table: float32 [32, 16], replicated, may hold values from -5 to 5
- norm_self: float32 [1024], replicated, may hold values from 0.5 to 1.5
- w_query: bfloat16 [1024, 1024], replicated, may hold values from -0.1875 to 0.1875
- w_key: bfloat16 [1024, 512], replicated, may hold values from -0.1875 to 0.1875
- w_value: bfloat16 [1024, 512], replicated, may hold values from -0.1875 to 0.1875
- w_out: bfloat16 [1024, 1024], replicated, may hold values from -1.5 to 1.5
- norm_cross: float32 [1024], replicated, may hold values from 0.5 to 1.5
- cross_query: bfloat16 [1024, 1024], replicated, may hold values from -0.1875 to 0.1875
- cross_key: bfloat16 [1024, 512], replicated, may hold values from -0.1875 to 0.1875
- cross_value: bfloat16 [1024, 512], replicated, may hold values from -0.1875 to 0.1875
- cross_out: bfloat16 [1024, 1024], replicated, may hold values from -1.5 to 1.5
- norm_ffn: float32 [1024], replicated, may hold values from 0.5 to 1.5
- w_gate: bfloat16 [1024, 2816], replicated, may hold values from -0.1875 to 0.1875
- w_up: bfloat16 [1024, 2816], replicated, may hold values from -0.1875 to 0.1875
- w_down: bfloat16 [2816, 1024], replicated, may hold values from -0.109375 to 0.109375
- grad_out: bfloat16 [8, 1024, 1024], P('dp', 'blk'), may hold values from -6 to 6
Outputs:
- block_out: bfloat16 [8, 1024, 1024], P('dp', 'blk')
- d_block_in: float32 [8, 1024, 1024], P('dp', 'blk')
- d_memory: float32 [8, 512, 1024], P('dp', 'blk')
- d_bias_table: float32 [32, 16], replicated
- d_norm_self: float32 [1024], replicated
- d_w_query: float32 [1024, 1024], P(('dp', 'blk'))
- d_w_key: float32 [1024, 512], P(('dp', 'blk'))
- d_w_value: float32 [1024, 512], P(('dp', 'blk'))
- d_w_out: float32 [1024, 1024], P(('dp', 'blk'))
- d_norm_cross: float32 [1024], replicated
- d_cross_query: float32 [1024, 1024], P(('dp', 'blk'))
- d_cross_key: float32 [1024, 512], P(('dp', 'blk'))
- d_cross_value: float32 [1024, 512], P(('dp', 'blk'))
- d_cross_out: float32 [1024, 1024], P(('dp', 'blk'))
- d_norm_ffn: float32 [1024], replicated
- d_w_gate: float32 [1024, 2816], P(('dp', 'blk'))
- d_w_up: float32 [1024, 2816], P(('dp', 'blk'))
- d_w_down: float32 [2816, 1024], P(('dp', 'blk'))
The draws below stay inside these ranges and needn't reach their ends.
Inputs may be any that keep to these rules, and one draw needn't show every extreme that they name: `memory_len`: one sequence in every draw has a memory of exactly 512 rows. `buckets`: the bucket never falls as the distance grows; each bucket covers 1 to 256 distances, one exactly 256.
All inputs are finite; a program needn't handle non-finite values. No bound on the sum of `cross_mask` on one device may be relied on, other than what follows from the above.
Results may differ from the reference program's by a relative error of at most 0.025.
Values may be sent and summed in bfloat16 or wider, within the bound.
No kernel may reach another device: no remote copies, remote signals or barrier semaphores. Data moves between devices by JAX's collectives and lax.ppermute only.
A program may use at most 256 MiB of HBM per device.

```python
import math
import jax
import jax.numpy as jnp
import numpy as np
from jax import lax

D = 1024
HEADS = 16
KV_HEADS = 8
HEAD_DIM = 64
FF = 2816
BUCKETS = 32
MEM = 512
SEQ = 1024
NSEQ = 8
MIN_MEM = 64
MAX_RUN = 256


def draw_memory_len(key, part):
    first_key, second_key = jax.random.split(jax.random.fold_in(key, 17))
    lengths = jax.random.randint(first_key, (NSEQ,), MIN_MEM, MEM + 1)
    chosen = jax.random.randint(second_key, (), 0, NSEQ)
    return jnp.where(jnp.arange(NSEQ) == chosen, MEM, lengths).astype(jnp.int32)


def touch_ends(entries, key, least, high):
    longest = entries.shape.index(max(entries.shape))
    spots = []
    for shift in (0, 1):
        where = [jax.random.randint(jax.random.fold_in(key, axis), (), 0, length) for axis, length in enumerate(entries.shape)]
        where[longest] = (where[longest] + shift) % entries.shape[longest]
        spots.append(tuple(where))
    return entries.at[spots[0]].set(least).at[spots[1]].set(high)


def spiked(values, key, source, target, blocks, factor):
    def block_of(axis_at):
        return (jnp.arange(values.shape[axis_at]) // (values.shape[axis_at] // blocks)).reshape((-1,) + (1,) * (values.ndim - 1 - axis_at))

    one_side = jax.random.permutation(key, blocks)[block_of(target)]
    far = (block_of(target) + blocks // 2) % blocks
    return jnp.where((block_of(source) == one_side) | (block_of(source) == far), factor * values, values)


def levels(key, extent, cuts, least, high):
    level, own = 1.0, jax.random.fold_in(key, 6)
    for axis_at, shards_of in cuts:
        steps = jnp.exp(jax.random.uniform(jax.random.fold_in(own, axis_at), (shards_of,), jnp.float32, least / len(cuts), high / len(cuts)))
        level = level * jnp.repeat(steps, extent[axis_at] // shards_of).reshape([-1 if axis == axis_at else 1 for axis in range(len(extent))])
    return level


def profile(number_of, total, limit, lean):
    weights = [(1 << 20) // math.isqrt(grade ** lean) + 1 for grade in range(2, number_of + 1)]
    rest, counts = total - limit - (number_of - 1), [1] * (number_of - 1)
    while rest > 0:
        movable = [i for i in range(number_of - 1) if counts[i] < limit]
        whole, remaining = sum([weights[i] for i in movable]), rest
        for i in movable:
            more = min(limit - counts[i], max(1, remaining * weights[i] // whole), rest)
            counts[i] = counts[i] + more
            rest = rest - more
    return np.array([limit] + counts)


def uneven(stream_key, amount, total, limit, skew):
    if amount == 2:
        one = jax.random.randint(stream_key, (), max(1, total - limit), min(limit, total - 1) + 1)
        return jnp.stack([one, total - one])
    sizes = jnp.asarray(profile(amount, total, limit, skew), jnp.int32)
    pairs = (amount - 1) // 2
    donor, taker = sizes[1:1 + 2 * pairs:2], sizes[2:2 + 2 * pairs:2]
    room = jnp.minimum(donor - 1, limit - taker)
    moved = jax.random.randint(jax.random.fold_in(stream_key, 1), (pairs,), 0, 1 << 20) % (room + 1)
    sizes = sizes.at[1:1 + 2 * pairs:2].set(donor - moved).at[2:2 + 2 * pairs:2].set(taker + moved)
    return sizes[jax.random.permutation(jax.random.fold_in(stream_key, 2), amount)]


def bell_draw(key, shape, width, reach, cuts=(), held_as=jnp.bfloat16):
    loudness = levels(key, shape, cuts, -0.22, 0.18) if cuts else 1.0
    array = jax.random.normal(key, shape, jnp.float32) * width * loudness
    return jnp.minimum(jnp.maximum(array, -reach), reach).astype(held_as)


def noise_with(own_key, dims, scale, most, pieces, heavy, dtype=jnp.bfloat16):
    values = scale * jax.random.normal(own_key, dims, jnp.float32)
    if pieces:
        values = values * levels(own_key, dims, pieces, -0.22, 0.18)
    return jnp.clip(spiked(values, jax.random.fold_in(own_key, 3), *heavy), -most, most).astype(dtype)


def setup_inputs(seed: int = 0) -> dict:
    key_list = jax.random.split(jax.random.key(seed), 22)
    block_in = noise_with(key_list[0], (NSEQ, SEQ, D), 1.0, 6.0, ((0, 8), (1, 4)), (0, 2, 8, 2.0))
    memory = bell_draw(key_list[1], (NSEQ, MEM, D), 1.0, 6.0, ((0, 8), (1, 4)))
    memory_len = draw_memory_len(jax.random.fold_in(key_list[21], 71), 0)
    cross_mask = touch_ends((jax.random.randint(key_list[3], (NSEQ, MEM), 0, 4) < 3).astype(jnp.int32), jax.random.fold_in(key_list[3], 1), 0, 1)
    buckets = jnp.searchsorted(jnp.cumsum(uneven(key_list[4], BUCKETS, SEQ, MAX_RUN, 2)), jnp.arange(SEQ), side="right").astype(jnp.int32)
    bias_table = bell_draw(key_list[5], (BUCKETS, HEADS), 1.0, 5.0, (), jnp.float32)
    norm_self = jnp.clip(1.0 + 0.1 * jax.random.normal(key_list[6], (D,), jnp.float32), 0.5, 1.5)
    w_query = bell_draw(key_list[7], (D, HEADS * HEAD_DIM), D ** -0.5, 0.1875)
    w_key = bell_draw(key_list[8], (D, KV_HEADS * HEAD_DIM), D ** -0.5, 0.1875)
    w_value = bell_draw(key_list[9], (D, KV_HEADS * HEAD_DIM), D ** -0.5, 0.1875)
    w_out = bell_draw(key_list[10], (HEADS * HEAD_DIM, D), HEADS ** -0.5, 1.5)
    norm_cross = jnp.clip(1.0 + 0.1 * jax.random.normal(key_list[11], (D,), jnp.float32), 0.5, 1.5)
    cross_query = bell_draw(key_list[12], (D, HEADS * HEAD_DIM), D ** -0.5, 0.1875)
    cross_key = bell_draw(key_list[13], (D, KV_HEADS * HEAD_DIM), D ** -0.5, 0.1875)
    cross_value = bell_draw(key_list[14], (D, KV_HEADS * HEAD_DIM), D ** -0.5, 0.1875)
    cross_out = bell_draw(key_list[15], (HEADS * HEAD_DIM, D), HEADS ** -0.5, 1.5)
    norm_ffn = jnp.clip(1.0 + 0.1 * jax.random.normal(key_list[16], (D,), jnp.float32), 0.5, 1.5)
    w_gate = bell_draw(key_list[17], (D, FF), D ** -0.5, 0.1875)
    w_up = bell_draw(key_list[18], (D, FF), D ** -0.5, 0.1875)
    w_down = bell_draw(key_list[19], (FF, D), FF ** -0.5, 0.109375)
    grad_out = bell_draw(key_list[20], (NSEQ, SEQ, D), 1.0, 6.0, ((0, 8), (1, 4)))
    return {"block_in": block_in, "memory": memory, "memory_len": memory_len, "cross_mask": cross_mask, "buckets": buckets, "bias_table": bias_table, "norm_self": norm_self, "w_query": w_query, "w_key": w_key, "w_value": w_value, "w_out": w_out, "norm_cross": norm_cross, "cross_query": cross_query, "cross_key": cross_key, "cross_value": cross_value, "cross_out": cross_out, "norm_ffn": norm_ffn, "w_gate": w_gate, "w_up": w_up, "w_down": w_down, "grad_out": grad_out}


PRECISE = lax.Precision.HIGHEST
EPSILON = 1e-06
NEGATIVE = -1e+30

@jax.custom_vjp
def low(v):
    return lax.optimization_barrier(v.astype(jnp.bfloat16)).astype(jnp.float32)

@jax.custom_vjp
def low_back(v):
    return v

def low_keep(v):
    return (low(v), None)

def low_pass(kept, grad):
    return (grad,)

def back_keep(v):
    return (v, None)

def back_low(kept, grad):
    return (low(grad),)
low.defvjp(low_keep, low_pass)
low_back.defvjp(back_keep, back_low)

def matmul(left, right):
    return jnp.dot(left, right, precision=PRECISE)

def rms_scale(stream, gain):
    inverse = lax.rsqrt(lax.optimization_barrier(jnp.mean(stream * stream, axis=-1, keepdims=True)) + EPSILON)
    return stream * inverse * gain

def softmax_rows(scores):
    top_value = lax.optimization_barrier(jnp.max(scores, axis=-1, keepdims=True))
    raised = jnp.exp(scores - top_value)
    return raised / lax.optimization_barrier(jnp.sum(raised, axis=-1, keepdims=True))

def block_forward(params, stream, encoded, allowed, buckets):
    bias_table, norm_self, w_query, w_key, w_value, w_out, norm_cross, cross_query, cross_key, cross_value, cross_out, norm_ffn, w_gate, w_up, w_down = params
    seq_len = stream.shape[0]
    mem_len = encoded.shape[0]
    groups = HEADS // KV_HEADS
    score_scale = HEAD_DIM ** (-0.5)
    self_in = low(rms_scale(stream, norm_self))
    query_rows = low(low_back(matmul(self_in, w_query))).reshape(seq_len, KV_HEADS, groups, HEAD_DIM)
    key_rows = low(low_back(matmul(self_in, w_key))).reshape(seq_len, KV_HEADS, HEAD_DIM)
    value_rows = low(low_back(matmul(self_in, w_value))).reshape(seq_len, KV_HEADS, HEAD_DIM)
    places = jnp.arange(seq_len)
    distance = places[:, None] - places[None, :]
    dist_bias = bias_table[buckets]
    full_bias = jnp.transpose(dist_bias[jnp.maximum(distance, 0)], (2, 0, 1)).reshape(KV_HEADS, groups, seq_len, seq_len)
    scores = jnp.einsum('qkgd,tkd->kgqt', query_rows, key_rows, precision=PRECISE) * score_scale + full_bias
    scores = jnp.where(distance >= 0, low_back(scores), NEGATIVE)
    self_prob = low(softmax_rows(scores))
    self_mix = jnp.einsum('kgqt,tkd->qkgd', self_prob, value_rows, precision=PRECISE)
    self_mix = low(low_back(self_mix)).reshape(seq_len, HEADS * HEAD_DIM)
    after_self = stream + low_back(matmul(self_mix, w_out))
    cross_in = low(rms_scale(after_self, norm_cross))
    cross_q = low(low_back(matmul(cross_in, cross_query))).reshape(seq_len, KV_HEADS, groups, HEAD_DIM)
    mem_key = low(low_back(matmul(encoded, cross_key))).reshape(mem_len, KV_HEADS, HEAD_DIM)
    mem_value = low(low_back(matmul(encoded, cross_value))).reshape(mem_len, KV_HEADS, HEAD_DIM)
    cross_scores = low_back(jnp.einsum('qkgd,mkd->kgqm', cross_q, mem_key, precision=PRECISE) * score_scale)
    cross_scores = jnp.where(allowed[None, None, None, :], cross_scores, NEGATIVE)
    cross_prob = low(softmax_rows(cross_scores))
    cross_mix = jnp.einsum('kgqm,mkd->qkgd', cross_prob, mem_value, precision=PRECISE)
    cross_mix = low(low_back(cross_mix)).reshape(seq_len, HEADS * HEAD_DIM)
    after_cross = after_self + low_back(matmul(cross_mix, cross_out))
    ffn_in = low(rms_scale(after_cross, norm_ffn))
    gate = low_back(matmul(ffn_in, w_gate))
    upward = low_back(matmul(ffn_in, w_up))
    hidden = low(jax.nn.gelu(gate, approximate=True) * upward)
    return after_cross + low_back(matmul(hidden, w_down))

def reference(block_in, memory, memory_len, cross_mask, buckets, bias_table, norm_self, w_query, w_key, w_value, w_out, norm_cross, cross_query, cross_key, cross_value, cross_out, norm_ffn, w_gate, w_up, w_down, grad_out):
    params = tuple((weight.astype(jnp.float32) for weight in (bias_table, norm_self, w_query, w_key, w_value, w_out, norm_cross, cross_query, cross_key, cross_value, cross_out, norm_ffn, w_gate, w_up, w_down)))
    zero_grads = tuple((jnp.zeros_like(weight) for weight in params))
    mem_places = jnp.arange(MEM)

    def per_sequence(totals, inputs):
        stream, encoded, length, mask_row, cotangent = inputs
        allowed = (mem_places == 0) | (mem_places < length) & (mask_row == 1)

        def forward(weights, seq_stream, seq_memory):
            return block_forward(weights, seq_stream, seq_memory, allowed, buckets)
        result, back_fn = jax.vjp(forward, params, stream.astype(jnp.float32), encoded.astype(jnp.float32))
        grads, d_stream, d_encoded = back_fn(cotangent.astype(jnp.float32))
        totals = jax.tree.map(lambda first, second: first + second, totals, grads)
        return (totals, (result.astype(jnp.bfloat16), d_stream, d_encoded))
    totals, stacked = lax.scan(per_sequence, zero_grads, (block_in, memory, memory_len, cross_mask, grad_out))
    block_out, d_block_in, d_memory = stacked
    return (block_out, d_block_in, d_memory, totals[0], totals[1], totals[2], totals[3], totals[4], totals[5], totals[6], totals[7], totals[8], totals[9], totals[10], totals[11], totals[12], totals[13], totals[14])
```

```python
import functools

import jax
import jax.numpy as jnp
from jax import lax
from jax.experimental import pallas as pl
from jax.experimental.pallas import tpu as pltpu
from jax.sharding import PartitionSpec as P

HEAD_DIM = 64
EPSILON = 1e-06
NEGATIVE = -1e30
SCALE = HEAD_DIM ** (-0.5)
LANES = 128
PAIR = 2 * HEAD_DIM
F32 = jnp.float32
BF16 = jnp.bfloat16
VMEM_LIMIT = 56 * 1024 * 1024

NT = (((1,), (1,)), ((), ()))
NN = (((1,), (0,)), ((), ()))
TN = (((0,), (0,)), ((), ()))


def dot32(a, b, dims=NN):
    return lax.dot_general(a, b, dims, preferred_element_type=F32)


def swap(x, axis, bit):
    return lax.ppermute(x, axis, [(i, i ^ bit) for i in range(lax.axis_size(axis))])


def gather_relative(x):
    size = lax.axis_size("blk")
    if size == 4:
        half = x.shape[0] // 2
        one = swap(x, "blk", 1)
        two = swap(x, "blk", 2)
        far_a = swap(one[:half], "blk", 2)
        far_b = swap(two[half:], "blk", 1)
        return jnp.concatenate([x, one, two, far_a, far_b], axis=0)
    bit = 1
    while bit < size:
        x = jnp.concatenate([x, swap(x, "blk", bit)], axis=0)
        bit *= 2
    return x


def add16(a, b):
    return (a.astype(F32) + b.astype(F32)).astype(BF16)


def scatter_relative(x):
    size = lax.axis_size("blk")
    width = x.shape[-1]
    x = x.reshape(size, -1, width)
    if size == 4:
        half = width // 2
        a, b = x[..., :half], x[..., half:]
        from_x = swap(jnp.stack([a[1], a[3]]), "blk", 1)
        from_y = swap(b[2:], "blk", 2)
        a_far = swap(add16(a[2], from_x[1]), "blk", 2)
        b_far = swap(add16(b[1], from_y[1]), "blk", 1)
        left = add16(a[0], from_x[0]).astype(F32) + a_far.astype(F32)
        right = add16(b[0], from_y[0]).astype(F32) + b_far.astype(F32)
        return jnp.concatenate([left, right], axis=-1)
    bit = size // 2
    while bit:
        x = add16(x[:bit], swap(x[bit:], "blk", bit))
        bit //= 2
    return x[0].astype(F32)


def sum_rows(x, first_blk_bit):
    dp_bits = lax.axis_size("dp").bit_length() - 1
    blk_bits = lax.axis_size("blk").bit_length() - 1
    rest = [("dp", k) for k in reversed(range(dp_bits))] + [("blk", k) for k in reversed(range(blk_bits))]
    rows, width = x.shape
    x = x.reshape((2,) * len(rest) + (rows >> len(rest), width))
    order = [("dp", 0)]
    order += [("blk", (first_blk_bit + k) % blk_bits) for k in range(blk_bits)]
    order += [("dp", k) for k in range(1, dp_bits)]
    for axis, k in order:
        place = rest.index((axis, k))
        mine = (lax.axis_index(axis) >> k) & 1
        out = lax.dynamic_index_in_dim(x, 1 - mine, place, keepdims=False)
        keep = lax.dynamic_index_in_dim(x, mine, place, keepdims=False)
        got = swap(out, axis, 1 << k)
        rest.pop(place)
        x = keep.astype(F32) + got.astype(F32)
        if rest:
            x = x.astype(BF16)
    return x


def stacked(ref, kv):
    low = kv * PAIR
    return jnp.concatenate([ref[:, low : low + HEAD_DIM], ref[:, low + HEAD_DIM : low + PAIR]], axis=0)


def unstack(ref, kv, columns):
    length = columns.shape[1] // 2
    rows = columns.T
    low = kv * PAIR
    ref[:, low : low + HEAD_DIM] = rows[:length].astype(ref.dtype)
    ref[:, low + HEAD_DIM : low + PAIR] = rows[length:].astype(ref.dtype)


def spread_bias(bias_ref, tile_ref, kv):
    for g in range(2):
        line = bias_ref[0, 2 * kv + g : 2 * kv + g + 1, :]
        width = line.shape[1]
        tile_ref[g] = pltpu.roll(
            jnp.broadcast_to(line, (LANES, width)), 0, 1, stride=1, stride_axis=0
        )


def bias_tile(tile_ref, start, length):
    heads = []
    for g in range(2):
        heads.append(
            jnp.concatenate(
                [
                    tile_ref[g, :, pl.ds(pl.multiple_of(start - LANES * m, LANES), length)]
                    for m in range(length // LANES)
                ],
                axis=0,
            )
        )
    return jnp.concatenate(heads, axis=1)


def self_forward_kernel(blocks, my_ref, q_ref, k_ref, v_ref, bias_ref, mix_ref, lse_ref, tile_ref, top_ref, sum_ref, acc_ref):
    length = q_ref.shape[0]
    my = my_ref[0]
    for kv in range(2):
        low = kv * HEAD_DIM
        spread_bias(bias_ref, tile_ref, kv)
        qq = stacked(q_ref, kv)
        top_ref[...] = jnp.full_like(top_ref, NEGATIVE)
        sum_ref[...] = jnp.zeros_like(sum_ref)
        acc_ref[...] = jnp.zeros_like(acc_ref)
        for j in range(blocks):
            source = my ^ j

            @pl.when(source <= my)
            def _(j=j, source=source):
                start = length + length * (my - source)
                keys = k_ref[j * length : (j + 1) * length, low : low + HEAD_DIM]
                values = v_ref[j * length : (j + 1) * length, low : low + HEAD_DIM]
                scores = dot32(keys, qq, NT) * SCALE + bias_tile(tile_ref, start, length)
                old = top_ref[...]
                new = jnp.maximum(old, jnp.max(scores, axis=0, keepdims=True))
                weights = jnp.exp(scores - new)
                shrink = jnp.exp(old - new)
                top_ref[...] = new
                sum_ref[...] = sum_ref[...] * shrink + jnp.sum(weights, axis=0, keepdims=True)
                acc_ref[...] = acc_ref[...] * shrink + dot32(values, weights.astype(BF16), TN)

        unstack(mix_ref, kv, acc_ref[...] / sum_ref[...])
        lse_ref[kv] = top_ref[...] + jnp.log(sum_ref[...])


def self_backward_kernel(blocks, my_ref, q_ref, k_ref, v_ref, bias_ref, mix_ref, lse_ref, grad_ref, dq_ref, dk_ref, dv_ref, dbias_ref, tile_ref, diag_ref, acc_ref):
    length = q_ref.shape[0]
    width = bias_ref.shape[2]
    my = my_ref[0]
    for kv in range(2):
        low = kv * HEAD_DIM
        spread_bias(bias_ref, tile_ref, kv)
        qq = stacked(q_ref, kv)
        dd = stacked(grad_ref, kv)
        delta = jnp.sum((dd.astype(F32) * stacked(mix_ref, kv).astype(F32)).T, axis=0, keepdims=True)
        lse = lse_ref[kv]
        diag_ref[...] = jnp.zeros_like(diag_ref)
        acc_ref[...] = jnp.zeros_like(acc_ref)
        for j in range(blocks):
            source = my ^ j
            rows = slice(j * length, (j + 1) * length)

            @pl.when(source <= my)
            def _(rows=rows, source=source):
                start = length + length * (my - source)
                keys = k_ref[rows, low : low + HEAD_DIM]
                values = v_ref[rows, low : low + HEAD_DIM]
                scores = dot32(keys, qq, NT) * SCALE + bias_tile(tile_ref, start, length)
                probs = jnp.exp(scores - lse)
                dv_ref[rows, low : low + HEAD_DIM] = dot32(probs.astype(BF16), dd).astype(BF16)
                change = dot32(values, dd, NT) - delta
                ds = (probs * change).astype(BF16)
                dk_ref[rows, low : low + HEAD_DIM] = (dot32(ds, qq) * SCALE).astype(BF16)
                acc_ref[...] += dot32(keys, ds, TN)
                ds = ds.astype(F32)
                for g in range(2):
                    for m in range(length // LANES):
                        where = pl.ds(pl.multiple_of(start - LANES * m, LANES), length)
                        diag_ref[g, :, where] += ds[m * LANES : (m + 1) * LANES, g * length : (g + 1) * length]

            @pl.when(source > my)
            def _(rows=rows):
                none = jnp.zeros((length, HEAD_DIM), BF16)
                dv_ref[rows, low : low + HEAD_DIM] = none
                dk_ref[rows, low : low + HEAD_DIM] = none

        unstack(dq_ref, kv, acc_ref[...] * SCALE)
        for g in range(2):
            part = diag_ref[g]
            half = LANES // 2
            while half:
                part = part[:half] + pltpu.roll(part[half:], width - half, 1)
                half //= 2
            dbias_ref[0, 2 * kv + g : 2 * kv + g + 1, :] = part


def cross_forward_kernel(allow_ref, q_ref, k_ref, v_ref, mix_ref, lse_ref):
    allow = allow_ref[...] > 0
    for kv in range(2):
        low = kv * HEAD_DIM
        qq = stacked(q_ref, kv)
        scores = dot32(k_ref[:, low : low + HEAD_DIM], qq, NT) * SCALE
        scores = jnp.where(allow, scores, NEGATIVE)
        top = jnp.max(scores, axis=0, keepdims=True)
        raised = jnp.exp(scores - top)
        total = jnp.sum(raised, axis=0, keepdims=True)
        probs = (raised * (1.0 / total)).astype(BF16)
        unstack(mix_ref, kv, dot32(v_ref[:, low : low + HEAD_DIM], probs, TN))
        lse_ref[kv] = top + jnp.log(total)


def cross_backward_kernel(allow_ref, q_ref, k_ref, v_ref, lse_ref, grad_ref, dq_ref, dk_ref, dv_ref):
    allow = allow_ref[...] > 0
    for kv in range(2):
        low = kv * HEAD_DIM
        qq = stacked(q_ref, kv)
        dd = stacked(grad_ref, kv)
        keys = k_ref[:, low : low + HEAD_DIM]
        scores = jnp.where(allow, dot32(keys, qq, NT) * SCALE, NEGATIVE)
        probs = jnp.exp(scores - lse_ref[kv])
        change = dot32(v_ref[:, low : low + HEAD_DIM], dd, NT)
        delta = jnp.sum(probs * change, axis=0, keepdims=True)
        ds = (probs * (change - delta)).astype(BF16)
        dv_ref[:, low : low + HEAD_DIM] = dot32(probs.astype(BF16), dd).astype(BF16)
        dk_ref[:, low : low + HEAD_DIM] = (dot32(ds, qq) * SCALE).astype(BF16)
        unstack(dq_ref, kv, dot32(keys, ds, TN) * SCALE)


def params():
    return pltpu.CompilerParams(dimension_semantics=("arbitrary",), vmem_limit_bytes=VMEM_LIMIT)


def cost(length, keys, heads, passes, moved):
    return pl.CostEstimate(
        flops=2 * length * keys * heads * HEAD_DIM * passes,
        transcendentals=length * keys * heads,
        bytes_accessed=moved,
    )


def lane_block(rows, width):
    return pl.BlockSpec((rows, width), lambda i: (0, i))


def self_forward(my, q, k, v, bias):
    length, keys, kv_heads = q.shape[0], k.shape[0], k.shape[1] // HEAD_DIM
    pairs, width = kv_heads // 2, bias.shape[2]
    lead = pl.BlockSpec((1, 4, width), lambda i: (i, 0, 0))
    return pl.pallas_call(
        functools.partial(self_forward_kernel, keys // length),
        grid=(pairs,),
        in_specs=[
            pl.BlockSpec(memory_space=pltpu.SMEM),
            lane_block(length, 2 * PAIR),
            lane_block(keys, PAIR),
            lane_block(keys, PAIR),
            lead,
        ],
        out_specs=[
            lane_block(length, 2 * PAIR),
            pl.BlockSpec((2, 1, 2 * length), lambda i: (i, 0, 0)),
        ],
        out_shape=[
            jax.ShapeDtypeStruct(q.shape, BF16),
            jax.ShapeDtypeStruct((kv_heads, 1, 2 * length), F32),
        ],
        scratch_shapes=[
            pltpu.VMEM((2, LANES, width), F32),
            pltpu.VMEM((1, 2 * length), F32),
            pltpu.VMEM((1, 2 * length), F32),
            pltpu.VMEM((HEAD_DIM, 2 * length), F32),
        ],
        compiler_params=params(),
        cost_estimate=cost(length, keys, 2 * kv_heads, 2, 4 * q.size + 4 * k.size),
        name="self_forward",
    )(my, q, k, v, bias)


def self_backward(my, q, k, v, bias, mix, lse, grad):
    length, keys, kv_heads = q.shape[0], k.shape[0], k.shape[1] // HEAD_DIM
    pairs, width = kv_heads // 2, bias.shape[2]
    lead = pl.BlockSpec((1, 4, width), lambda i: (i, 0, 0))
    return pl.pallas_call(
        functools.partial(self_backward_kernel, keys // length),
        grid=(pairs,),
        in_specs=[
            pl.BlockSpec(memory_space=pltpu.SMEM),
            lane_block(length, 2 * PAIR),
            lane_block(keys, PAIR),
            lane_block(keys, PAIR),
            lead,
            lane_block(length, 2 * PAIR),
            pl.BlockSpec((2, 1, 2 * length), lambda i: (i, 0, 0)),
            lane_block(length, 2 * PAIR),
        ],
        out_specs=[
            lane_block(length, 2 * PAIR),
            lane_block(keys, PAIR),
            lane_block(keys, PAIR),
            lead,
        ],
        out_shape=[
            jax.ShapeDtypeStruct(q.shape, BF16),
            jax.ShapeDtypeStruct(k.shape, BF16),
            jax.ShapeDtypeStruct(v.shape, BF16),
            jax.ShapeDtypeStruct(bias.shape, F32),
        ],
        scratch_shapes=[
            pltpu.VMEM((2, LANES, width), F32),
            pltpu.VMEM((2, LANES, width), F32),
            pltpu.VMEM((HEAD_DIM, 2 * length), F32),
        ],
        compiler_params=params(),
        cost_estimate=cost(length, keys, 2 * kv_heads, 5, 8 * q.size + 8 * k.size),
        name="self_backward",
    )(my, q, k, v, bias, mix, lse, grad)


def cross_forward(allow, q, k, v):
    length, keys, kv_heads = q.shape[0], k.shape[0], k.shape[1] // HEAD_DIM
    return pl.pallas_call(
        cross_forward_kernel,
        grid=(kv_heads // 2,),
        in_specs=[
            pl.BlockSpec((keys, 1), lambda i: (0, 0)),
            lane_block(length, 2 * PAIR),
            lane_block(keys, PAIR),
            lane_block(keys, PAIR),
        ],
        out_specs=[
            lane_block(length, 2 * PAIR),
            pl.BlockSpec((2, 1, 2 * length), lambda i: (i, 0, 0)),
        ],
        out_shape=[
            jax.ShapeDtypeStruct(q.shape, BF16),
            jax.ShapeDtypeStruct((kv_heads, 1, 2 * length), F32),
        ],
        compiler_params=params(),
        cost_estimate=cost(length, keys, 2 * kv_heads, 2, 4 * q.size + 4 * k.size),
        name="cross_forward",
    )(allow, q, k, v)


def cross_backward(allow, q, k, v, lse, grad):
    length, keys, kv_heads = q.shape[0], k.shape[0], k.shape[1] // HEAD_DIM
    return pl.pallas_call(
        cross_backward_kernel,
        grid=(kv_heads // 2,),
        in_specs=[
            pl.BlockSpec((keys, 1), lambda i: (0, 0)),
            lane_block(length, 2 * PAIR),
            lane_block(keys, PAIR),
            lane_block(keys, PAIR),
            pl.BlockSpec((2, 1, 2 * length), lambda i: (i, 0, 0)),
            lane_block(length, 2 * PAIR),
        ],
        out_specs=[
            lane_block(length, 2 * PAIR),
            lane_block(keys, PAIR),
            lane_block(keys, PAIR),
        ],
        out_shape=[
            jax.ShapeDtypeStruct(q.shape, BF16),
            jax.ShapeDtypeStruct(k.shape, BF16),
            jax.ShapeDtypeStruct(v.shape, BF16),
        ],
        compiler_params=params(),
        cost_estimate=cost(length, keys, 2 * kv_heads, 5, 6 * q.size + 8 * k.size),
        name="cross_backward",
    )(allow, q, k, v, lse, grad)


def inverse_rms(x):
    return lax.rsqrt(jnp.mean(x * x, axis=-1, keepdims=True) + EPSILON)


def norm_back(x, inverse, gain, grad):
    scaled = grad * gain
    along = jnp.mean(scaled * x, axis=-1, keepdims=True)
    d_x = inverse * scaled - x * (inverse * inverse * inverse * along)
    return d_x, jnp.sum(grad * x * inverse, axis=0)


def body(
    block_in,
    memory,
    memory_len,
    cross_mask,
    buckets,
    bias_table,
    norm_self,
    w_query,
    w_key,
    w_value,
    w_out,
    norm_cross,
    cross_query,
    cross_key,
    cross_value,
    cross_out,
    norm_ffn,
    w_gate,
    w_up,
    w_down,
    grad_out,
):
    seq_count, length, model_width = block_in.shape
    assert seq_count == 1
    mem_rows = memory.shape[1]
    mem_total = cross_mask.shape[1]
    blocks = lax.axis_size("blk")
    my = lax.axis_index("blk")
    kv_width = w_key.shape[1]
    head_count = w_query.shape[1] // HEAD_DIM
    bucket_count = bias_table.shape[0]
    my_ref = my.reshape(1).astype(jnp.int32)

    x_all = gather_relative(block_in[0])
    mem_all = gather_relative(memory[0])

    bucket_hot = (buckets[:, None] == jnp.arange(bucket_count)[None, :]).astype(F32)
    dist_bias = lax.dot_general(bias_table, bucket_hot, (((0,), (1,)), ((), ())), precision=lax.Precision.HIGHEST)
    bias = jnp.concatenate([jnp.full((head_count, length), NEGATIVE, F32), dist_bias], axis=1)
    bias = bias.reshape(head_count // 4, 4, -1)

    mem_places = jnp.arange(mem_total)
    allowed = (mem_places == 0) | (mem_places < memory_len[0]) & (cross_mask[0] == 1)
    allow = allowed.astype(F32).reshape(blocks, mem_rows)[my ^ jnp.arange(blocks)].reshape(mem_total, 1)

    stream_all = x_all.astype(F32)
    inv_self_all = inverse_rms(stream_all)
    self_all = (stream_all * inv_self_all * norm_self).astype(BF16)
    stream, inv_self, self_in = stream_all[:length], inv_self_all[:length], self_all[:length]
    query = dot32(self_in, w_query).astype(BF16)
    key = dot32(self_all, w_key).astype(BF16)
    value = dot32(self_all, w_value).astype(BF16)
    self_mix, lse = self_forward(my_ref, query, key, value, bias)
    after_self = stream + dot32(self_mix, w_out)

    inv_cross = inverse_rms(after_self)
    cross_in = (after_self * inv_cross * norm_cross).astype(BF16)
    cross_q = dot32(cross_in, cross_query).astype(BF16)
    mem_key = dot32(mem_all, cross_key).astype(BF16)
    mem_value = dot32(mem_all, cross_value).astype(BF16)
    cross_mix, cross_lse = cross_forward(allow, cross_q, mem_key, mem_value)
    after_cross = after_self + dot32(cross_mix, cross_out)

    inv_ffn = inverse_rms(after_cross)
    ffn_in = (after_cross * inv_ffn * norm_ffn).astype(BF16)
    gate = dot32(ffn_in, w_gate)
    up = dot32(ffn_in, w_up)
    (act, hidden_full), gated_back = jax.vjp(lambda g, u: (jax.nn.gelu(g, approximate=True), jax.nn.gelu(g, approximate=True) * u), gate, up)
    hidden = hidden_full.astype(BF16)
    block_out = (after_cross + dot32(hidden, w_down)).astype(BF16)

    ffn_grad = grad_out[0]
    grad_top = ffn_grad.astype(F32)
    d_hidden = dot32(ffn_grad, w_down, NT)
    gate_full, up_full = gated_back((jnp.zeros_like(act), d_hidden))
    both_grad = jnp.concatenate([gate_full.astype(BF16), up_full.astype(BF16)], axis=1)
    ff = gate.shape[1]
    gate_grad, up_grad = both_grad[:, :ff], both_grad[:, ff:]
    dw_down = sum_rows(dot32(hidden, ffn_grad, TN).astype(BF16), 1)
    dw_both = sum_rows(dot32(ffn_in, both_grad, TN).astype(BF16), 0)
    d_stream, d_gain_ffn = norm_back(after_cross, inv_ffn, norm_ffn, dot32(gate_grad, w_gate, NT) + dot32(up_grad, w_up, NT))
    grad_cross = grad_top + d_stream

    cross_grad = grad_cross.astype(BF16)
    mix_grad = dot32(cross_grad, cross_out, NT).astype(BF16)
    cq_grad, mem_key_part, mem_value_part = cross_backward(allow, cross_q, mem_key, mem_value, cross_lse, mix_grad)
    mem_part = jnp.concatenate([mem_key_part, mem_value_part], axis=1)
    mem_grad = scatter_relative(mem_part).astype(BF16)
    d_memory = dot32(mem_grad[:, :kv_width], cross_key, NT) + dot32(mem_grad[:, kv_width:], cross_value, NT)
    dw_cross = jnp.concatenate(
        [
            dot32(cross_mix, cross_grad, TN).astype(BF16),
            dot32(cross_in, cq_grad, TN).astype(BF16),
            dot32(mem_all, mem_part, TN).astype(BF16),
        ],
        axis=1,
    )
    dw_cross = sum_rows(dw_cross, 1)
    d_stream, d_gain_cross = norm_back(after_self, inv_cross, norm_cross, dot32(cq_grad, cross_query, NT))
    grad_self = grad_cross + d_stream

    self_grad = grad_self.astype(BF16)
    attn_grad = dot32(self_grad, w_out, NT).astype(BF16)
    query_grad, key_part, value_part, bias_grad = self_backward(my_ref, query, key, value, bias, self_mix, lse, attn_grad)
    pair_part = jnp.concatenate([key_part, value_part], axis=1)
    dw_self = jnp.concatenate(
        [
            dot32(self_mix, self_grad, TN).astype(BF16),
            dot32(self_in, query_grad, TN).astype(BF16),
            dot32(self_all, pair_part, TN).astype(BF16),
        ],
        axis=1,
    )
    dw_self = sum_rows(dw_self, 1)
    pair_grad = scatter_relative(pair_part).astype(BF16)
    d_self_norm = (
        dot32(query_grad, w_query, NT)
        + dot32(pair_grad[:, :kv_width], w_key, NT)
        + dot32(pair_grad[:, kv_width:], w_value, NT)
    )
    d_stream, d_gain_self = norm_back(stream, inv_self, norm_self, d_self_norm)
    d_block_in = grad_self + d_stream
    d_table = lax.dot_general(
        bucket_hot,
        bias_grad.reshape(head_count, -1)[:, length:],
        (((0,), (1,)), ((), ())),
        precision=lax.Precision.HIGHEST,
    )
    gain_self, gain_cross, gain_ffn, table_sum = lax.psum((d_gain_self, d_gain_cross, d_gain_ffn, d_table), ("dp", "blk"))
    d = model_width
    return (
        block_out[None],
        d_block_in[None],
        d_memory[None],
        table_sum,
        gain_self,
        dw_self[:, d : 2 * d],
        dw_self[:, 2 * d : 2 * d + kv_width],
        dw_self[:, 2 * d + kv_width :],
        dw_self[:, :d],
        gain_cross,
        dw_cross[:, d : 2 * d],
        dw_cross[:, 2 * d : 2 * d + kv_width],
        dw_cross[:, 2 * d + kv_width :],
        dw_cross[:, :d],
        gain_ffn,
        dw_both[:, :ff],
        dw_both[:, ff:],
        dw_down,
    )


def solution(mesh):
    rows = P("dp", "blk", None)
    split = P(("dp", "blk"), None)
    whole = P()
    return jax.shard_map(
        body,
        mesh=mesh,
        in_specs=(rows, rows, P("dp"), P("dp", None)) + (whole,) * 16 + (rows,),
        out_specs=(rows, rows, rows, whole, whole)
        + (split,) * 4
        + (whole,)
        + (split,) * 4
        + (whole,)
        + (split,) * 3,
        check_vma=False,
    )
```

```python
import functools

import jax
import jax.numpy as jnp
from jax import lax
from jax.experimental import pallas as pl
from jax.experimental.pallas import tpu as pltpu
from jax.sharding import PartitionSpec as P

HEAD_DIM = 64
EPSILON = 1e-06
NEGATIVE = -1e30
SCALE = HEAD_DIM ** (-0.5)
LANES = 128
PAIR = 2 * HEAD_DIM
SLAB = 512
STEP_ELEMENTS = 768 * 1024
F32 = jnp.float32
BF16 = jnp.bfloat16
VMEM_LIMIT = 56 * 1024 * 1024

NT = (((1,), (1,)), ((), ()))
NN = (((1,), (0,)), ((), ()))
TN = (((0,), (0,)), ((), ()))


def dot32(a, b, dims=NN):
    return lax.dot_general(a, b, dims, preferred_element_type=F32)


def swap(x, axis, bit):
    return lax.ppermute(x, axis, [(i, i ^ bit) for i in range(lax.axis_size(axis))])


def gather_relative(x, later):
    size = lax.axis_size("blk")
    if size == 4:
        half = x.shape[0] // 2
        one, two = swap(x, "blk", 1), swap(x, "blk", 2)
        far_a, far_b, later = tie(swap(one[:half], "blk", 2), swap(two[half:], "blk", 1), later)
        return jnp.concatenate([x, one, two, far_a, far_b], axis=0), later
    bit = 1
    while bit < size:
        x = jnp.concatenate([x, swap(x, "blk", bit)], axis=0)
        bit *= 2
    return x, later


def trade(parts, axis, bit):
    return [swap(part, axis, k * bit) for k, part in enumerate(parts) if k]


def tie(*groups):
    return lax.optimization_barrier(groups)


def row_blocks(x, count):
    length = x.shape[0] // count
    return [x[k * length : (k + 1) * length] for k in range(count)]


def column_blocks(x, count):
    width = x.shape[1] // count
    return [x[:, k * width : (k + 1) * width] for k in range(count)]


def add16(a, b):
    return (a.astype(F32) + b.astype(F32)).astype(BF16)


def sum_everywhere(x):
    for axis, low in (("dp", 0), ("blk", 0), ("dp", 1)):
        bits = lax.axis_size(axis).bit_length() - 1
        high = 1 if axis == "dp" and low == 0 else bits
        while low < high:
            if high - low >= 2:
                one, two, three = trade([x] * 4, axis, 1 << low)
                x = (x + one) + (two + three)
                low += 2
            else:
                x = x + swap(x, axis, 1 << low)
                low += 1
    return x


def sum_rows(x, first_blk_bit):
    dp_bits = lax.axis_size("dp").bit_length() - 1
    blk_bits = lax.axis_size("blk").bit_length() - 1
    rest = [("dp", k) for k in reversed(range(dp_bits))] + [("blk", k) for k in reversed(range(blk_bits))]
    rows, width = x.shape
    x = x.reshape((2,) * len(rest) + (rows >> len(rest), width))
    order = [("dp", 0)]
    order += [("blk", (first_blk_bit + k) % blk_bits) for k in range(blk_bits)]
    order += [("dp", k) for k in range(1, dp_bits)]
    for axis, k in order:
        place = rest.index((axis, k))
        mine = (lax.axis_index(axis) >> k) & 1
        out = lax.dynamic_index_in_dim(x, 1 - mine, place, keepdims=False)
        keep = lax.dynamic_index_in_dim(x, mine, place, keepdims=False)
        got = swap(out, axis, 1 << k)
        rest.pop(place)
        x = keep.astype(F32) + got.astype(F32)
        if rest:
            x = x.astype(BF16)
    return x


def stacked(ref, kv):
    low = kv * PAIR
    return jnp.concatenate([ref[:, low : low + HEAD_DIM], ref[:, low + HEAD_DIM : low + PAIR]], axis=0)


def unstack(ref, kv, columns):
    length = columns.shape[1] // 2
    rows = columns.T
    low = kv * PAIR
    ref[:, low : low + HEAD_DIM] = rows[:length].astype(ref.dtype)
    ref[:, low + HEAD_DIM : low + PAIR] = rows[length:].astype(ref.dtype)


def spread_bias(bias_ref, tile_ref):
    heads, width = bias_ref.shape
    for h in range(heads):
        line = jnp.broadcast_to(bias_ref[h : h + 1, :], (LANES, width))
        tile_ref[h] = pltpu.roll(line, 0, 1, stride=1, stride_axis=0)


def bias_tile(tile_ref, kv, start, length):
    heads = []
    for g in range(2):
        parts = [
            tile_ref[2 * kv + g, :, pl.ds(pl.multiple_of(start - LANES * m, LANES), length)]
            for m in range(length // LANES)
        ]
        heads.append(jnp.concatenate(parts, axis=0))
    return jnp.concatenate(heads, axis=1)


def head_columns(kv_local, kv):
    return kv * PAIR, kv_local * PAIR + kv * HEAD_DIM, kv_local * (PAIR + HEAD_DIM) + kv * HEAD_DIM


def two_heads(ref, rows, low):
    return jnp.concatenate([ref[rows, low : low + HEAD_DIM], ref[rows, low + HEAD_DIM : low + PAIR]], axis=0)


def self_forward_kernel(blocks, kv_local, my_ref, qkv_ref, bias_ref, mix_ref, lse_ref, tile_ref, top_ref, sum_ref, acc_ref):
    a = pl.program_id(0)
    length = qkv_ref.shape[0] // blocks
    my = my_ref[0]
    mine = my ^ a

    @pl.when(a == 0)
    def _():
        spread_bias(bias_ref, tile_ref)

    rows = pl.ds(pl.multiple_of(a * length, length), length)
    top_ref[...] = jnp.full_like(top_ref, NEGATIVE)
    sum_ref[...] = jnp.zeros_like(sum_ref)
    acc_ref[...] = jnp.zeros_like(acc_ref)
    for b in range(blocks):
        source = my ^ b
        keys_at = slice(b * length, (b + 1) * length)

        @pl.when(source <= mine)
        def _(source=source, keys_at=keys_at):
            start = length + length * (mine - source)
            for kv in range(kv_local):
                q_at, k_at, v_at = head_columns(kv_local, kv)
                qq = two_heads(qkv_ref, rows, q_at)
                keys = qkv_ref[keys_at, k_at : k_at + HEAD_DIM]
                values = qkv_ref[keys_at, v_at : v_at + HEAD_DIM]
                scores = dot32(keys, qq, NT) * SCALE + bias_tile(tile_ref, kv, start, length)
                old = top_ref[kv]
                new = jnp.maximum(old, jnp.max(scores, axis=0, keepdims=True))
                weights = jnp.exp(scores - new)
                shrink = jnp.exp(old - new)
                top_ref[kv] = new
                sum_ref[kv] = sum_ref[kv] * shrink + jnp.sum(weights, axis=0, keepdims=True)
                acc_ref[kv] = acc_ref[kv] * shrink + dot32(values, weights.astype(BF16), TN)

    for kv in range(kv_local):
        unstack(mix_ref, kv, acc_ref[kv] / sum_ref[kv])
        lse_ref[0, kv] = top_ref[kv] + jnp.log(sum_ref[kv])


def self_backward_kernel(blocks, kv_local, my_ref, qkv_ref, bias_ref, mix_ref, lse_ref, grad_ref, out_ref, dbias_ref, tile_ref, diag_ref, dq_ref, dk_ref, dv_ref):
    a = pl.program_id(0)
    length = qkv_ref.shape[0] // blocks
    width = bias_ref.shape[1]
    my = my_ref[0]
    mine = my ^ a

    @pl.when(a == 0)
    def _():
        spread_bias(bias_ref, tile_ref)
        diag_ref[...] = jnp.zeros_like(diag_ref)
        dk_ref[...] = jnp.zeros_like(dk_ref)
        dv_ref[...] = jnp.zeros_like(dv_ref)

    rows = pl.ds(pl.multiple_of(a * length, length), length)
    every = slice(0, length)
    dq_ref[...] = jnp.zeros_like(dq_ref)
    deltas = []
    for kv in range(kv_local):
        both = two_heads(grad_ref, every, kv * PAIR).astype(F32) * two_heads(mix_ref, every, kv * PAIR).astype(F32)
        deltas.append(jnp.sum(both.T, axis=0, keepdims=True))
    for b in range(blocks):
        source = my ^ b
        keys_at = slice(b * length, (b + 1) * length)

        @pl.when(source <= mine)
        def _(source=source, keys_at=keys_at):
            start = length + length * (mine - source)
            for kv in range(kv_local):
                q_at, k_at, v_at = head_columns(kv_local, kv)
                qq = two_heads(qkv_ref, rows, q_at)
                dd = two_heads(grad_ref, every, q_at)
                keys = qkv_ref[keys_at, k_at : k_at + HEAD_DIM]
                values = qkv_ref[keys_at, v_at : v_at + HEAD_DIM]
                scores = dot32(keys, qq, NT) * SCALE + bias_tile(tile_ref, kv, start, length)
                probs = jnp.exp(scores - lse_ref[0, kv])
                dv_ref[kv, keys_at, :] += dot32(probs.astype(BF16), dd)
                change = dot32(values, dd, NT) - deltas[kv]
                ds = (probs * change).astype(BF16)
                dk_ref[kv, keys_at, :] += dot32(ds, qq)
                dq_ref[kv] += dot32(keys, ds, TN)
                ds = ds.astype(F32)
                for g in range(2):
                    for m in range(length // LANES):
                        where = pl.ds(pl.multiple_of(start - LANES * m, LANES), length)
                        diag_ref[2 * kv + g, :, where] += ds[m * LANES : (m + 1) * LANES, g * length : (g + 1) * length]

    for kv in range(kv_local):
        back = (dq_ref[kv] * SCALE).T.astype(BF16)
        out_ref[rows, kv * PAIR : kv * PAIR + HEAD_DIM] = back[:length]
        out_ref[rows, kv * PAIR + HEAD_DIM : (kv + 1) * PAIR] = back[length:]

    @pl.when(a == blocks - 1)
    def _():
        for kv in range(kv_local):
            _, k_at, v_at = head_columns(kv_local, kv)
            out_ref[:, k_at : k_at + HEAD_DIM] = (dk_ref[kv] * SCALE).astype(BF16)
            out_ref[:, v_at : v_at + HEAD_DIM] = dv_ref[kv].astype(BF16)
        for h in range(2 * kv_local):
            part = diag_ref[h]
            half = LANES // 2
            while half:
                part = part[:half] + pltpu.roll(part[half:], width - half, 1)
                half //= 2
            dbias_ref[h : h + 1, :] = part


def cross_forward_kernel(allow_ref, q_ref, k_ref, v_ref, mix_ref, lse_ref):
    allow = allow_ref[...] > 0
    for kv in range(2):
        low = kv * HEAD_DIM
        qq = stacked(q_ref, kv)
        scores = dot32(k_ref[:, low : low + HEAD_DIM], qq, NT) * SCALE
        scores = jnp.where(allow, scores, NEGATIVE)
        top = jnp.max(scores, axis=0, keepdims=True)
        raised = jnp.exp(scores - top)
        total = jnp.sum(raised, axis=0, keepdims=True)
        probs = (raised * (1.0 / total)).astype(BF16)
        unstack(mix_ref, kv, dot32(v_ref[:, low : low + HEAD_DIM], probs, TN))
        lse_ref[kv] = top + jnp.log(total)


def cross_backward_kernel(allow_ref, q_ref, k_ref, v_ref, lse_ref, grad_ref, dq_ref, dkv_ref):
    allow = allow_ref[...] > 0
    for kv in range(2):
        low = kv * HEAD_DIM
        qq = stacked(q_ref, kv)
        dd = stacked(grad_ref, kv)
        keys = k_ref[:, low : low + HEAD_DIM]
        scores = jnp.where(allow, dot32(keys, qq, NT) * SCALE, NEGATIVE)
        probs = jnp.exp(scores - lse_ref[kv])
        change = dot32(v_ref[:, low : low + HEAD_DIM], dd, NT)
        delta = jnp.sum(probs * change, axis=0, keepdims=True)
        ds = (probs * (change - delta)).astype(BF16)
        dkv_ref[1, :, low : low + HEAD_DIM] = dot32(probs.astype(BF16), dd).astype(BF16)
        dkv_ref[0, :, low : low + HEAD_DIM] = (dot32(ds, qq) * SCALE).astype(BF16)
        unstack(dq_ref, kv, dot32(keys, ds, TN) * SCALE)


TINY = pl.CostEstimate(flops=1, transcendentals=0, bytes_accessed=1)


def params():
    return pltpu.CompilerParams(dimension_semantics=("arbitrary",), vmem_limit_bytes=VMEM_LIMIT)


def cost(length, keys, heads, passes, moved):
    return pl.CostEstimate(
        flops=2 * length * keys * heads * HEAD_DIM * passes,
        transcendentals=length * keys * heads,
        bytes_accessed=moved,
    )


def lane_block(rows, width):
    return pl.BlockSpec((rows, width), lambda i: (0, i))


def self_forward(blocks, my, qkv, bias):
    tokens, columns = qkv.shape
    length, kv_local, width = tokens // blocks, columns // (2 * PAIR), bias.shape[1]
    q_width = kv_local * PAIR
    return pl.pallas_call(
        functools.partial(self_forward_kernel, blocks, kv_local),
        grid=(blocks,),
        in_specs=[
            pl.BlockSpec(memory_space=pltpu.SMEM),
            pl.BlockSpec((tokens, columns), lambda i: (0, 0)),
            pl.BlockSpec(bias.shape, lambda i: (0, 0)),
        ],
        out_specs=[
            pl.BlockSpec((length, q_width), lambda i: (i, 0)),
            pl.BlockSpec((1, kv_local, 1, 2 * length), lambda i: (i, 0, 0, 0)),
        ],
        out_shape=[
            jax.ShapeDtypeStruct((tokens, q_width), BF16),
            jax.ShapeDtypeStruct((blocks, kv_local, 1, 2 * length), F32),
        ],
        scratch_shapes=[
            pltpu.VMEM((2 * kv_local, LANES, width), F32),
            pltpu.VMEM((kv_local, 1, 2 * length), F32),
            pltpu.VMEM((kv_local, 1, 2 * length), F32),
            pltpu.VMEM((kv_local, HEAD_DIM, 2 * length), F32),
        ],
        compiler_params=params(),
        cost_estimate=TINY,
        name="self_forward",
    )(my, qkv, bias)


def self_backward(blocks, my, qkv, bias, mix, lse, grad):
    tokens, columns = qkv.shape
    length, kv_local, width = tokens // blocks, columns // (2 * PAIR), bias.shape[1]
    q_width = kv_local * PAIR
    whole = pl.BlockSpec((tokens, columns), lambda i: (0, 0))
    lines = pl.BlockSpec(bias.shape, lambda i: (0, 0))
    return pl.pallas_call(
        functools.partial(self_backward_kernel, blocks, kv_local),
        grid=(blocks,),
        in_specs=[
            pl.BlockSpec(memory_space=pltpu.SMEM),
            whole,
            lines,
            pl.BlockSpec((length, q_width), lambda i: (i, 0)),
            pl.BlockSpec((1, kv_local, 1, 2 * length), lambda i: (i, 0, 0, 0)),
            pl.BlockSpec((length, q_width), lambda i: (i, 0)),
        ],
        out_specs=[whole, lines],
        out_shape=[
            jax.ShapeDtypeStruct(qkv.shape, BF16),
            jax.ShapeDtypeStruct(bias.shape, F32),
        ],
        scratch_shapes=[
            pltpu.VMEM((2 * kv_local, LANES, width), F32),
            pltpu.VMEM((2 * kv_local, LANES, width), F32),
            pltpu.VMEM((kv_local, HEAD_DIM, 2 * length), F32),
            pltpu.VMEM((kv_local, tokens, HEAD_DIM), F32),
            pltpu.VMEM((kv_local, tokens, HEAD_DIM), F32),
        ],
        compiler_params=params(),
        cost_estimate=TINY,
        name="self_backward",
    )(my, qkv, bias, mix, lse, grad)


def cross_forward(allow, q, k, v):
    length, keys, kv_heads = q.shape[0], k.shape[0], k.shape[1] // HEAD_DIM
    return pl.pallas_call(
        cross_forward_kernel,
        grid=(kv_heads // 2,),
        in_specs=[
            pl.BlockSpec((keys, 1), lambda i: (0, 0)),
            lane_block(length, 2 * PAIR),
            lane_block(keys, PAIR),
            lane_block(keys, PAIR),
        ],
        out_specs=[
            lane_block(length, 2 * PAIR),
            pl.BlockSpec((2, 1, 2 * length), lambda i: (i, 0, 0)),
        ],
        out_shape=[
            jax.ShapeDtypeStruct(q.shape, BF16),
            jax.ShapeDtypeStruct((kv_heads, 1, 2 * length), F32),
        ],
        compiler_params=params(),
        cost_estimate=TINY,
        name="cross_forward",
    )(allow, q, k, v)


def cross_backward(allow, q, k, v, lse, grad):
    length, keys, kv_heads = q.shape[0], k.shape[0], k.shape[1] // HEAD_DIM
    return pl.pallas_call(
        cross_backward_kernel,
        grid=(kv_heads // 2,),
        in_specs=[
            pl.BlockSpec((keys, 1), lambda i: (0, 0)),
            lane_block(length, 2 * PAIR),
            lane_block(keys, PAIR),
            lane_block(keys, PAIR),
            pl.BlockSpec((2, 1, 2 * length), lambda i: (i, 0, 0)),
            lane_block(length, 2 * PAIR),
        ],
        out_specs=[
            lane_block(length, 2 * PAIR),
            pl.BlockSpec((2, keys, PAIR), lambda i: (0, 0, i)),
        ],
        out_shape=[
            jax.ShapeDtypeStruct(q.shape, BF16),
            jax.ShapeDtypeStruct((2,) + k.shape, BF16),
        ],
        compiler_params=params(),
        cost_estimate=TINY,
        name="cross_backward",
    )(allow, q, k, v, lse, grad)


def slab_kernel(kind, later, order_ref, x_ref, g_ref, *refs):
    keep_ref, send_ref, turned_ref, whole_ref = refs[-4:]
    slab = pl.program_id(0)
    kind = jnp.where(slab < later, 0, 1) if kind is None else kind

    @pl.when(slab == 0)
    def _():
        turned_ref[...] = x_ref[...].T

    chunks, rows, width = whole_ref.shape
    whole_ref[...] = dot32(turned_ref[...], g_ref[...]).reshape(chunks, rows, width)
    half = chunks // 2
    for c in range(half):
        keep_ref[c] = whole_ref[order_ref[kind, c]].astype(BF16)
        send_ref[c] = whole_ref[order_ref[kind, half + c]].astype(BF16)


def slabs(order, x, g, total, at, later, buffers, kind=None, slab=SLAB):
    tokens, features = x.shape
    chunks = order.shape[1]
    rows = features // chunks
    if g.ndim == 3:
        count = g.shape[0]
        g_spec = pl.BlockSpec((None, tokens, slab), lambda i: (i, 0, 0))
    else:
        count = g.shape[1] // slab
        g_spec = pl.BlockSpec((tokens, slab), lambda i: (0, i))
    assert at % rows == 0 and features % chunks == 0 and rows % 8 == 0
    out = pl.BlockSpec((chunks // 2, rows, slab), lambda i: (0, at // rows + i, 0))
    shape = jax.ShapeDtypeStruct((chunks // 2, total, slab), BF16)
    extra = [] if buffers is None else list(buffers)
    return pl.pallas_call(
        functools.partial(slab_kernel, kind, later),
        grid=(count,),
        in_specs=[
            pl.BlockSpec(memory_space=pltpu.SMEM),
            pl.BlockSpec((tokens, features), lambda i: (0, 0)),
            g_spec,
        ]
        + [pl.BlockSpec(memory_space=pl.ANY)] * len(extra),
        out_specs=[out, out],
        out_shape=[shape, shape],
        scratch_shapes=[pltpu.VMEM((features, tokens), BF16), pltpu.VMEM((chunks, rows, slab), F32)],
        input_output_aliases={3: 0, 4: 1} if extra else {},
        compiler_params=params(),
        cost_estimate=TINY,
        name="slabs",
    )(order, x, g, *extra)


def sum_pieces(pieces, offset, count, outs):
    places = [(start, start + array.shape[1]) for array, start in pieces]
    cuts = sorted({p for place in places for p in place} | {p for out in outs for p in out})
    width = pieces[0][0].shape[2]
    step = count
    while step % 2 == 0 and step * (places[0][1] - places[0][0]) * width > STEP_ELEMENTS:
        step //= 2
    first = offset // step
    assert first * step == offset
    return pl.pallas_call(
        functools.partial(sum_split_kernel, places, outs, cuts),
        grid=(count // step,),
        in_specs=[pl.BlockSpec((step,) + array.shape[1:], lambda i: (first + i, 0, 0)) for array, _ in pieces],
        out_specs=[pl.BlockSpec((step, high - low, width), lambda i: (i, 0, 0)) for low, high in outs],
        out_shape=[jax.ShapeDtypeStruct((count, high - low, width), BF16) for low, high in outs],
        compiler_params=params(),
        cost_estimate=TINY,
        name="sum_pieces",
    )(*[array for array, _ in pieces])


def add_range(places, pieces, low, high):
    total = None
    for (start, stop), piece in zip(places, pieces):
        if start <= low and high <= stop:
            part = piece[:, low - start : high - start, :].astype(F32)
            total = part if total is None else total + part
    return total


def sum_split_kernel(places, outs, cuts, *refs):
    pieces, results = refs[: len(places)], refs[len(places) :]
    for (low, high), result in zip(outs, results):
        inner = [c for c in cuts if low <= c <= high]
        for a, b in zip(inner[:-1], inner[1:]):
            result[:, a - low : b - low, :] = add_range(places, pieces, a, b).astype(result.dtype)


def finish_kernel(places, outs, *refs):
    pieces, results = refs[: len(places)], refs[len(places) :]
    for row, rows, number, column, start, width in outs:
        total = add_range(places, pieces, row, row + rows)[0]
        results[number][:, column : column + width] = total[:, start : start + width]


def finish(pieces, shapes, outs):
    places = [(start, start + array.shape[1]) for array, start in pieces]
    return pl.pallas_call(
        functools.partial(finish_kernel, places, outs),
        grid=(1,),
        in_specs=[pl.BlockSpec((1,) + array.shape[1:], lambda i: (0, 0, 0)) for array, _ in pieces],
        out_specs=[pl.BlockSpec(shape, lambda i: (0, 0)) for shape in shapes],
        out_shape=[jax.ShapeDtypeStruct(shape, F32) for shape in shapes],
        compiler_params=params(),
        cost_estimate=TINY,
        name="finish",
    )(*[array for array, _ in pieces])


def pair_dot_kernel(x_count, *refs):
    result = refs[-1]
    xs, gs = refs[:x_count], refs[x_count:-1]
    x = jnp.concatenate([ref[...] for ref in xs], axis=0)
    g = jnp.concatenate([ref[...] for ref in gs], axis=0)
    result[...] = dot32(x, g, TN).astype(BF16)


def pair_dot(xs, gs):
    features, width = xs[0].shape[1], gs[0].shape[1]
    return pl.pallas_call(
        functools.partial(pair_dot_kernel, len(xs)),
        grid=(1,),
        in_specs=[pl.BlockSpec(x.shape, lambda i: (0, 0)) for x in list(xs) + list(gs)],
        out_specs=pl.BlockSpec((features, width), lambda i: (0, 0)),
        out_shape=jax.ShapeDtypeStruct((features, width), BF16),
        compiler_params=params(),
        cost_estimate=TINY,
        name="pair_dot",
    )(*xs, *gs)


def place_kernel(share, widths, my_ref, *refs):
    count = len(widths) + 2
    parts, halves, results = refs[:-count], refs[-count : 2 - count], refs[2 - count :]
    per_half = len(parts) // 2
    for j, part in enumerate(parts):
        owner = my_ref[0] ^ j
        for number, result in enumerate(halves):

            @pl.when(owner // per_half == number)
            def _(part=part, result=result, number=number, owner=owner):
                columns = pl.ds(pl.multiple_of((owner - number * per_half) * share, LANES), share)
                result[:, columns] = part[:, :share].astype(F32)

        low = share
        for width, result in zip(widths, results):
            columns = pl.ds(pl.multiple_of(owner * width, LANES), width)
            result[:, columns] = part[:, low : low + width].astype(F32)
            low += width


def place(my, parts, share, widths):
    rows, count = parts[0].shape[0], len(parts)
    shapes = [(rows, count // 2 * share)] * 2 + [(rows, count * width) for width in widths]
    return pl.pallas_call(
        functools.partial(place_kernel, share, widths),
        grid=(1,),
        in_specs=[pl.BlockSpec(memory_space=pltpu.SMEM)] + [pl.BlockSpec(part.shape, lambda i: (0, 0)) for part in parts],
        out_specs=[pl.BlockSpec(shape, lambda i: (0, 0)) for shape in shapes],
        out_shape=[jax.ShapeDtypeStruct(shape, F32) for shape in shapes],
        compiler_params=params(),
        cost_estimate=TINY,
        name="place",
    )(my, *parts)


def exchange_order():
    dp, blk = lax.axis_size("dp"), lax.axis_size("blk")
    dp_bits, blk_bits = dp.bit_length() - 1, blk.bit_length() - 1
    mine = lax.axis_index("dp") * blk + lax.axis_index("blk")
    deep = list(reversed(range(blk_bits + 1, blk_bits + dp_bits)))
    up, down = list(range(blk_bits)), list(reversed(range(blk_bits)))
    tables = []
    for order in (up + deep, down + deep, deep + down, down + deep):
        order = [blk_bits] + order
        table = []
        for place in range(dp * blk):
            relative = 0
            for k, bit in enumerate(order):
                relative |= ((place >> (len(order) - 1 - k)) & 1) << bit
            table.append(relative)
        tables.append(table)
    return jnp.array(tables, jnp.int32) ^ mine.astype(jnp.int32)


def combine_kernel(plan, *refs):
    inputs, results = refs[: -len(plan)], refs[-len(plan) :]
    rows = results[0].shape[1]
    for sources, result in zip(plan, results):
        cuts = sorted({0, rows} | {r for _, row, size in sources for r in (row, row + size)})
        for a, b in zip(cuts[:-1], cuts[1:]):
            total = None
            for number, row, size in sources:
                if row <= a and b <= row + size:
                    part = inputs[number][0, a - row : b - row, :].astype(F32)
                    total = part if total is None else total + part
            result[0, a:b, :] = total.astype(result.dtype)


def combine(pieces, groups):
    plan, specs, arrays = [], [], []
    steps = groups[0][1] - groups[0][0]
    rows, width = max(array.shape[1] + row for array, row in pieces), pieces[0][0].shape[2]
    for low, _ in groups:
        sources = []
        for array, row in pieces:
            sources.append((len(arrays), row, array.shape[1]))
            arrays.append(array)
            specs.append(pl.BlockSpec((1,) + array.shape[1:], lambda i, low=low: (low + i, 0, 0)))
        plan.append(sources)
    out = pl.BlockSpec((1, rows, width), lambda i: (i, 0, 0))
    return pl.pallas_call(
        functools.partial(combine_kernel, plan),
        grid=(steps,),
        in_specs=specs,
        out_specs=[out] * len(groups),
        out_shape=[jax.ShapeDtypeStruct((steps, rows, width), BF16)] * len(groups),
        compiler_params=params(),
        cost_estimate=TINY,
        name="combine",
    )(*arrays)


class Exchange:
    def __init__(self, keep, send):
        self.send, self.pieces = send, [(keep, 0)]

    def core(self):
        self.got = [swap(self.send, "dp", 1)]

    def pack(self):
        self.pieces += [(got, 0) for got in self.got]
        step = self.got[0].shape[0] // 4
        self.out = combine(self.pieces, [(k * step, (k + 1) * step) for k in range(1, 4)])

    def hop(self, axis, bit):
        self.got = trade([None, *self.out], axis, bit)

    def done(self, row=0):
        return [(array, row) for array, _ in self.pieces + [(got, 0) for got in self.got]]


class Halves:
    def __init__(self, keep, send, cut):
        self.cut, self.total = cut, keep.shape[1]
        self.parts = [(0, cut), (cut, self.total)]
        self.pieces, self.send = [(keep, 0)], send

    def core(self):
        self.got = [swap(self.send, "dp", 1)]

    def arrive(self):
        rows = [0] if len(self.got) == 1 else [low for low, _ in self.parts]
        self.pieces += list(zip(self.got, rows))

    def pack(self):
        self.arrive()
        half = self.got[0].shape[0] // 2
        self.out = sum_pieces(self.pieces, half, half, self.parts)

    def hop(self, bits):
        self.got = [swap(out, "blk", bit) for out, bit in zip(self.out, bits)]

    def pack_deep(self):
        self.arrive()
        self.out = combine(self.pieces, [(k, k + 1) for k in range(1, self.got[0].shape[0])])

    def hop_deep(self):
        self.got = trade([None, *self.out], "dp", 2)

    def done(self):
        return self.pieces + [(got, 0) for got in self.got]


def turn_rows(x, rows):
    my = lax.axis_index("blk")
    return jnp.concatenate([lax.dynamic_slice_in_dim(x, (my ^ j) * rows, rows, 0) for j in range(lax.axis_size("blk"))], axis=0)


def inverse_rms(x):
    return lax.rsqrt(jnp.mean(x * x, axis=-1, keepdims=True) + EPSILON)


def norm_back(x, inverse, gain, grad):
    scaled = grad * gain
    along = jnp.mean(scaled * x, axis=-1, keepdims=True)
    d_x = inverse * scaled - x * (inverse * inverse * inverse * along)
    return d_x, jnp.sum(grad * x * inverse, axis=0)


def body(
    block_in,
    memory,
    memory_len,
    cross_mask,
    buckets,
    bias_table,
    norm_self,
    w_query,
    w_key,
    w_value,
    w_out,
    norm_cross,
    cross_query,
    cross_key,
    cross_value,
    cross_out,
    norm_ffn,
    w_gate,
    w_up,
    w_down,
    grad_out,
):
    seq_count, length, model_width = block_in.shape
    assert seq_count == 1
    mem_rows = memory.shape[1]
    mem_total = cross_mask.shape[1]
    blocks = lax.axis_size("blk")
    my = lax.axis_index("blk")
    kv_width = w_key.shape[1]
    head_count = w_query.shape[1] // HEAD_DIM
    bucket_count = bias_table.shape[0]
    my_ref = my.reshape(1).astype(jnp.int32)

    x_all, mem_own = gather_relative(block_in[0], memory[0])
    mem_all = lax.all_gather(mem_own, "blk", axis=0, tiled=True)

    own_heads = head_count // blocks
    own_q, own_kv = own_heads * HEAD_DIM, kv_width // blocks
    turned_qkv = [
        jnp.concatenate(
            [
                lax.dynamic_slice_in_dim(w, (my ^ j) * width, width, 1)
                for w, width in ((w_query, own_q), (w_key, own_kv), (w_value, own_kv))
            ],
            axis=1,
        )
        for j in range(blocks)
    ]
    out_turned = jnp.concatenate([lax.dynamic_slice_in_dim(w_out, (my ^ j) * own_q, own_q, 0) for j in range(blocks)], axis=0)

    bucket_hot = (buckets[:, None] == jnp.arange(bucket_count)[None, :]).astype(F32)
    own_table = lax.dynamic_slice_in_dim(bias_table, my * own_heads, own_heads, 1)
    dist_bias = lax.dot_general(own_table, bucket_hot, (((0,), (1,)), ((), ())), precision=lax.Precision.HIGHEST)
    bias = jnp.concatenate([jnp.full((own_heads, length), NEGATIVE, F32), dist_bias], axis=1)

    mem_places = jnp.arange(mem_total)
    allowed = (mem_places == 0) | (mem_places < memory_len[0]) & (cross_mask[0] == 1)
    allow = allowed.astype(F32).reshape(mem_total, 1)

    stream_all = x_all.astype(F32)
    inv_self_all = inverse_rms(stream_all)
    self_all = (stream_all * inv_self_all * norm_self).astype(BF16)
    stream = block_in[0].astype(F32)
    inv_self = inv_self_all[:length]
    qkv = dot32(self_all, turned_qkv[0]).astype(BF16)
    own_mix, lse = self_forward(blocks, my_ref, qkv, bias)
    mix_parts = row_blocks(own_mix, blocks)
    mem_key = dot32(mem_all, cross_key).astype(BF16)
    mem_value = dot32(mem_all, cross_value).astype(BF16)
    mix_got, mem_key, mem_value = tie(trade(mix_parts, "blk", 1), mem_key, mem_value)
    self_mix = jnp.concatenate([mix_parts[0]] + mix_got, axis=1)
    after_self = stream + dot32(self_mix, out_turned)

    inv_cross = inverse_rms(after_self)
    cross_in = (after_self * inv_cross * norm_cross).astype(BF16)
    cross_q = dot32(cross_in, cross_query).astype(BF16)
    cross_mix, cross_lse = cross_forward(allow, cross_q, mem_key, mem_value)
    after_cross = after_self + dot32(cross_mix, cross_out)

    inv_ffn = inverse_rms(after_cross)
    ffn_in = (after_cross * inv_ffn * norm_ffn).astype(BF16)
    devices = blocks * lax.axis_size("dp")
    d, ff = model_width, w_gate.shape[1]
    share = 2 * ff // blocks
    fast = (
        blocks == 4
        and lax.axis_size("dp") == 8
        and d % (8 * devices) == 0
        and ff % (8 * devices) == 0
        and kv_width == SLAB
        and d % SLAB == 0
        and share % LANES == 0
    )
    gate = dot32(ffn_in, w_gate)
    up = dot32(ffn_in, w_up)
    (act, hidden_full), gated_back = jax.vjp(lambda g, u: (jax.nn.gelu(g, approximate=True), jax.nn.gelu(g, approximate=True) * u), gate, up)
    hidden = hidden_full.astype(BF16)

    ffn_grad = grad_out[0]
    grad_top = ffn_grad.astype(F32)
    d_hidden = dot32(ffn_grad, w_down, NT)
    gate_full, up_full = gated_back((jnp.zeros_like(act), d_hidden))
    gate_grad, up_grad = gate_full.astype(BF16), up_full.astype(BF16)
    if fast:
        order = exchange_order()
        turned = order ^ ((my * (devices // blocks)).astype(jnp.int32))
        small, large = d // devices, ff // devices
        d_slabs = d // SLAB
        half = length // 2
        near = trade([ffn_in] * 3, "blk", 1)
        gate_grad, up_grad, near = tie(gate_grad, up_grad, near)
        both_grad = jnp.concatenate([gate_grad, up_grad], axis=1)
        shares = [lax.dynamic_slice_in_dim(both_grad, (my ^ j) * share, share, 1) for j in range(blocks)]
        shares, hidden = tie(shares, hidden)
        shares_near = trade(shares[:3], "blk", 1)
        keep, send = slabs(order, hidden, ffn_grad, d_slabs * large, 0, 0, None, 3)
    else:
        dw_down = sum_rows(dot32(hidden, ffn_grad, TN).astype(BF16), 1)
        ffn_outs = (
            sum_rows(dot32(ffn_in, gate_grad, TN).astype(BF16), 0),
            sum_rows(dot32(ffn_in, up_grad, TN).astype(BF16), 1),
            dw_down,
        )
    d_ffn_norm = dot32(gate_grad, w_gate, NT) + dot32(up_grad, w_up, NT)
    if fast:
        down_got = swap(send, "dp", 1)
        d_ffn_norm, shares_near, shares[3], near, keep = tie(d_ffn_norm, shares_near, shares[3], near, keep)
        down = Exchange(keep, send)
        down.got = [down_got]
        far = [swap(near[0][:half], "blk", 2), swap(near[1][half:], "blk", 1)]
        share_far = swap(shares[3], "blk", 3)
    d_stream, d_gain_ffn = norm_back(after_cross, inv_ffn, norm_ffn, d_ffn_norm)
    grad_cross = grad_top + d_stream

    cross_grad = grad_cross.astype(BF16)
    mix_grad = dot32(cross_grad, cross_out, NT).astype(BF16)
    cq_grad, mem_part = cross_backward(allow, cross_q, mem_key, mem_value, cross_lse, mix_grad)
    if fast:
        cq_grad, mem_part, share_far, down.got = tie(cq_grad, mem_part, share_far, down.got)
        total = 4 * d_slabs * small
        held = slabs(order, cross_mix, cross_grad, total, 0, total, None)
    d_stream, d_gain_cross = norm_back(after_self, inv_cross, norm_cross, dot32(cq_grad, cross_query, NT))
    grad_self = grad_cross + d_stream

    self_grad = grad_self.astype(BF16)
    grad_parts = column_blocks(dot32(self_grad, out_turned, NT).astype(BF16), blocks)
    if fast:
        grad_parts, mem_part, down.got, far, held = tie(grad_parts, mem_part, down.got, far, held)
    grad_got = trade(grad_parts, "blk", 1)
    if fast:
        down.pack()
        grad_parts[0], down.out = tie(grad_parts[0], down.out)
        down.hop("blk", 1)
        held = slabs(order, cross_in, cq_grad, total, d_slabs * small, total, held)
        held = slabs(order, mem_all, mem_part, total, 2 * d_slabs * small, 0, held)
        cross = Halves(*slabs(turned, self_mix, self_grad, total, 3 * d_slabs * small, 0, held), total // 2)
        cross.core()
        grad_got, keep = tie(grad_got, cross.pieces[0][0])
        cross.pieces = [(keep, 0)]
        wide = pair_dot([ffn_in] + near + far, [shares[0]] + shares_near + [share_far])
        wide, cross.got = tie(wide, cross.got)
        wide = lax.psum_scatter(wide, "dp", scatter_dimension=0, tiled=True)
        cross.pack()
        grad_got, cross.out = tie(grad_got, cross.out)
        cross.hop((1, 2))
    attn_grad = jnp.concatenate([grad_parts[0]] + grad_got, axis=0)
    qkv_grad, bias_grad = self_backward(blocks, my_ref, qkv, bias, own_mix, lse, attn_grad)
    if fast:
        qkv_grad, bias_grad, hidden, cross.got, mem_part, down.got = tie(
            qkv_grad, bias_grad, hidden, cross.got, mem_part, down.got
        )
    qkv_parts = row_blocks(qkv_grad, blocks)
    attn = dot32(self_all, qkv_grad, TN)
    gain_part = jnp.sum(attn * turned_qkv[0].astype(F32), axis=1)
    attn = attn.astype(BF16)
    if fast:
        attn = lax.psum_scatter(attn, "dp", scatter_dimension=0, tiled=True)
    qkv_got = trade(qkv_parts, "blk", 1)
    if fast:
        cross.pack()
        cross.hop((2, 1))
        down.pack()
        down.hop("dp", 2)
        qkv_got, hidden = tie(qkv_got, hidden)
    block_out = (after_cross + dot32(hidden, w_down)).astype(BF16)
    d_self_norm = None
    for part, weight in zip([qkv_parts[0]] + qkv_got, turned_qkv):
        term = dot32(part, weight, NT)
        d_self_norm = term if d_self_norm is None else d_self_norm + term
    d_stream, _ = norm_back(stream, inv_self, norm_self, d_self_norm)
    d_gain_self = gain_part / norm_self
    d_block_in = grad_self + d_stream
    mem_blocks = [lax.dynamic_slice_in_dim(mem_part, (my ^ j) * mem_rows, mem_rows, 1) for j in range(blocks)]
    mem_grad = mem_blocks[0].astype(F32)
    for got in trade(mem_blocks, "blk", 1):
        mem_grad = mem_grad + got.astype(F32)
    mem_grad = mem_grad.astype(BF16)
    d_memory = dot32(mem_grad[0], cross_key, NT) + dot32(mem_grad[1], cross_value, NT)
    d_table = lax.dot_general(bucket_hot, bias_grad[:, length:], (((0,), (1,)), ((), ())), precision=lax.Precision.HIGHEST)
    d_table = lax.dynamic_update_slice_in_dim(jnp.zeros_like(bias_table), d_table, my * own_heads, 1)
    lines = sum_everywhere(
        jnp.concatenate([d_gain_self, d_gain_cross, d_gain_ffn, d_table.reshape(-1)]).reshape(-1, LANES)
    ).reshape(-1)
    gain_self, gain_cross, gain_ffn = lines[:d], lines[d : 2 * d], lines[2 * d : 3 * d]
    table_sum = lines[3 * d :].reshape(bias_table.shape)
    if fast:
        cross.pack_deep()
        cross.hop_deep()
        pieces = cross.done() + down.done(total)
        dealt = jnp.concatenate([wide, attn], axis=1)
        dealt = [lax.dynamic_slice_in_dim(dealt, (my ^ j) * small, small, 0) for j in range(blocks)]
        dealt = [dealt[0]] + trade(dealt, "blk", 1)
        dw_gate, dw_up, dw_q, dw_k, dw_v = place(my_ref, dealt, share, (own_q, own_kv, own_kv))
        shapes = [(small, d), (small, d), (small, kv_width), (small, kv_width), (small, d), (large, d)]
        outs, row = [], 0
        for number, (rows, width) in enumerate(shapes):
            for k in range(width // SLAB):
                outs.append((row, rows, number, k * SLAB, 0, SLAB))
                row += rows
        dw_co, dw_cq, dw_ck, dw_cv, dw_o, dw_down = finish(pieces, shapes, outs)
        ffn_outs = (dw_gate, dw_up, dw_down)
    else:
        dw_co = sum_rows(dot32(cross_mix, cross_grad, TN).astype(BF16), 0)
        dw_cq = sum_rows(dot32(cross_in, cq_grad, TN).astype(BF16), 1)
        dw_ck = sum_rows(dot32(mem_all, mem_part[0], TN).astype(BF16), 0)
        dw_cv = sum_rows(dot32(mem_all, mem_part[1], TN).astype(BF16), 1)
        dw_o = sum_rows(turn_rows(dot32(self_mix, self_grad, TN).astype(BF16), own_q), 0)
        dw_q, dw_k, dw_v = [
            sum_rows(lax.dynamic_update_slice_in_dim(jnp.zeros((d, width), BF16), attn[:, low : low + width // blocks], my * (width // blocks), 1), 0)
            for width, low in ((blocks * own_q, 0), (kv_width, own_q), (kv_width, own_q + own_kv))
        ]
    return (
        block_out[None],
        d_block_in[None],
        d_memory[None],
        table_sum,
        gain_self,
        dw_q,
        dw_k,
        dw_v,
        dw_o,
        gain_cross,
        dw_cq,
        dw_ck,
        dw_cv,
        dw_co,
        gain_ffn,
        *ffn_outs,
    )


def solution(mesh):
    rows = P("dp", "blk", None)
    split = P(("dp", "blk"), None)
    whole = P()
    return jax.shard_map(
        body,
        mesh=mesh,
        in_specs=(rows, rows, P("dp"), P("dp", None)) + (whole,) * 16 + (rows,),
        out_specs=(rows, rows, rows, whole, whole)
        + (split,) * 4
        + (whole,)
        + (split,) * 4
        + (whole,)
        + (split,) * 3,
        check_vma=False,
    )
```

```python
import functools

import jax
import jax.numpy as jnp
from jax import lax
from jax.experimental import pallas as pl
from jax.experimental.pallas import tpu as pltpu
from jax.sharding import PartitionSpec as P

HEAD_DIM = 64
EPSILON = 1e-06
NEGATIVE = -1e30
SCALE = HEAD_DIM ** (-0.5)
LANES = 128
PAIR = 2 * HEAD_DIM
SLAB = 512
STEP_ELEMENTS = 768 * 1024
F32 = jnp.float32
BF16 = jnp.bfloat16
VMEM_LIMIT = 56 * 1024 * 1024

NT = (((1,), (1,)), ((), ()))
NN = (((1,), (0,)), ((), ()))
TN = (((0,), (0,)), ((), ()))


def dot32(a, b, dims=NN):
    return lax.dot_general(a, b, dims, preferred_element_type=F32)


def swap(x, axis, bit):
    return lax.ppermute(x, axis, [(i, i ^ bit) for i in range(lax.axis_size(axis))])


def trade(parts, axis, bit):
    return [swap(part, axis, k * bit) for k, part in enumerate(parts) if k]


def tie(*groups):
    return lax.optimization_barrier(groups)


def row_blocks(x, count):
    length = x.shape[0] // count
    return [x[k * length : (k + 1) * length] for k in range(count)]


def column_blocks(x, count):
    width = x.shape[1] // count
    return [x[:, k * width : (k + 1) * width] for k in range(count)]


def add16(a, b):
    return (a.astype(F32) + b.astype(F32)).astype(BF16)


def sum_axis(x, axis, last, bit=1):
    while bit <= last:
        x = x + swap(x, axis, bit)
        bit *= 2
    return x


def sum_rows(x, first_blk_bit):
    dp_bits = lax.axis_size("dp").bit_length() - 1
    blk_bits = lax.axis_size("blk").bit_length() - 1
    rest = [("dp", k) for k in reversed(range(dp_bits))] + [("blk", k) for k in reversed(range(blk_bits))]
    rows, width = x.shape
    x = x.reshape((2,) * len(rest) + (rows >> len(rest), width))
    order = [("dp", 0)]
    order += [("blk", (first_blk_bit + k) % blk_bits) for k in range(blk_bits)]
    order += [("dp", k) for k in range(1, dp_bits)]
    for axis, k in order:
        place = rest.index((axis, k))
        mine = (lax.axis_index(axis) >> k) & 1
        out = lax.dynamic_index_in_dim(x, 1 - mine, place, keepdims=False)
        keep = lax.dynamic_index_in_dim(x, mine, place, keepdims=False)
        got = swap(out, axis, 1 << k)
        rest.pop(place)
        x = keep.astype(F32) + got.astype(F32)
        if rest:
            x = x.astype(BF16)
    return x


def stacked(ref, kv):
    low = kv * PAIR
    return jnp.concatenate([ref[:, low : low + HEAD_DIM], ref[:, low + HEAD_DIM : low + PAIR]], axis=0)


def unstack(ref, kv, columns):
    length = columns.shape[1] // 2
    rows = columns.T
    low = kv * PAIR
    ref[:, low : low + HEAD_DIM] = rows[:length].astype(ref.dtype)
    ref[:, low + HEAD_DIM : low + PAIR] = rows[length:].astype(ref.dtype)


def spread_bias(bias_ref, tile_ref):
    heads, width = bias_ref.shape
    for h in range(heads):
        line = jnp.broadcast_to(bias_ref[h : h + 1, :], (LANES, width))
        tile_ref[h] = pltpu.roll(line, 0, 1, stride=1, stride_axis=0)


def bias_tile(tile_ref, kv, start, length):
    heads = []
    for g in range(2):
        parts = [
            tile_ref[2 * kv + g, :, pl.ds(pl.multiple_of(start - LANES * m, LANES), length)]
            for m in range(length // LANES)
        ]
        heads.append(jnp.concatenate(parts, axis=0))
    return jnp.concatenate(heads, axis=1)


def head_columns(kv_local, kv):
    return kv * PAIR, kv_local * PAIR + kv * HEAD_DIM, kv_local * (PAIR + HEAD_DIM) + kv * HEAD_DIM


def two_heads(ref, rows, low):
    return jnp.concatenate([ref[rows, low : low + HEAD_DIM], ref[rows, low + HEAD_DIM : low + PAIR]], axis=0)


def self_forward_kernel(blocks, kv_local, my_ref, qkv_ref, bias_ref, *refs):
    mix_refs, (lse_ref, tile_ref, top_ref, sum_ref, acc_ref) = refs[:blocks], refs[blocks:]
    a = pl.program_id(0)
    length = qkv_ref.shape[0] // blocks
    my = my_ref[0]
    mine = my ^ a

    @pl.when(a == 0)
    def _():
        spread_bias(bias_ref, tile_ref)

    rows = pl.ds(pl.multiple_of(a * length, length), length)
    top_ref[...] = jnp.full_like(top_ref, NEGATIVE)
    sum_ref[...] = jnp.zeros_like(sum_ref)
    acc_ref[...] = jnp.zeros_like(acc_ref)
    for b in range(blocks):
        source = my ^ b
        keys_at = slice(b * length, (b + 1) * length)

        @pl.when(source <= mine)
        def _(source=source, keys_at=keys_at):
            start = length + length * (mine - source)
            for kv in range(kv_local):
                q_at, k_at, v_at = head_columns(kv_local, kv)
                qq = two_heads(qkv_ref, rows, q_at)
                keys = qkv_ref[keys_at, k_at : k_at + HEAD_DIM]
                values = qkv_ref[keys_at, v_at : v_at + HEAD_DIM]
                scores = dot32(keys, qq, NT) * SCALE + bias_tile(tile_ref, kv, start, length)
                old = top_ref[kv]
                new = jnp.maximum(old, jnp.max(scores, axis=0, keepdims=True))
                weights = jnp.exp(scores - new)
                shrink = jnp.exp(old - new)
                top_ref[kv] = new
                sum_ref[kv] = sum_ref[kv] * shrink + jnp.sum(weights, axis=0, keepdims=True)
                acc_ref[kv] = acc_ref[kv] * shrink + dot32(values, weights.astype(BF16), TN)

    for kv in range(kv_local):
        lse_ref[0, kv] = top_ref[kv] + jnp.log(sum_ref[kv])
    for b, mix_ref in enumerate(mix_refs):

        @pl.when(a == b)
        def _(mix_ref=mix_ref):
            for kv in range(kv_local):
                unstack(mix_ref, kv, acc_ref[kv] / sum_ref[kv])


def self_backward_kernel(blocks, kv_local, my_ref, qkv_ref, bias_ref, lse_ref, *refs):
    mix_refs, grad_refs, out_refs = refs[:blocks], refs[blocks : 2 * blocks], refs[2 * blocks : 3 * blocks]
    dbias_ref, tile_ref, diag_ref, dq_ref, dk_ref, dv_ref, grad_ref, mix_ref = refs[3 * blocks :]
    a = pl.program_id(0)
    length = qkv_ref.shape[0] // blocks
    width = bias_ref.shape[1]
    my = my_ref[0]
    mine = my ^ a

    @pl.when(a == 0)
    def _():
        spread_bias(bias_ref, tile_ref)
        diag_ref[...] = jnp.zeros_like(diag_ref)
        dk_ref[...] = jnp.zeros_like(dk_ref)
        dv_ref[...] = jnp.zeros_like(dv_ref)

    rows = pl.ds(pl.multiple_of(a * length, length), length)
    every = slice(0, length)
    for b in range(blocks):

        @pl.when(a == b)
        def _(b=b):
            grad_ref[...] = grad_refs[b][...]
            mix_ref[...] = mix_refs[b][...]

    dq_ref[...] = jnp.zeros_like(dq_ref)
    deltas = []
    for kv in range(kv_local):
        both = two_heads(grad_ref, every, kv * PAIR).astype(F32) * two_heads(mix_ref, every, kv * PAIR).astype(F32)
        deltas.append(jnp.sum(both.T, axis=0, keepdims=True))
    for b in range(blocks):
        source = my ^ b
        keys_at = slice(b * length, (b + 1) * length)

        @pl.when(source <= mine)
        def _(source=source, keys_at=keys_at):
            start = length + length * (mine - source)
            for kv in range(kv_local):
                q_at, k_at, v_at = head_columns(kv_local, kv)
                qq = two_heads(qkv_ref, rows, q_at)
                dd = two_heads(grad_ref, every, q_at)
                keys = qkv_ref[keys_at, k_at : k_at + HEAD_DIM]
                values = qkv_ref[keys_at, v_at : v_at + HEAD_DIM]
                scores = dot32(keys, qq, NT) * SCALE + bias_tile(tile_ref, kv, start, length)
                probs = jnp.exp(scores - lse_ref[0, kv])
                dv_ref[kv, keys_at, :] += dot32(probs.astype(BF16), dd)
                change = dot32(values, dd, NT) - deltas[kv]
                ds = (probs * change).astype(BF16)
                dk_ref[kv, keys_at, :] += dot32(ds, qq)
                dq_ref[kv] += dot32(keys, ds, TN)
                ds = ds.astype(F32)
                for g in range(2):
                    for m in range(length // LANES):
                        where = pl.ds(pl.multiple_of(start - LANES * m, LANES), length)
                        diag_ref[2 * kv + g, :, where] += ds[m * LANES : (m + 1) * LANES, g * length : (g + 1) * length]

    for b in range(blocks):

        @pl.when(a == b)
        def _(out_ref=out_refs[b]):
            for kv in range(kv_local):
                back = (dq_ref[kv] * SCALE).T.astype(BF16)
                out_ref[:, kv * PAIR : kv * PAIR + HEAD_DIM] = back[:length]
                out_ref[:, kv * PAIR + HEAD_DIM : (kv + 1) * PAIR] = back[length:]

    @pl.when(a == blocks - 1)
    def _():
        for kv in range(kv_local):
            _, k_at, v_at = head_columns(kv_local, kv)
            for b, out_ref in enumerate(out_refs):
                keys_at = slice(b * length, (b + 1) * length)
                out_ref[:, k_at : k_at + HEAD_DIM] = (dk_ref[kv, keys_at, :] * SCALE).astype(BF16)
                out_ref[:, v_at : v_at + HEAD_DIM] = dv_ref[kv, keys_at, :].astype(BF16)
        for h in range(2 * kv_local):
            part = diag_ref[h]
            half = LANES // 2
            while half:
                part = part[:half] + pltpu.roll(part[half:], width - half, 1)
                half //= 2
            dbias_ref[h : h + 1, :] = part


def cross_forward_kernel(allow_ref, q_ref, k_ref, v_ref, mix_ref, lse_ref):
    allow = allow_ref[...] > 0
    for kv in range(2):
        low = kv * HEAD_DIM
        qq = stacked(q_ref, kv)
        scores = dot32(k_ref[:, low : low + HEAD_DIM], qq, NT) * SCALE
        scores = jnp.where(allow, scores, NEGATIVE)
        top = jnp.max(scores, axis=0, keepdims=True)
        raised = jnp.exp(scores - top)
        total = jnp.sum(raised, axis=0, keepdims=True)
        probs = (raised * (1.0 / total)).astype(BF16)
        unstack(mix_ref, kv, dot32(v_ref[:, low : low + HEAD_DIM], probs, TN))
        lse_ref[kv] = top + jnp.log(total)


def cross_backward_kernel(allow_ref, q_ref, k_ref, v_ref, lse_ref, grad_ref, dq_ref, dkv_ref):
    allow = allow_ref[...] > 0
    for kv in range(2):
        low = kv * HEAD_DIM
        qq = stacked(q_ref, kv)
        dd = stacked(grad_ref, kv)
        keys = k_ref[:, low : low + HEAD_DIM]
        scores = jnp.where(allow, dot32(keys, qq, NT) * SCALE, NEGATIVE)
        probs = jnp.exp(scores - lse_ref[kv])
        change = dot32(v_ref[:, low : low + HEAD_DIM], dd, NT)
        delta = jnp.sum(probs * change, axis=0, keepdims=True)
        ds = (probs * (change - delta)).astype(BF16)
        dkv_ref[1, :, low : low + HEAD_DIM] = dot32(probs.astype(BF16), dd).astype(BF16)
        dkv_ref[0, :, low : low + HEAD_DIM] = (dot32(ds, qq) * SCALE).astype(BF16)
        unstack(dq_ref, kv, dot32(keys, ds, TN) * SCALE)


TINY = pl.CostEstimate(flops=1, transcendentals=0, bytes_accessed=1)


def params():
    return pltpu.CompilerParams(dimension_semantics=("arbitrary",), vmem_limit_bytes=VMEM_LIMIT)


def cost(length, keys, heads, passes, moved):
    return pl.CostEstimate(
        flops=2 * length * keys * heads * HEAD_DIM * passes,
        transcendentals=length * keys * heads,
        bytes_accessed=moved,
    )


def lane_block(rows, width):
    return pl.BlockSpec((rows, width), lambda i: (0, i))


def self_forward(blocks, my, qkv, bias):
    tokens, columns = qkv.shape
    length, kv_local, width = tokens // blocks, columns // (2 * PAIR), bias.shape[1]
    q_width = kv_local * PAIR
    return pl.pallas_call(
        functools.partial(self_forward_kernel, blocks, kv_local),
        grid=(blocks,),
        in_specs=[
            pl.BlockSpec(memory_space=pltpu.SMEM),
            pl.BlockSpec((tokens, columns), lambda i: (0, 0)),
            pl.BlockSpec(bias.shape, lambda i: (0, 0)),
        ],
        out_specs=[pl.BlockSpec((length, q_width), lambda i: (0, 0))] * blocks
        + [pl.BlockSpec((1, kv_local, 1, 2 * length), lambda i: (i, 0, 0, 0))],
        out_shape=[jax.ShapeDtypeStruct((length, q_width), BF16)] * blocks
        + [jax.ShapeDtypeStruct((blocks, kv_local, 1, 2 * length), F32)],
        scratch_shapes=[
            pltpu.VMEM((2 * kv_local, LANES, width), F32),
            pltpu.VMEM((kv_local, 1, 2 * length), F32),
            pltpu.VMEM((kv_local, 1, 2 * length), F32),
            pltpu.VMEM((kv_local, HEAD_DIM, 2 * length), F32),
        ],
        compiler_params=params(),
        cost_estimate=TINY,
        name="self_forward",
    )(my, qkv, bias)


def self_backward(blocks, my, qkv, bias, mixes, lse, grads):
    tokens, columns = qkv.shape
    length, kv_local, width = tokens // blocks, columns // (2 * PAIR), bias.shape[1]
    q_width = kv_local * PAIR
    lines = pl.BlockSpec(bias.shape, lambda i: (0, 0))
    *outs, d_bias = pl.pallas_call(
        functools.partial(self_backward_kernel, blocks, kv_local),
        grid=(blocks,),
        in_specs=[
            pl.BlockSpec(memory_space=pltpu.SMEM),
            pl.BlockSpec((tokens, columns), lambda i: (0, 0)),
            lines,
            pl.BlockSpec((1, kv_local, 1, 2 * length), lambda i: (i, 0, 0, 0)),
        ]
        + [pl.BlockSpec((length, q_width), lambda i: (0, 0))] * (2 * blocks),
        out_specs=[pl.BlockSpec((length, columns), lambda i: (0, 0))] * blocks + [lines],
        out_shape=[jax.ShapeDtypeStruct((length, columns), BF16)] * blocks + [jax.ShapeDtypeStruct(bias.shape, F32)],
        scratch_shapes=[
            pltpu.VMEM((2 * kv_local, LANES, width), F32),
            pltpu.VMEM((2 * kv_local, LANES, width), F32),
            pltpu.VMEM((kv_local, HEAD_DIM, 2 * length), F32),
            pltpu.VMEM((kv_local, tokens, HEAD_DIM), F32),
            pltpu.VMEM((kv_local, tokens, HEAD_DIM), F32),
            pltpu.VMEM((length, q_width), BF16),
            pltpu.VMEM((length, q_width), BF16),
        ],
        compiler_params=params(),
        cost_estimate=TINY,
        name="self_backward",
    )(my, qkv, bias, lse, *mixes, *grads)
    return outs, d_bias


def cross_forward(allow, q, k, v):
    length, keys, kv_heads = q.shape[0], k.shape[0], k.shape[1] // HEAD_DIM
    return pl.pallas_call(
        cross_forward_kernel,
        grid=(kv_heads // 2,),
        in_specs=[
            pl.BlockSpec((keys, 1), lambda i: (0, 0)),
            lane_block(length, 2 * PAIR),
            lane_block(keys, PAIR),
            lane_block(keys, PAIR),
        ],
        out_specs=[
            lane_block(length, 2 * PAIR),
            pl.BlockSpec((2, 1, 2 * length), lambda i: (i, 0, 0)),
        ],
        out_shape=[
            jax.ShapeDtypeStruct(q.shape, BF16),
            jax.ShapeDtypeStruct((kv_heads, 1, 2 * length), F32),
        ],
        compiler_params=params(),
        cost_estimate=TINY,
        name="cross_forward",
    )(allow, q, k, v)


def cross_backward(allow, q, k, v, lse, grad):
    length, keys, kv_heads = q.shape[0], k.shape[0], k.shape[1] // HEAD_DIM
    return pl.pallas_call(
        cross_backward_kernel,
        grid=(kv_heads // 2,),
        in_specs=[
            pl.BlockSpec((keys, 1), lambda i: (0, 0)),
            lane_block(length, 2 * PAIR),
            lane_block(keys, PAIR),
            lane_block(keys, PAIR),
            pl.BlockSpec((2, 1, 2 * length), lambda i: (i, 0, 0)),
            lane_block(length, 2 * PAIR),
        ],
        out_specs=[
            lane_block(length, 2 * PAIR),
            pl.BlockSpec((2, keys, PAIR), lambda i: (0, 0, i)),
        ],
        out_shape=[
            jax.ShapeDtypeStruct(q.shape, BF16),
            jax.ShapeDtypeStruct((2,) + k.shape, BF16),
        ],
        compiler_params=params(),
        cost_estimate=TINY,
        name="cross_backward",
    )(allow, q, k, v, lse, grad)


def slab_kernel(kind, later, x_count, g_count, gained, order_ref, *refs):
    xs, gs = refs[:x_count], refs[x_count : x_count + g_count]
    turned_ref, whole_ref = refs[-2:]
    keep_ref, send_ref = refs[-5:-3] if gained else refs[-4:-2]
    slab = pl.program_id(0)
    kind = jnp.where(slab < later, 0, 1) if kind is None else kind

    @pl.when(slab == 0)
    def _():
        low = 0
        for x in xs:
            turned_ref[low : low + x.shape[1], :] = x[...].T
            low += x.shape[1]

    chunks, rows, width = whole_ref.shape
    g = gs[0][...] if g_count == 1 else jnp.concatenate([ref[...] for ref in gs], axis=0)
    full = dot32(turned_ref[...], g)
    whole_ref[...] = full.reshape(chunks, rows, width)
    half = chunks // 2
    for c in range(half):
        keep_ref[c] = whole_ref[order_ref[kind, c]].astype(BF16)
        send_ref[c] = whole_ref[order_ref[kind, half + c]].astype(BF16)
    if gained:
        refs[-3][...] = jnp.sum(full * refs[x_count + g_count][...].astype(F32), axis=1, keepdims=True)


def slabs(order, x, g, total, at, later, buffers, kind=None, slab=SLAB, weight=None):
    xs = x if isinstance(x, list) else [x]
    tokens, features = xs[0].shape[0], sum(part.shape[1] for part in xs)
    chunks = order.shape[1]
    rows = features // chunks
    gs = g if isinstance(g, list) else [g]
    if len(gs) > 1:
        count, g_specs = 1, whole_blocks(gs)
    elif g.ndim == 3:
        count, g_specs = g.shape[0], [pl.BlockSpec((None, tokens, slab), lambda i: (i, 0, 0))]
    else:
        count, g_specs = g.shape[1] // slab, [pl.BlockSpec((tokens, slab), lambda i: (0, i))]
    assert at % rows == 0 and features % chunks == 0 and rows % 8 == 0
    out = pl.BlockSpec((chunks // 2, rows, slab), lambda i: (0, at // rows + i, 0))
    shapes = [jax.ShapeDtypeStruct((chunks // 2, total, slab), BF16)] * 2
    outs = [out, out]
    extra = [] if buffers is None else list(buffers)
    first = 1 + len(xs) + len(gs)
    weights = []
    if weight is not None:
        weights = [weight]
        shapes.append(jax.ShapeDtypeStruct((features, 1), F32))
        outs.append(pl.BlockSpec((features, 1), lambda i: (0, 0)))
    return pl.pallas_call(
        functools.partial(slab_kernel, kind, later, len(xs), len(gs), weight is not None),
        grid=(count,),
        in_specs=[pl.BlockSpec(memory_space=pltpu.SMEM)]
        + whole_blocks(xs)
        + g_specs
        + whole_blocks(weights)
        + [pl.BlockSpec(memory_space=pl.ANY)] * len(extra),
        out_specs=outs,
        out_shape=shapes,
        scratch_shapes=[pltpu.VMEM((features, tokens), BF16), pltpu.VMEM((chunks, rows, slab), F32)],
        input_output_aliases={first: 0, first + 1: 1} if extra else {},
        compiler_params=params(),
        cost_estimate=TINY,
        name="slabs",
    )(order, *xs, *gs, *weights, *extra)


def cover(*ranges):
    held, row = [], 0
    for low, high in ranges:
        held.append((low, high, row))
        row += high - low
    return held


def add_range(sources, refs, low, high):
    total = None
    for number, segments in sources:
        for start, stop, row in segments:
            if start <= low and high <= stop:
                part = refs[number][:, row + low - start : row + high - start, :].astype(F32)
                total = part if total is None else total + part
    return total


def cut_points(pieces, low, high):
    marks = {low, high}
    for _, segments in pieces:
        marks |= {m for start, stop, _ in segments for m in (start, stop) if low < m < high}
    marks = sorted(marks)
    return list(zip(marks[:-1], marks[1:]))


def total_kernel(plan, *refs):
    inputs, results = refs[: -len(plan)], refs[-len(plan) :]
    for (sources, writes), result in zip(plan, results):
        for row, low, high in writes:
            result[:, row : row + high - low, :] = add_range(sources, inputs, low, high).astype(result.dtype)


def totals(pieces, groups, steps):
    plan, specs, arrays, shapes, outs = [], [], [], [], []
    width = pieces[0][0].shape[2]
    for first, count, ranges in groups:
        step = count // steps
        sources = []
        for array, segments in pieces:
            sources.append((len(arrays), segments))
            arrays.append(array)
            specs.append(pl.BlockSpec((step,) + array.shape[1:], lambda i, low=first // step: (low + i, 0, 0)))
        writes, rows = [], 0
        for low, high in ranges:
            for a, b in cut_points(pieces, low, high):
                writes.append((rows, a, b))
                rows += b - a
        plan.append((sources, writes))
        outs.append(pl.BlockSpec((step, rows, width), lambda i: (i, 0, 0)))
        shapes.append(jax.ShapeDtypeStruct((count, rows, width), BF16))
    return pl.pallas_call(
        functools.partial(total_kernel, plan),
        grid=(steps,),
        in_specs=specs,
        out_specs=outs,
        out_shape=shapes,
        compiler_params=params(),
        cost_estimate=TINY,
        name="totals",
    )(*arrays)


def finish_kernel(sources, outs, dealt, my_ref, *refs):
    inputs, results = refs[: len(sources)], refs[len(sources) :]
    for row, rows, number, column in outs:
        results[number][:, column : column + SLAB] = add_range(sources, inputs, row, row + rows)[0]
    for j, row, rows, parts in dealt:
        block = add_range(sources, inputs, row, row + rows)[0]
        low = 0
        for number, width in parts:
            columns = pl.ds(pl.multiple_of((my_ref[0] ^ j) * width, LANES), width)
            results[number][:, columns] = block[:, low : low + width]
            low += width


def finish(my, pieces, shapes, outs, dealt):
    sources = [(number, segments) for number, (_, segments) in enumerate(pieces)]
    return pl.pallas_call(
        functools.partial(finish_kernel, sources, outs, dealt),
        grid=(1,),
        in_specs=[pl.BlockSpec(memory_space=pltpu.SMEM)]
        + [pl.BlockSpec((1,) + array.shape[1:], lambda i: (0, 0, 0)) for array, _ in pieces],
        out_specs=[pl.BlockSpec(shape, lambda i: (0, 0)) for shape in shapes],
        out_shape=[jax.ShapeDtypeStruct(shape, F32) for shape in shapes],
        compiler_params=params(),
        cost_estimate=TINY,
        name="finish",
    )(my, *[array for array, _ in pieces])


def pair_dot_kernel(x_count, *refs):
    result = refs[-1]
    xs, gs = refs[:x_count], refs[x_count:-1]
    x = jnp.concatenate([ref[...] for ref in xs], axis=0)
    g = jnp.concatenate([ref[...] for ref in gs], axis=0)
    result[...] = dot32(x, g, TN).astype(BF16)


def whole_blocks(arrays):
    return [pl.BlockSpec(a.shape, lambda i, n=a.ndim: (0,) * n) for a in arrays]


def pair_dot(xs, gs):
    features, width = xs[0].shape[1], gs[0].shape[1]
    return pl.pallas_call(
        functools.partial(pair_dot_kernel, len(xs)),
        grid=(1,),
        in_specs=whole_blocks(list(xs) + list(gs)),
        out_specs=pl.BlockSpec((features, width), lambda i: (0, 0)),
        out_shape=jax.ShapeDtypeStruct((features, width), BF16),
        compiler_params=params(),
        cost_estimate=TINY,
        name="pair_dot",
    )(*xs, *gs)


def dot_gain_kernel(x_ref, g_ref, w_ref, out_ref, gain_ref):
    full = dot32(x_ref[...], g_ref[...], TN)
    out_ref[...] = full.astype(BF16)
    gain_ref[...] = jnp.sum(full * w_ref[...].astype(F32), axis=1, keepdims=True)


def dot_gain(x, g, w):
    features, width = w.shape
    return pl.pallas_call(
        dot_gain_kernel,
        grid=(1,),
        in_specs=whole_blocks([x, g, w]),
        out_specs=[pl.BlockSpec((features, width), lambda i: (0, 0)), pl.BlockSpec((features, 1), lambda i: (0, 0))],
        out_shape=[jax.ShapeDtypeStruct((features, width), BF16), jax.ShapeDtypeStruct((features, 1), F32)],
        compiler_params=params(),
        cost_estimate=TINY,
        name="dot_gain",
    )(x, g, w)


def add_norm_kernel(count, has_next, *refs):
    xs, ws = refs[:count], refs[count : 2 * count]
    base_ref, gain_ref = refs[2 * count : 2 * count + 2]
    total = base_ref[...].astype(F32)
    for x, w in zip(xs, ws):
        total = total + dot32(x[...], w[...])
    normed = (total * inverse_rms(total) * gain_ref[...]).astype(BF16)
    if has_next:
        next_ref, total_ref, normed_ref, out_ref = refs[2 * count + 2 :]
        out_ref[...] = dot32(normed, next_ref[...]).astype(BF16)
    else:
        total_ref, normed_ref = refs[2 * count + 2 :]
    total_ref[...] = total
    normed_ref[...] = normed


def add_norm(base, xs, ws, gain, after=None):
    shapes = [jax.ShapeDtypeStruct(base.shape, F32), jax.ShapeDtypeStruct(base.shape, BF16)]
    inputs = [*xs, *ws, base, gain[None]]
    if after is not None:
        inputs.append(after)
        shapes.append(jax.ShapeDtypeStruct((base.shape[0], after.shape[1]), BF16))
    return pl.pallas_call(
        functools.partial(add_norm_kernel, len(xs), after is not None),
        grid=(1,),
        in_specs=whole_blocks(inputs),
        out_specs=whole_blocks(shapes),
        out_shape=shapes,
        compiler_params=params(),
        cost_estimate=TINY,
        name="add_norm",
    )(*inputs)


def norm_grad_kernel(count, nexts, *refs):
    gs, ws = refs[:count], refs[count : 2 * count]
    x_ref, gain_ref, base_ref = refs[2 * count : 2 * count + 3]
    after = refs[2 * count + 3 : 2 * count + 3 + nexts]
    grad_ref, low_ref, gain_grad_ref = refs[2 * count + 3 + nexts : 2 * count + 6 + nexts]
    outs, acc_ref = refs[2 * count + 6 + nexts : -1], refs[-1]
    step = pl.program_id(0)

    @pl.when(step == 0)
    def _():
        acc_ref[...] = jnp.zeros_like(acc_ref)

    part = None
    for g, w in zip(gs, ws):
        term = dot32(g[...], w[...], NT)
        part = term if part is None else part + term
    acc_ref[...] += part

    @pl.when(step == pl.num_programs(0) - 1)
    def _():
        total = acc_ref[...]
        x = x_ref[...].astype(F32)
        d_x, d_gain = norm_back(x, inverse_rms(x), gain_ref[...], total)
        grad = base_ref[...].astype(F32) + d_x
        low = grad.astype(BF16)
        grad_ref[...] = grad
        low_ref[...] = low
        gain_grad_ref[...] = d_gain[None]
        for w, out in zip(after, outs):
            out[...] = dot32(low, w[...], NT).astype(BF16)


def norm_grad(base, gs, ws, x, gain, after, tile):
    length, width = x.shape
    inner = gs[0].shape[1]
    fixed = [x, gain[None], base, *after]
    shapes = [
        jax.ShapeDtypeStruct(x.shape, F32),
        jax.ShapeDtypeStruct(x.shape, BF16),
        jax.ShapeDtypeStruct((1, width), F32),
    ] + [jax.ShapeDtypeStruct((length, w.shape[0]), BF16) for w in after]
    grad, low, d_gain, *outs = pl.pallas_call(
        functools.partial(norm_grad_kernel, len(gs), len(after)),
        grid=(inner // tile,),
        in_specs=[pl.BlockSpec((length, tile), lambda i: (0, i))] * len(gs)
        + [pl.BlockSpec((width, tile), lambda i: (0, i))] * len(ws)
        + whole_blocks(fixed),
        out_specs=whole_blocks(shapes),
        out_shape=shapes,
        scratch_shapes=[pltpu.VMEM((length, width), F32)],
        compiler_params=params(),
        cost_estimate=TINY,
        name="norm_grad",
    )(*gs, *ws, *fixed)
    return grad, low, d_gain[0], outs


def norm_dot_kernel(count, *refs):
    gain_ref, w_ref, normed_ref, out_ref = refs[count:]
    for k, ref in enumerate(refs[:count]):
        length = ref.shape[0]
        rows = slice(k * length, (k + 1) * length)
        x = ref[...].astype(F32)
        normed = (x * inverse_rms(x) * gain_ref[...]).astype(BF16)
        normed_ref[rows, :] = normed
        out_ref[rows, :] = dot32(normed, w_ref[...]).astype(BF16)


def norm_dot(xs, gain, w):
    rows = len(xs) * xs[0].shape[0]
    shapes = [(rows, w.shape[0]), (rows, w.shape[1])]
    return pl.pallas_call(
        functools.partial(norm_dot_kernel, len(xs)),
        grid=(1,),
        in_specs=whole_blocks([*xs, gain, w]),
        out_specs=[pl.BlockSpec(shape, lambda i: (0, 0)) for shape in shapes],
        out_shape=[jax.ShapeDtypeStruct(shape, BF16) for shape in shapes],
        compiler_params=params(),
        cost_estimate=TINY,
        name="norm_dot",
    )(*xs, gain, w)


def turn_kernel(my_ref, x_ref, *refs):
    results, chunk_ref = refs[:-1], refs[-1]
    count = len(results)
    chunk_ref[...] = x_ref[...].astype(F32).T.reshape(chunk_ref.shape)
    for j, result in enumerate(results):
        for k in range(result.shape[0]):
            result[k] = chunk_ref[k * count + (my_ref[0] ^ j)].astype(BF16)


def turn_chunks(my, x, blocks, devices):
    tokens, features = x.shape
    shape = (devices // blocks, features // devices, tokens)
    return pl.pallas_call(
        turn_kernel,
        grid=(1,),
        in_specs=[pl.BlockSpec(memory_space=pltpu.SMEM)] + whole_blocks([x]),
        out_specs=[pl.BlockSpec(shape, lambda i: (0, 0, 0))] * blocks,
        out_shape=[jax.ShapeDtypeStruct(shape, BF16)] * blocks,
        scratch_shapes=[pltpu.VMEM((devices, features // devices, tokens), F32)],
        compiler_params=params(),
        cost_estimate=TINY,
        name="turn_chunks",
    )(my, x)


def turned_dot_kernel(count, my_ref, *refs):
    xs, (g_ref, result) = refs[:count], refs[count:]
    chunks, rows, tokens = xs[0].shape
    total = None
    for j, ref in enumerate(xs):
        x = ref[...].astype(F32).reshape(chunks * rows, tokens).astype(BF16)
        term = dot32(x, g_ref[my_ref[0] ^ j])
        total = term if total is None else total + term
    result[...] = total.reshape(result.shape).astype(BF16)


def turned_dot(my, xs, g):
    chunks, rows, tokens = xs[0].shape
    width = g.shape[1]
    g = g.reshape(len(xs), tokens, width)
    return pl.pallas_call(
        functools.partial(turned_dot_kernel, len(xs)),
        grid=(1,),
        in_specs=[pl.BlockSpec(memory_space=pltpu.SMEM)] + whole_blocks([*xs, g]),
        out_specs=pl.BlockSpec((chunks, rows, width), lambda i: (0, 0, 0)),
        out_shape=jax.ShapeDtypeStruct((chunks, rows, width), BF16),
        compiler_params=params(),
        cost_estimate=TINY,
        name="turned_dot",
    )(my, *xs, g)


def place_kernel(my_ref, *refs):
    parts, results = refs[:-2], refs[-2:]
    per_half = len(parts) // 2
    share = parts[0].shape[1]
    for j, part in enumerate(parts):
        owner = my_ref[0] ^ j
        for number, result in enumerate(results):

            @pl.when(owner // per_half == number)
            def _(part=part, result=result, number=number, owner=owner):
                columns = pl.ds(pl.multiple_of((owner - number * per_half) * share, LANES), share)
                result[:, columns] = part[...].astype(F32)


def place(my, parts):
    shape = (parts[0].shape[0], len(parts) // 2 * parts[0].shape[1])
    return pl.pallas_call(
        place_kernel,
        grid=(1,),
        in_specs=[pl.BlockSpec(memory_space=pltpu.SMEM)] + whole_blocks(parts),
        out_specs=[pl.BlockSpec(shape, lambda i: (0, 0))] * 2,
        out_shape=[jax.ShapeDtypeStruct(shape, F32)] * 2,
        compiler_params=params(),
        cost_estimate=TINY,
        name="place",
    )(my, *parts)


def exchange_order():
    dp, blk = lax.axis_size("dp"), lax.axis_size("blk")
    dp_bits, blk_bits = dp.bit_length() - 1, blk.bit_length() - 1
    mine = lax.axis_index("dp") * blk + lax.axis_index("blk")
    deep = list(range(blk_bits + 1, blk_bits + dp_bits))
    up, down = list(range(blk_bits)), list(reversed(range(blk_bits)))
    tables = []
    for order in (up + deep, down + deep, deep + down):
        order = [blk_bits] + order
        table = []
        for place in range(dp * blk):
            relative = 0
            for k, bit in enumerate(order):
                relative |= ((place >> (len(order) - 1 - k)) & 1) << bit
            table.append(relative)
        tables.append(table)
    return jnp.array(tables, jnp.int32) ^ mine.astype(jnp.int32)


class Halves:
    def __init__(self, keep, got, over_x, over_y):
        self.rows = [(0, keep.shape[1])]
        self.pieces = [(keep, cover(*self.rows)), (got, cover(*self.rows))]
        self.parts, self.chunks = (over_x, over_y), keep.shape[0]

    def pack(self, deep=False):
        half = self.chunks // 2
        parts = [self.rows] if deep else self.parts
        self.out = totals(self.pieces, [(half, half, part) for part in parts], 2 if half > 4 else 1)
        self.chunks = half

    def hop(self, bits):
        self.got = [swap(out, "blk", bit) for out, bit in zip(self.out, bits)]

    def join(self, pieces, end):
        self.pieces += pieces
        self.rows = [(0, end)]

    def hop_deep(self, bit):
        self.got = [swap(self.out[0], "dp", bit)]

    def arrive(self):
        parts = [self.rows] if len(self.got) == 1 else self.parts
        self.pieces += [(array, cover(*part)) for array, part in zip(self.got, parts)]


def turn_rows(x, rows):
    my = lax.axis_index("blk")
    return jnp.concatenate([lax.dynamic_slice_in_dim(x, (my ^ j) * rows, rows, 0) for j in range(lax.axis_size("blk"))], axis=0)


def inverse_rms(x):
    return lax.rsqrt(jnp.mean(x * x, axis=-1, keepdims=True) + EPSILON)


def norm_back(x, inverse, gain, grad):
    scaled = grad * gain
    along = jnp.mean(scaled * x, axis=-1, keepdims=True)
    d_x = inverse * scaled - x * (inverse * inverse * inverse * along)
    return d_x, jnp.sum(grad * (x * inverse), axis=0)


def body(
    block_in,
    memory,
    memory_len,
    cross_mask,
    buckets,
    bias_table,
    norm_self,
    w_query,
    w_key,
    w_value,
    w_out,
    norm_cross,
    cross_query,
    cross_key,
    cross_value,
    cross_out,
    norm_ffn,
    w_gate,
    w_up,
    w_down,
    grad_out,
):
    seq_count, length, model_width = block_in.shape
    assert seq_count == 1
    mem_rows = memory.shape[1]
    mem_total = cross_mask.shape[1]
    blocks = lax.axis_size("blk")
    my = lax.axis_index("blk")
    kv_width = w_key.shape[1]
    head_count = w_query.shape[1] // HEAD_DIM
    bucket_count = bias_table.shape[0]
    my_ref = my.reshape(1).astype(jnp.int32)

    x_parts = [block_in[0]] + trade([block_in[0]] * blocks, "blk", 1)

    own_heads = head_count // blocks
    own_q, own_kv = own_heads * HEAD_DIM, kv_width // blocks
    turned_qkv = [
        jnp.concatenate(
            [
                lax.dynamic_slice_in_dim(w, (my ^ j) * width, width, 1)
                for w, width in ((w_query, own_q), (w_key, own_kv), (w_value, own_kv))
            ],
            axis=1,
        )
        for j in range(blocks)
    ]
    out_turned = [lax.dynamic_slice_in_dim(w_out, (my ^ j) * own_q, own_q, 0) for j in range(blocks)]

    bucket_hot = (buckets[:, None] == jnp.arange(bucket_count)[None, :]).astype(F32)
    own_table = lax.dynamic_slice_in_dim(bias_table, my * own_heads, own_heads, 1)
    dist_bias = lax.dot_general(own_table, bucket_hot, (((0,), (1,)), ((), ())), precision=lax.Precision.HIGHEST)
    bias = jnp.concatenate([jnp.full((own_heads, length), NEGATIVE, F32), dist_bias], axis=1)

    mem_places = jnp.arange(mem_total)
    allowed = (mem_places == 0) | (mem_places < memory_len[0]) & (cross_mask[0] == 1)
    allow = allowed.astype(F32).reshape(blocks, mem_rows)[my ^ jnp.arange(blocks)].reshape(mem_total, 1)

    d_hidden = dot32(grad_out[0], w_down, NT)
    x_parts, mem_own, turned_qkv, out_turned, d_hidden, bias, allow, top_own = tie(
        x_parts, memory[0], turned_qkv, out_turned, d_hidden, bias, allow, grad_out[0]
    )
    top_all = lax.all_gather(top_own, "blk", axis=0, tiled=True)
    mem_all = jnp.concatenate([mem_own] + trade([mem_own] * blocks, "blk", 1), axis=0)
    self_all, qkv = norm_dot(x_parts, norm_self[None], turned_qkv[0])
    *own_mix, lse = self_forward(blocks, my_ref, qkv, bias)
    mem_key = dot32(mem_all, cross_key).astype(BF16)
    mem_value = dot32(mem_all, cross_value).astype(BF16)
    mix_got, mem_key, mem_value = tie(trade(own_mix, "blk", 1), mem_key, mem_value)
    mixes = [own_mix[0]] + mix_got
    after_self, cross_in, cross_q = add_norm(block_in[0], mixes, out_turned, norm_cross, cross_query)
    cross_mix, cross_lse = cross_forward(allow, cross_q, mem_key, mem_value)
    after_cross, ffn_in = add_norm(after_self, [cross_mix], [cross_out], norm_ffn)
    devices = blocks * lax.axis_size("dp")
    d, ff = model_width, w_gate.shape[1]
    share = 2 * ff // blocks
    fast = (
        blocks == 4
        and lax.axis_size("dp") == 8
        and d % (8 * devices) == 0
        and ff % (8 * devices) == 0
        and kv_width == SLAB
        and d % SLAB == 0
        and share % LANES == 0
    )
    gate = dot32(ffn_in, w_gate)
    up = dot32(ffn_in, w_up)
    (act, hidden_full), gated_back = jax.vjp(lambda g, u: (jax.nn.gelu(g, approximate=True), jax.nn.gelu(g, approximate=True) * u), gate, up)
    hidden = hidden_full.astype(BF16)

    ffn_grad = grad_out[0]
    gate_full, up_full = gated_back((jnp.zeros_like(act), d_hidden))
    gate_grad, up_grad = gate_full.astype(BF16), up_full.astype(BF16)
    if fast:
        order = exchange_order()
        turned = order ^ ((my * (devices // blocks)).astype(jnp.int32))
        small, large = d // devices, ff // devices
        d_slabs = d // SLAB
        half = length // 2
        near = trade([ffn_in] * 3, "blk", 1)
        gate_grad, up_grad, top_all, near = tie(gate_grad, up_grad, top_all, near)
        far = [swap(near[0][:half], "blk", 2), swap(near[1][half:], "blk", 1)]
        both_grad = jnp.concatenate([gate_grad, up_grad], axis=1)
        shares = [lax.dynamic_slice_in_dim(both_grad, (my ^ j) * share, share, 1) for j in range(blocks)]
        shares, hidden = tie(shares, hidden)
        shares_near = trade(shares[:3], "blk", 1)
        hidden_parts = turn_chunks(my_ref, hidden, blocks, devices)
    else:
        dw_down = sum_rows(dot32(hidden, ffn_grad, TN).astype(BF16), 1)
        ffn_outs = (
            sum_rows(dot32(ffn_in, gate_grad, TN).astype(BF16), 0),
            sum_rows(dot32(ffn_in, up_grad, TN).astype(BF16), 1),
            dw_down,
        )
    tile = ff // 2 if ff % (2 * LANES) == 0 else ff
    grad_cross, cross_grad, d_gain_ffn, (mix_grad,) = norm_grad(
        ffn_grad, [gate_grad, up_grad], [w_gate, w_up], after_cross, norm_ffn, [cross_out], tile
    )
    if fast:
        mix_grad, shares_near, shares[3], hidden_parts, far = tie(mix_grad, shares_near, shares[3], hidden_parts, far)
        ffn_parts = [ffn_in] + near + far
        share_far = swap(shares[3], "blk", 3)
        hidden_got = trade(hidden_parts, "blk", 1)
    block_out = (after_cross + dot32(hidden, w_down)).astype(BF16)
    cq_grad, mem_part = cross_backward(allow, cross_q, mem_key, mem_value, cross_lse, mix_grad)
    if fast:
        total = 4 * d_slabs * small
        held = slabs(order, cross_mix, cross_grad, total, 0, total, None)
        cq_grad, mem_part, share_far, hidden_got, block_out, held = tie(cq_grad, mem_part, share_far, hidden_got, block_out, held)
    grad_self, self_grad, d_gain_cross, grad_parts = norm_grad(
        grad_cross, [cq_grad], [cross_query], after_self, norm_cross, out_turned, d
    )
    grad_got = trade(grad_parts, "blk", 1)
    if fast:
        shares_near, held, cq_late, self_late = tie(shares_near, held, cq_grad, self_grad)
        wide = pair_dot(ffn_parts, [shares[0]] + shares_near + [share_far])
        grad_got, wide, held, mem_late = tie(grad_got, wide, held, mem_part)
        wide = lax.psum_scatter(wide, "dp", scatter_dimension=0, tiled=True)
        held = slabs(order, cross_in, cq_late, total, d_slabs * small, total, held)
        held = slabs(order, mem_all, mem_late, total, 2 * d_slabs * small, 0, held)
        keep, send = slabs(turned, mixes, self_late, total, 3 * d_slabs * small, 0, held)
        got = swap(send, "dp", 1)
        hidden_got, keep = tie(hidden_got, keep)
        down = turned_dot(my_ref, [hidden_parts[0]] + hidden_got, top_all)
        down, got = tie(down, got)
        cross = Halves(keep, got, [(0, total // 2)], [(total // 2, total)])
        cross.pack()
        grad_got, cross.out = tie(grad_got, cross.out)
        cross.hop((1, 2))
    qkv_parts, bias_grad = self_backward(blocks, my_ref, qkv, bias, own_mix, lse, [grad_parts[0]] + grad_got)
    d_table = lax.dot_general(bucket_hot, bias_grad[:, length:], (((0,), (1,)), ((), ())), precision=lax.Precision.HIGHEST)
    d_table = lax.dynamic_update_slice_in_dim(jnp.zeros_like(bias_table), d_table, my * own_heads, 1)
    if fast:
        qkv_parts, mem_part, cross.got, wide = tie(qkv_parts, mem_part, cross.got, wide)
        down = lax.psum_scatter(down, "dp", scatter_dimension=0, tiled=True)
        cross.arrive()
        cross.pack()
        qkv_parts, cross.out = tie(qkv_parts, cross.out)
        cross.hop((2, 1))
        own = own_q + 2 * own_kv
        keep, send, gain_part = slabs(order, self_all, qkv_parts, small, 0, 0, None, 2, own, turned_qkv[0])
        gain_part = gain_part[:, 0]
        view = (-1, blocks * small, own)
        got = swap(send, "dp", 1)
        wides = [lax.dynamic_slice_in_dim(wide, (my ^ j) * small, small, 0) for j in range(blocks)]
        wides, got = tie(wides, got)
        sides = [(keep.reshape(view), cover((0, view[1]))), (got.reshape(view), cover((0, view[1])))]
        sides = totals(sides, [(0, cross.chunks, [(j * small, (j + 1) * small)]) for j in range(blocks)], 1)
        sides = [sides[0]] + trade(sides, "blk", 1)
        gain_part, cross.got, sides = tie(gain_part, cross.got, sides)
        cross.arrive()
        cross.join([(side, cover((total + j * small, total + (j + 1) * small))) for j, side in enumerate(sides)], total + view[1])
        cross.pack(True)
        gain_part, qkv_parts, cross.out, wides, d_table = tie(gain_part, qkv_parts, cross.out, wides, d_table)
        cross.hop_deep(2)
    else:
        attn, gain_part = dot_gain(self_all, jnp.concatenate(qkv_parts, axis=0), turned_qkv[0])
        gain_part = gain_part[:, 0]
    d_gain_self = gain_part / norm_self
    qkv_got = trade(qkv_parts, "blk", 1)
    d_block_in, _, _, _ = norm_grad(
        grad_self, [qkv_parts[0]] + qkv_got, turned_qkv, block_in[0], norm_self, [], own_q + 2 * own_kv
    )
    lines = jnp.concatenate([d_gain_self, d_gain_cross, d_gain_ffn, d_table.reshape(-1)]).reshape(-1, LANES)
    if fast:
        lines = sum_axis(sum_axis(lines, "dp", 1), "blk", blocks // 2)
        d_block_in, cross.got, mem_part, lines, down = tie(d_block_in, cross.got, mem_part, lines, down)
        cross.arrive()
        cross.pack(True)
        mem_part, lines, wides, cross.out = tie(mem_part, lines, wides, cross.out)
        cross.hop_deep(4)
        wides = [wides[0]] + trade(wides, "blk", 1)
    mem_blocks = mem_part.reshape(2, blocks, mem_rows, kv_width)
    bit = blocks // 2
    while bit:
        mem_blocks = add16(mem_blocks[:, :bit], swap(mem_blocks[:, bit:], "blk", bit))
        bit //= 2
    mem_grad = mem_blocks[:, 0]
    d_memory = dot32(mem_grad[0], cross_key, NT) + dot32(mem_grad[1], cross_value, NT)
    if fast:
        cross.arrive()
        lines = sum_axis(lines, "dp", lax.axis_size("dp") // 2, 2).reshape(-1)
    else:
        lines = sum_axis(sum_axis(lines, "dp", lax.axis_size("dp") // 2), "blk", blocks // 2).reshape(-1)
    gain_self, gain_cross, gain_ffn = lines[:d], lines[d : 2 * d], lines[2 * d : 3 * d]
    table_sum = lines[3 * d :].reshape(bias_table.shape)
    if fast:
        dw_gate, dw_up = place(my_ref, wides)
        shapes = [(small, d), (small, d), (small, kv_width), (small, kv_width), (small, d)]
        outs, row = [], 0
        for number, (_, width) in enumerate(shapes):
            for k in range(width // SLAB):
                outs.append((row, small, number, k * SLAB))
                row += small
        shapes += [(small, d), (small, kv_width), (small, kv_width)]
        dealt = [(j, row + j * small, small, ((5, own_q), (6, own_kv), (7, own_kv))) for j in range(blocks)]
        dw_co, dw_cq, dw_ck, dw_cv, dw_o, dw_q, dw_k, dw_v = finish(my_ref, cross.pieces, shapes, outs, dealt)
        dw_down = down[0].astype(F32)
        ffn_outs = (dw_gate, dw_up, dw_down)
    else:
        dw_co = sum_rows(dot32(cross_mix, cross_grad, TN).astype(BF16), 0)
        dw_cq = sum_rows(dot32(cross_in, cq_grad, TN).astype(BF16), 1)
        dw_ck = sum_rows(dot32(mem_all, mem_part[0], TN).astype(BF16), 0)
        dw_cv = sum_rows(dot32(mem_all, mem_part[1], TN).astype(BF16), 1)
        dw_o = sum_rows(turn_rows(dot32(jnp.concatenate(mixes, axis=1), self_grad, TN).astype(BF16), own_q), 0)
        dw_q, dw_k, dw_v = [
            sum_rows(lax.dynamic_update_slice_in_dim(jnp.zeros((d, width), BF16), attn[:, low : low + width // blocks], my * (width // blocks), 1), 0)
            for width, low in ((blocks * own_q, 0), (kv_width, own_q), (kv_width, own_q + own_kv))
        ]
    return (
        block_out[None],
        d_block_in[None],
        d_memory[None],
        table_sum,
        gain_self,
        dw_q,
        dw_k,
        dw_v,
        dw_o,
        gain_cross,
        dw_cq,
        dw_ck,
        dw_cv,
        dw_co,
        gain_ffn,
        *ffn_outs,
    )


def solution(mesh):
    rows = P("dp", "blk", None)
    split = P(("dp", "blk"), None)
    whole = P()
    return jax.shard_map(
        body,
        mesh=mesh,
        in_specs=(rows, rows, P("dp"), P("dp", None)) + (whole,) * 16 + (rows,),
        out_specs=(rows, rows, rows, whole, whole)
        + (split,) * 4
        + (whole,)
        + (split,) * 4
        + (whole,)
        + (split,) * 3,
        check_vma=False,
    )
```

```python
import functools

import jax
import jax.numpy as jnp
from jax import lax
from jax.experimental import pallas as pl
from jax.experimental.pallas import tpu as pltpu
from jax.sharding import PartitionSpec as P

HEAD_DIM = 64
EPSILON = 1e-06
NEGATIVE = -1e30
SCALE = HEAD_DIM ** (-0.5)
LANES = 128
PAIR = 2 * HEAD_DIM
SLAB = 512
STEP_ELEMENTS = 768 * 1024
F32 = jnp.float32
BF16 = jnp.bfloat16
VMEM_LIMIT = 56 * 1024 * 1024

NT = (((1,), (1,)), ((), ()))
NN = (((1,), (0,)), ((), ()))
TN = (((0,), (0,)), ((), ()))


def dot32(a, b, dims=NN):
    return lax.dot_general(a, b, dims, preferred_element_type=F32)


def swap(x, axis, bit):
    return lax.ppermute(x, axis, [(i, i ^ bit) for i in range(lax.axis_size(axis))])


def trade(parts, axis, bit):
    return [swap(part, axis, k * bit) for k, part in enumerate(parts) if k]


def tie(*groups):
    return lax.optimization_barrier(groups)


def row_blocks(x, count):
    length = x.shape[0] // count
    return [x[k * length : (k + 1) * length] for k in range(count)]


def column_blocks(x, count):
    width = x.shape[1] // count
    return [x[:, k * width : (k + 1) * width] for k in range(count)]


def add16(a, b):
    return (a.astype(F32) + b.astype(F32)).astype(BF16)


def sum_axis(x, axis, last, bit=1):
    while bit <= last:
        x = x + swap(x, axis, bit)
        bit *= 2
    return x


def sum_rows(x, first_blk_bit):
    dp_bits = lax.axis_size("dp").bit_length() - 1
    blk_bits = lax.axis_size("blk").bit_length() - 1
    rest = [("dp", k) for k in reversed(range(dp_bits))] + [("blk", k) for k in reversed(range(blk_bits))]
    rows, width = x.shape
    x = x.reshape((2,) * len(rest) + (rows >> len(rest), width))
    order = [("dp", 0)]
    order += [("blk", (first_blk_bit + k) % blk_bits) for k in range(blk_bits)]
    order += [("dp", k) for k in range(1, dp_bits)]
    for axis, k in order:
        place = rest.index((axis, k))
        mine = (lax.axis_index(axis) >> k) & 1
        out = lax.dynamic_index_in_dim(x, 1 - mine, place, keepdims=False)
        keep = lax.dynamic_index_in_dim(x, mine, place, keepdims=False)
        got = swap(out, axis, 1 << k)
        rest.pop(place)
        x = keep.astype(F32) + got.astype(F32)
        if rest:
            x = x.astype(BF16)
    return x


def stacked(ref, kv):
    low = kv * PAIR
    return jnp.concatenate([ref[:, low : low + HEAD_DIM], ref[:, low + HEAD_DIM : low + PAIR]], axis=0)


def unstack(ref, kv, columns):
    length = columns.shape[1] // 2
    rows = columns.T
    low = kv * PAIR
    ref[:, low : low + HEAD_DIM] = rows[:length].astype(ref.dtype)
    ref[:, low + HEAD_DIM : low + PAIR] = rows[length:].astype(ref.dtype)


def spread_bias(bias_ref, tile_ref):
    heads, width = bias_ref.shape
    for h in range(heads):
        line = jnp.broadcast_to(bias_ref[h : h + 1, :], (LANES, width))
        tile_ref[h] = pltpu.roll(line, 0, 1, stride=1, stride_axis=0)


def bias_tile(tile_ref, kv, start, length):
    heads = []
    for g in range(2):
        parts = [
            tile_ref[2 * kv + g, :, pl.ds(pl.multiple_of(start - LANES * m, LANES), length)]
            for m in range(length // LANES)
        ]
        heads.append(jnp.concatenate(parts, axis=0))
    return jnp.concatenate(heads, axis=1)


def head_columns(kv_local, kv):
    return kv * PAIR, kv_local * PAIR + kv * HEAD_DIM, kv_local * (PAIR + HEAD_DIM) + kv * HEAD_DIM


def two_heads(ref, rows, low):
    return jnp.concatenate([ref[rows, low : low + HEAD_DIM], ref[rows, low + HEAD_DIM : low + PAIR]], axis=0)


def self_forward_kernel(blocks, kv_local, my_ref, qkv_ref, bias_ref, *refs):
    mix_refs, (lse_ref, tile_ref, top_ref, sum_ref, acc_ref) = refs[:blocks], refs[blocks:]
    a = pl.program_id(0)
    length = qkv_ref.shape[0] // blocks
    my = my_ref[0]
    mine = my ^ a

    @pl.when(a == 0)
    def _():
        spread_bias(bias_ref, tile_ref)

    rows = pl.ds(pl.multiple_of(a * length, length), length)
    top_ref[...] = jnp.full_like(top_ref, NEGATIVE)
    sum_ref[...] = jnp.zeros_like(sum_ref)
    acc_ref[...] = jnp.zeros_like(acc_ref)
    for b in range(blocks):
        source = my ^ b
        keys_at = slice(b * length, (b + 1) * length)

        @pl.when(source <= mine)
        def _(source=source, keys_at=keys_at):
            start = length + length * (mine - source)
            for kv in range(kv_local):
                q_at, k_at, v_at = head_columns(kv_local, kv)
                qq = two_heads(qkv_ref, rows, q_at)
                keys = qkv_ref[keys_at, k_at : k_at + HEAD_DIM]
                values = qkv_ref[keys_at, v_at : v_at + HEAD_DIM]
                scores = dot32(keys, qq, NT) * SCALE + bias_tile(tile_ref, kv, start, length)
                old = top_ref[kv]
                new = jnp.maximum(old, jnp.max(scores, axis=0, keepdims=True))
                weights = jnp.exp(scores - new)
                shrink = jnp.exp(old - new)
                top_ref[kv] = new
                sum_ref[kv] = sum_ref[kv] * shrink + jnp.sum(weights, axis=0, keepdims=True)
                acc_ref[kv] = acc_ref[kv] * shrink + dot32(values, weights.astype(BF16), TN)

    for kv in range(kv_local):
        lse_ref[0, kv] = top_ref[kv] + jnp.log(sum_ref[kv])
    for b, mix_ref in enumerate(mix_refs):

        @pl.when(a == b)
        def _(mix_ref=mix_ref):
            for kv in range(kv_local):
                unstack(mix_ref, kv, acc_ref[kv] / sum_ref[kv])


def self_backward_kernel(blocks, kv_local, my_ref, qkv_ref, bias_ref, lse_ref, *refs):
    mix_refs, grad_refs, out_refs = refs[:blocks], refs[blocks : 2 * blocks], refs[2 * blocks : 3 * blocks]
    dbias_ref, tile_ref, diag_ref, dq_ref, dk_ref, dv_ref, grad_ref, mix_ref = refs[3 * blocks :]
    a = pl.program_id(0)
    length = qkv_ref.shape[0] // blocks
    width = bias_ref.shape[1]
    my = my_ref[0]
    mine = my ^ a

    @pl.when(a == 0)
    def _():
        spread_bias(bias_ref, tile_ref)
        diag_ref[...] = jnp.zeros_like(diag_ref)
        dk_ref[...] = jnp.zeros_like(dk_ref)
        dv_ref[...] = jnp.zeros_like(dv_ref)

    rows = pl.ds(pl.multiple_of(a * length, length), length)
    every = slice(0, length)
    for b in range(blocks):

        @pl.when(a == b)
        def _(b=b):
            grad_ref[...] = grad_refs[b][...]
            mix_ref[...] = mix_refs[b][...]

    dq_ref[...] = jnp.zeros_like(dq_ref)
    deltas = []
    for kv in range(kv_local):
        both = two_heads(grad_ref, every, kv * PAIR).astype(F32) * two_heads(mix_ref, every, kv * PAIR).astype(F32)
        deltas.append(jnp.sum(both.T, axis=0, keepdims=True))
    for b in range(blocks):
        source = my ^ b
        keys_at = slice(b * length, (b + 1) * length)

        @pl.when(source <= mine)
        def _(source=source, keys_at=keys_at):
            start = length + length * (mine - source)
            for kv in range(kv_local):
                q_at, k_at, v_at = head_columns(kv_local, kv)
                qq = two_heads(qkv_ref, rows, q_at)
                dd = two_heads(grad_ref, every, q_at)
                keys = qkv_ref[keys_at, k_at : k_at + HEAD_DIM]
                values = qkv_ref[keys_at, v_at : v_at + HEAD_DIM]
                scores = dot32(keys, qq, NT) * SCALE + bias_tile(tile_ref, kv, start, length)
                probs = jnp.exp(scores - lse_ref[0, kv])
                dv_ref[kv, keys_at, :] += dot32(probs.astype(BF16), dd)
                change = dot32(values, dd, NT) - deltas[kv]
                ds = (probs * change).astype(BF16)
                dk_ref[kv, keys_at, :] += dot32(ds, qq)
                dq_ref[kv] += dot32(keys, ds, TN)
                ds = ds.astype(F32)
                for g in range(2):
                    for m in range(length // LANES):
                        where = pl.ds(pl.multiple_of(start - LANES * m, LANES), length)
                        diag_ref[2 * kv + g, :, where] += ds[m * LANES : (m + 1) * LANES, g * length : (g + 1) * length]

    for b in range(blocks):

        @pl.when(a == b)
        def _(out_ref=out_refs[b]):
            for kv in range(kv_local):
                back = (dq_ref[kv] * SCALE).T.astype(BF16)
                out_ref[:, kv * PAIR : kv * PAIR + HEAD_DIM] = back[:length]
                out_ref[:, kv * PAIR + HEAD_DIM : (kv + 1) * PAIR] = back[length:]

    @pl.when(a == blocks - 1)
    def _():
        for kv in range(kv_local):
            _, k_at, v_at = head_columns(kv_local, kv)
            for b, out_ref in enumerate(out_refs):
                keys_at = slice(b * length, (b + 1) * length)
                out_ref[:, k_at : k_at + HEAD_DIM] = (dk_ref[kv, keys_at, :] * SCALE).astype(BF16)
                out_ref[:, v_at : v_at + HEAD_DIM] = dv_ref[kv, keys_at, :].astype(BF16)
        for h in range(2 * kv_local):
            part = diag_ref[h]
            half = LANES // 2
            while half:
                part = part[:half] + pltpu.roll(part[half:], width - half, 1)
                half //= 2
            dbias_ref[h : h + 1, :] = part


def cross_forward_kernel(allow_ref, q_ref, k_ref, v_ref, mix_ref, lse_ref):
    allow = allow_ref[...] > 0
    for kv in range(2):
        low = kv * HEAD_DIM
        qq = stacked(q_ref, kv)
        scores = dot32(k_ref[:, low : low + HEAD_DIM], qq, NT) * SCALE
        scores = jnp.where(allow, scores, NEGATIVE)
        top = jnp.max(scores, axis=0, keepdims=True)
        raised = jnp.exp(scores - top)
        total = jnp.sum(raised, axis=0, keepdims=True)
        probs = (raised * (1.0 / total)).astype(BF16)
        unstack(mix_ref, kv, dot32(v_ref[:, low : low + HEAD_DIM], probs, TN))
        lse_ref[kv] = top + jnp.log(total)


def cross_backward_kernel(allow_ref, q_ref, k_ref, v_ref, lse_ref, grad_ref, dq_ref, dkv_ref):
    allow = allow_ref[...] > 0
    for kv in range(2):
        low = kv * HEAD_DIM
        qq = stacked(q_ref, kv)
        dd = stacked(grad_ref, kv)
        keys = k_ref[:, low : low + HEAD_DIM]
        scores = jnp.where(allow, dot32(keys, qq, NT) * SCALE, NEGATIVE)
        probs = jnp.exp(scores - lse_ref[kv])
        change = dot32(v_ref[:, low : low + HEAD_DIM], dd, NT)
        delta = jnp.sum(probs * change, axis=0, keepdims=True)
        ds = (probs * (change - delta)).astype(BF16)
        dkv_ref[1, :, low : low + HEAD_DIM] = dot32(probs.astype(BF16), dd).astype(BF16)
        dkv_ref[0, :, low : low + HEAD_DIM] = (dot32(ds, qq) * SCALE).astype(BF16)
        unstack(dq_ref, kv, dot32(keys, ds, TN) * SCALE)


TINY = pl.CostEstimate(flops=1, transcendentals=0, bytes_accessed=1)


def params():
    return pltpu.CompilerParams(dimension_semantics=("arbitrary",), vmem_limit_bytes=VMEM_LIMIT)


def cost(length, keys, heads, passes, moved):
    return pl.CostEstimate(
        flops=2 * length * keys * heads * HEAD_DIM * passes,
        transcendentals=length * keys * heads,
        bytes_accessed=moved,
    )


def lane_block(rows, width):
    return pl.BlockSpec((rows, width), lambda i: (0, i))


def self_forward(blocks, my, qkv, bias):
    tokens, columns = qkv.shape
    length, kv_local, width = tokens // blocks, columns // (2 * PAIR), bias.shape[1]
    q_width = kv_local * PAIR
    return pl.pallas_call(
        functools.partial(self_forward_kernel, blocks, kv_local),
        grid=(blocks,),
        in_specs=[
            pl.BlockSpec(memory_space=pltpu.SMEM),
            pl.BlockSpec((tokens, columns), lambda i: (0, 0)),
            pl.BlockSpec(bias.shape, lambda i: (0, 0)),
        ],
        out_specs=[pl.BlockSpec((length, q_width), lambda i: (0, 0))] * blocks
        + [pl.BlockSpec((1, kv_local, 1, 2 * length), lambda i: (i, 0, 0, 0))],
        out_shape=[jax.ShapeDtypeStruct((length, q_width), BF16)] * blocks
        + [jax.ShapeDtypeStruct((blocks, kv_local, 1, 2 * length), F32)],
        scratch_shapes=[
            pltpu.VMEM((2 * kv_local, LANES, width), F32),
            pltpu.VMEM((kv_local, 1, 2 * length), F32),
            pltpu.VMEM((kv_local, 1, 2 * length), F32),
            pltpu.VMEM((kv_local, HEAD_DIM, 2 * length), F32),
        ],
        compiler_params=params(),
        cost_estimate=TINY,
        name="self_forward",
    )(my, qkv, bias)


def self_backward(blocks, my, qkv, bias, mixes, lse, grads):
    tokens, columns = qkv.shape
    length, kv_local, width = tokens // blocks, columns // (2 * PAIR), bias.shape[1]
    q_width = kv_local * PAIR
    lines = pl.BlockSpec(bias.shape, lambda i: (0, 0))
    *outs, d_bias = pl.pallas_call(
        functools.partial(self_backward_kernel, blocks, kv_local),
        grid=(blocks,),
        in_specs=[
            pl.BlockSpec(memory_space=pltpu.SMEM),
            pl.BlockSpec((tokens, columns), lambda i: (0, 0)),
            lines,
            pl.BlockSpec((1, kv_local, 1, 2 * length), lambda i: (i, 0, 0, 0)),
        ]
        + [pl.BlockSpec((length, q_width), lambda i: (0, 0))] * (2 * blocks),
        out_specs=[pl.BlockSpec((length, columns), lambda i: (0, 0))] * blocks + [lines],
        out_shape=[jax.ShapeDtypeStruct((length, columns), BF16)] * blocks + [jax.ShapeDtypeStruct(bias.shape, F32)],
        scratch_shapes=[
            pltpu.VMEM((2 * kv_local, LANES, width), F32),
            pltpu.VMEM((2 * kv_local, LANES, width), F32),
            pltpu.VMEM((kv_local, HEAD_DIM, 2 * length), F32),
            pltpu.VMEM((kv_local, tokens, HEAD_DIM), F32),
            pltpu.VMEM((kv_local, tokens, HEAD_DIM), F32),
            pltpu.VMEM((length, q_width), BF16),
            pltpu.VMEM((length, q_width), BF16),
        ],
        compiler_params=params(),
        cost_estimate=TINY,
        name="self_backward",
    )(my, qkv, bias, lse, *mixes, *grads)
    return outs, d_bias


def cross_forward(allow, q, k, v):
    length, keys, kv_heads = q.shape[0], k.shape[0], k.shape[1] // HEAD_DIM
    return pl.pallas_call(
        cross_forward_kernel,
        grid=(kv_heads // 2,),
        in_specs=[
            pl.BlockSpec((keys, 1), lambda i: (0, 0)),
            lane_block(length, 2 * PAIR),
            lane_block(keys, PAIR),
            lane_block(keys, PAIR),
        ],
        out_specs=[
            lane_block(length, 2 * PAIR),
            pl.BlockSpec((2, 1, 2 * length), lambda i: (i, 0, 0)),
        ],
        out_shape=[
            jax.ShapeDtypeStruct(q.shape, BF16),
            jax.ShapeDtypeStruct((kv_heads, 1, 2 * length), F32),
        ],
        compiler_params=params(),
        cost_estimate=TINY,
        name="cross_forward",
    )(allow, q, k, v)


def cross_backward(allow, q, k, v, lse, grad):
    length, keys, kv_heads = q.shape[0], k.shape[0], k.shape[1] // HEAD_DIM
    return pl.pallas_call(
        cross_backward_kernel,
        grid=(kv_heads // 2,),
        in_specs=[
            pl.BlockSpec((keys, 1), lambda i: (0, 0)),
            lane_block(length, 2 * PAIR),
            lane_block(keys, PAIR),
            lane_block(keys, PAIR),
            pl.BlockSpec((2, 1, 2 * length), lambda i: (i, 0, 0)),
            lane_block(length, 2 * PAIR),
        ],
        out_specs=[
            lane_block(length, 2 * PAIR),
            pl.BlockSpec((2, keys, PAIR), lambda i: (0, 0, i)),
        ],
        out_shape=[
            jax.ShapeDtypeStruct(q.shape, BF16),
            jax.ShapeDtypeStruct((2,) + k.shape, BF16),
        ],
        compiler_params=params(),
        cost_estimate=TINY,
        name="cross_backward",
    )(allow, q, k, v, lse, grad)


def slab_kernel(kind, later, x_count, g_count, gained, order_ref, *refs):
    xs, gs = refs[:x_count], refs[x_count : x_count + g_count]
    turned_ref, whole_ref = refs[-2:]
    keep_ref, send_ref = refs[-5:-3] if gained else refs[-4:-2]
    slab = pl.program_id(0)
    kind = jnp.where(slab < later, 0, 1) if kind is None else kind

    @pl.when(slab == 0)
    def _():
        low = 0
        for x in xs:
            turned_ref[low : low + x.shape[1], :] = x[...].T
            low += x.shape[1]

    chunks, rows, width = whole_ref.shape
    g = gs[0][...] if g_count == 1 else jnp.concatenate([ref[...] for ref in gs], axis=0)
    full = dot32(turned_ref[...], g)
    whole_ref[...] = full.reshape(chunks, rows, width)
    half = chunks // 2
    for c in range(half):
        keep_ref[c] = whole_ref[order_ref[kind, c]].astype(BF16)
        send_ref[c] = whole_ref[order_ref[kind, half + c]].astype(BF16)
    if gained:
        refs[-3][...] = jnp.sum(full * refs[x_count + g_count][...].astype(F32), axis=1, keepdims=True)


def slabs(order, x, g, total, at, later, buffers, kind=None, slab=SLAB, weight=None):
    xs = x if isinstance(x, list) else [x]
    tokens, features = xs[0].shape[0], sum(part.shape[1] for part in xs)
    chunks = order.shape[1]
    rows = features // chunks
    gs = g if isinstance(g, list) else [g]
    if len(gs) > 1:
        count, g_specs = 1, whole_blocks(gs)
    elif g.ndim == 3:
        count, g_specs = g.shape[0], [pl.BlockSpec((None, tokens, slab), lambda i: (i, 0, 0))]
    else:
        count, g_specs = g.shape[1] // slab, [pl.BlockSpec((tokens, slab), lambda i: (0, i))]
    assert at % rows == 0 and features % chunks == 0 and rows % 8 == 0
    out = pl.BlockSpec((chunks // 2, rows, slab), lambda i: (0, at // rows + i, 0))
    shapes = [jax.ShapeDtypeStruct((chunks // 2, total, slab), BF16)] * 2
    outs = [out, out]
    extra = [] if buffers is None else list(buffers)
    first = 1 + len(xs) + len(gs)
    weights = []
    if weight is not None:
        weights = [weight]
        shapes.append(jax.ShapeDtypeStruct((features, 1), F32))
        outs.append(pl.BlockSpec((features, 1), lambda i: (0, 0)))
    return pl.pallas_call(
        functools.partial(slab_kernel, kind, later, len(xs), len(gs), weight is not None),
        grid=(count,),
        in_specs=[pl.BlockSpec(memory_space=pltpu.SMEM)]
        + whole_blocks(xs)
        + g_specs
        + whole_blocks(weights)
        + [pl.BlockSpec(memory_space=pl.ANY)] * len(extra),
        out_specs=outs,
        out_shape=shapes,
        scratch_shapes=[pltpu.VMEM((features, tokens), BF16), pltpu.VMEM((chunks, rows, slab), F32)],
        input_output_aliases={first: 0, first + 1: 1} if extra else {},
        compiler_params=params(),
        cost_estimate=TINY,
        name="slabs",
    )(order, *xs, *gs, *weights, *extra)


def cover(*ranges):
    held, row = [], 0
    for low, high in ranges:
        held.append((low, high, row))
        row += high - low
    return held


def add_range(sources, refs, low, high):
    total = None
    for number, segments in sources:
        for start, stop, row in segments:
            if start <= low and high <= stop:
                part = refs[number][:, row + low - start : row + high - start, :].astype(F32)
                total = part if total is None else total + part
    return total


def cut_points(pieces, low, high):
    marks = {low, high}
    for _, segments in pieces:
        marks |= {m for start, stop, _ in segments for m in (start, stop) if low < m < high}
    marks = sorted(marks)
    return list(zip(marks[:-1], marks[1:]))


def total_kernel(plan, *refs):
    inputs, results = refs[: -len(plan)], refs[-len(plan) :]
    for (sources, writes), result in zip(plan, results):
        for row, low, high in writes:
            result[:, row : row + high - low, :] = add_range(sources, inputs, low, high).astype(result.dtype)


def totals(pieces, groups, steps):
    plan, specs, arrays, shapes, outs = [], [], [], [], []
    width = pieces[0][0].shape[2]
    for first, count, ranges in groups:
        step = count // steps
        sources = []
        for array, segments in pieces:
            sources.append((len(arrays), segments))
            arrays.append(array)
            specs.append(pl.BlockSpec((step,) + array.shape[1:], lambda i, low=first // step: (low + i, 0, 0)))
        writes, rows = [], 0
        for low, high in ranges:
            for a, b in cut_points(pieces, low, high):
                writes.append((rows, a, b))
                rows += b - a
        plan.append((sources, writes))
        outs.append(pl.BlockSpec((step, rows, width), lambda i: (i, 0, 0)))
        shapes.append(jax.ShapeDtypeStruct((count, rows, width), BF16))
    return pl.pallas_call(
        functools.partial(total_kernel, plan),
        grid=(steps,),
        in_specs=specs,
        out_specs=outs,
        out_shape=shapes,
        compiler_params=params(),
        cost_estimate=TINY,
        name="totals",
    )(*arrays)


def finish_kernel(sources, outs, dealt, my_ref, *refs):
    inputs, results = refs[: len(sources)], refs[len(sources) :]
    for row, rows, number, column in outs:
        results[number][:, column : column + SLAB] = add_range(sources, inputs, row, row + rows)[0]
    for j, row, rows, parts in dealt:
        block = add_range(sources, inputs, row, row + rows)[0]
        low = 0
        for number, width in parts:
            columns = pl.ds(pl.multiple_of((my_ref[0] ^ j) * width, LANES), width)
            results[number][:, columns] = block[:, low : low + width]
            low += width


def finish(my, pieces, shapes, outs, dealt):
    sources = [(number, segments) for number, (_, segments) in enumerate(pieces)]
    return pl.pallas_call(
        functools.partial(finish_kernel, sources, outs, dealt),
        grid=(1,),
        in_specs=[pl.BlockSpec(memory_space=pltpu.SMEM)]
        + [pl.BlockSpec((1,) + array.shape[1:], lambda i: (0, 0, 0)) for array, _ in pieces],
        out_specs=[pl.BlockSpec(shape, lambda i: (0, 0)) for shape in shapes],
        out_shape=[jax.ShapeDtypeStruct(shape, F32) for shape in shapes],
        compiler_params=params(),
        cost_estimate=TINY,
        name="finish",
    )(my, *[array for array, _ in pieces])


def pair_dot_kernel(my_ref, x_ref, *refs):
    gs, result = refs[:-1], refs[-1]
    x = jnp.concatenate([x_ref[my_ref[0] ^ j] for j in range(len(gs))], axis=0)
    g = jnp.concatenate([ref[...] for ref in gs], axis=0)
    result[...] = dot32(x, g, TN).astype(BF16)


def whole_blocks(arrays):
    return [pl.BlockSpec(a.shape, lambda i, n=a.ndim: (0,) * n) for a in arrays]


def pair_dot(my, x, gs):
    features, width = x.shape[1], gs[0].shape[1]
    x = x.reshape(len(gs), -1, features)
    return pl.pallas_call(
        pair_dot_kernel,
        grid=(1,),
        in_specs=[pl.BlockSpec(memory_space=pltpu.SMEM)] + whole_blocks([x, *gs]),
        out_specs=pl.BlockSpec((features, width), lambda i: (0, 0)),
        out_shape=jax.ShapeDtypeStruct((features, width), BF16),
        compiler_params=params(),
        cost_estimate=TINY,
        name="pair_dot",
    )(my, x, *gs)


def dot_gain_kernel(x_ref, g_ref, w_ref, out_ref, gain_ref):
    full = dot32(x_ref[...], g_ref[...], TN)
    out_ref[...] = full.astype(BF16)
    gain_ref[...] = jnp.sum(full * w_ref[...].astype(F32), axis=1, keepdims=True)


def dot_gain(x, g, w):
    features, width = w.shape
    return pl.pallas_call(
        dot_gain_kernel,
        grid=(1,),
        in_specs=whole_blocks([x, g, w]),
        out_specs=[pl.BlockSpec((features, width), lambda i: (0, 0)), pl.BlockSpec((features, 1), lambda i: (0, 0))],
        out_shape=[jax.ShapeDtypeStruct((features, width), BF16), jax.ShapeDtypeStruct((features, 1), F32)],
        compiler_params=params(),
        cost_estimate=TINY,
        name="dot_gain",
    )(x, g, w)


def add_norm_kernel(count, has_next, *refs):
    xs, ws = refs[:count], refs[count : 2 * count]
    base_ref, gain_ref = refs[2 * count : 2 * count + 2]
    total = base_ref[...].astype(F32)
    for x, w in zip(xs, ws):
        total = total + dot32(x[...], w[...])
    normed = (total * inverse_rms(total) * gain_ref[...]).astype(BF16)
    if has_next:
        next_ref, total_ref, normed_ref, out_ref = refs[2 * count + 2 :]
        out_ref[...] = dot32(normed, next_ref[...]).astype(BF16)
    else:
        total_ref, normed_ref = refs[2 * count + 2 :]
    total_ref[...] = total
    normed_ref[...] = normed


def add_norm(base, xs, ws, gain, after=None):
    shapes = [jax.ShapeDtypeStruct(base.shape, F32), jax.ShapeDtypeStruct(base.shape, BF16)]
    inputs = [*xs, *ws, base, gain[None]]
    if after is not None:
        inputs.append(after)
        shapes.append(jax.ShapeDtypeStruct((base.shape[0], after.shape[1]), BF16))
    return pl.pallas_call(
        functools.partial(add_norm_kernel, len(xs), after is not None),
        grid=(1,),
        in_specs=whole_blocks(inputs),
        out_specs=whole_blocks(shapes),
        out_shape=shapes,
        compiler_params=params(),
        cost_estimate=TINY,
        name="add_norm",
    )(*inputs)


def norm_grad_kernel(count, nexts, *refs):
    gs, ws = refs[:count], refs[count : 2 * count]
    x_ref, gain_ref, base_ref = refs[2 * count : 2 * count + 3]
    after = refs[2 * count + 3 : 2 * count + 3 + nexts]
    grad_ref, low_ref, gain_grad_ref = refs[2 * count + 3 + nexts : 2 * count + 6 + nexts]
    outs, acc_ref = refs[2 * count + 6 + nexts : -1], refs[-1]
    step = pl.program_id(0)

    @pl.when(step == 0)
    def _():
        acc_ref[...] = jnp.zeros_like(acc_ref)

    part = None
    for g, w in zip(gs, ws):
        term = dot32(g[...], w[...], NT)
        part = term if part is None else part + term
    acc_ref[...] += part

    @pl.when(step == pl.num_programs(0) - 1)
    def _():
        total = acc_ref[...]
        x = x_ref[...].astype(F32)
        d_x, d_gain = norm_back(x, inverse_rms(x), gain_ref[...], total)
        grad = base_ref[...].astype(F32) + d_x
        low = grad.astype(BF16)
        grad_ref[...] = grad
        low_ref[...] = low
        gain_grad_ref[...] = d_gain[None]
        for w, out in zip(after, outs):
            out[...] = dot32(low, w[...], NT).astype(BF16)


def norm_grad(base, gs, ws, x, gain, after, tile):
    length, width = x.shape
    inner = gs[0].shape[1]
    fixed = [x, gain[None], base, *after]
    shapes = [
        jax.ShapeDtypeStruct(x.shape, F32),
        jax.ShapeDtypeStruct(x.shape, BF16),
        jax.ShapeDtypeStruct((1, width), F32),
    ] + [jax.ShapeDtypeStruct((length, w.shape[0]), BF16) for w in after]
    grad, low, d_gain, *outs = pl.pallas_call(
        functools.partial(norm_grad_kernel, len(gs), len(after)),
        grid=(inner // tile,),
        in_specs=[pl.BlockSpec((length, tile), lambda i: (0, i))] * len(gs)
        + [pl.BlockSpec((width, tile), lambda i: (0, i))] * len(ws)
        + whole_blocks(fixed),
        out_specs=whole_blocks(shapes),
        out_shape=shapes,
        scratch_shapes=[pltpu.VMEM((length, width), F32)],
        compiler_params=params(),
        cost_estimate=TINY,
        name="norm_grad",
    )(*gs, *ws, *fixed)
    return grad, low, d_gain[0], outs


def norm_dot_kernel(count, *refs):
    gain_ref, w_ref, normed_ref, out_ref = refs[count:]
    for k, ref in enumerate(refs[:count]):
        length = ref.shape[0]
        rows = slice(k * length, (k + 1) * length)
        x = ref[...].astype(F32)
        normed = (x * inverse_rms(x) * gain_ref[...]).astype(BF16)
        normed_ref[rows, :] = normed
        out_ref[rows, :] = dot32(normed, w_ref[...]).astype(BF16)


def norm_dot(xs, gain, w):
    rows = len(xs) * xs[0].shape[0]
    shapes = [(rows, w.shape[0]), (rows, w.shape[1])]
    return pl.pallas_call(
        functools.partial(norm_dot_kernel, len(xs)),
        grid=(1,),
        in_specs=whole_blocks([*xs, gain, w]),
        out_specs=[pl.BlockSpec(shape, lambda i: (0, 0)) for shape in shapes],
        out_shape=[jax.ShapeDtypeStruct(shape, BF16) for shape in shapes],
        compiler_params=params(),
        cost_estimate=TINY,
        name="norm_dot",
    )(*xs, gain, w)


def turn_kernel(my_ref, x_ref, *refs):
    results, chunk_ref = refs[:-1], refs[-1]
    count = len(results)
    chunk_ref[...] = x_ref[...].astype(F32).T.reshape(chunk_ref.shape)
    for j, result in enumerate(results):
        for k in range(result.shape[0]):
            result[k] = chunk_ref[k * count + (my_ref[0] ^ j)].astype(BF16)


def turn_chunks(my, x, blocks, devices):
    tokens, features = x.shape
    shape = (devices // blocks, features // devices, tokens)
    return pl.pallas_call(
        turn_kernel,
        grid=(1,),
        in_specs=[pl.BlockSpec(memory_space=pltpu.SMEM)] + whole_blocks([x]),
        out_specs=[pl.BlockSpec(shape, lambda i: (0, 0, 0))] * blocks,
        out_shape=[jax.ShapeDtypeStruct(shape, BF16)] * blocks,
        scratch_shapes=[pltpu.VMEM((devices, features // devices, tokens), F32)],
        compiler_params=params(),
        cost_estimate=TINY,
        name="turn_chunks",
    )(my, x)


def turned_dot_kernel(count, my_ref, *refs):
    xs, (g_ref, result) = refs[:count], refs[count:]
    chunks, rows, tokens = xs[0].shape
    total = None
    for j, ref in enumerate(xs):
        x = ref[...].astype(F32).reshape(chunks * rows, tokens).astype(BF16)
        term = dot32(x, g_ref[my_ref[0] ^ j])
        total = term if total is None else total + term
    result[...] = total.reshape(result.shape).astype(BF16)


def turned_dot(my, xs, g):
    chunks, rows, tokens = xs[0].shape
    width = g.shape[1]
    g = g.reshape(len(xs), tokens, width)
    return pl.pallas_call(
        functools.partial(turned_dot_kernel, len(xs)),
        grid=(1,),
        in_specs=[pl.BlockSpec(memory_space=pltpu.SMEM)] + whole_blocks([*xs, g]),
        out_specs=pl.BlockSpec((chunks, rows, width), lambda i: (0, 0, 0)),
        out_shape=jax.ShapeDtypeStruct((chunks, rows, width), BF16),
        compiler_params=params(),
        cost_estimate=TINY,
        name="turned_dot",
    )(my, *xs, g)


def place_kernel(my_ref, *refs):
    parts, results = refs[:-2], refs[-2:]
    per_half = len(parts) // 2
    share = parts[0].shape[1]
    for j, part in enumerate(parts):
        owner = my_ref[0] ^ j
        for number, result in enumerate(results):

            @pl.when(owner // per_half == number)
            def _(part=part, result=result, number=number, owner=owner):
                columns = pl.ds(pl.multiple_of((owner - number * per_half) * share, LANES), share)
                result[:, columns] = part[...].astype(F32)


def place(my, parts):
    shape = (parts[0].shape[0], len(parts) // 2 * parts[0].shape[1])
    return pl.pallas_call(
        place_kernel,
        grid=(1,),
        in_specs=[pl.BlockSpec(memory_space=pltpu.SMEM)] + whole_blocks(parts),
        out_specs=[pl.BlockSpec(shape, lambda i: (0, 0))] * 2,
        out_shape=[jax.ShapeDtypeStruct(shape, F32)] * 2,
        compiler_params=params(),
        cost_estimate=TINY,
        name="place",
    )(my, *parts)


def exchange_order():
    dp, blk = lax.axis_size("dp"), lax.axis_size("blk")
    dp_bits, blk_bits = dp.bit_length() - 1, blk.bit_length() - 1
    mine = lax.axis_index("dp") * blk + lax.axis_index("blk")
    deep = list(range(blk_bits + 1, blk_bits + dp_bits))
    up, down = list(range(blk_bits)), list(reversed(range(blk_bits)))
    tables = []
    for order in (up + deep, down + deep, deep + down):
        order = [blk_bits] + order
        table = []
        for place in range(dp * blk):
            relative = 0
            for k, bit in enumerate(order):
                relative |= ((place >> (len(order) - 1 - k)) & 1) << bit
            table.append(relative)
        tables.append(table)
    return jnp.array(tables, jnp.int32) ^ mine.astype(jnp.int32)


class Halves:
    def __init__(self, keep, got, over_x, over_y):
        self.rows = [(0, keep.shape[1])]
        self.pieces = [(keep, cover(*self.rows)), (got, cover(*self.rows))]
        self.parts, self.chunks = (over_x, over_y), keep.shape[0]

    def pack(self, deep=False):
        half = self.chunks // 2
        parts = [self.rows] if deep else self.parts
        self.out = totals(self.pieces, [(half, half, part) for part in parts], 2 if half > 4 else 1)
        self.chunks = half

    def hop(self, bits):
        self.got = [swap(out, "blk", bit) for out, bit in zip(self.out, bits)]

    def join(self, pieces, end):
        self.pieces += pieces
        self.rows = [(0, end)]

    def hop_deep(self, bit):
        self.got = [swap(self.out[0], "dp", bit)]

    def arrive(self):
        parts = [self.rows] if len(self.got) == 1 else self.parts
        self.pieces += [(array, cover(*part)) for array, part in zip(self.got, parts)]


def turn_rows(x, rows):
    my = lax.axis_index("blk")
    return jnp.concatenate([lax.dynamic_slice_in_dim(x, (my ^ j) * rows, rows, 0) for j in range(lax.axis_size("blk"))], axis=0)


def inverse_rms(x):
    return lax.rsqrt(jnp.mean(x * x, axis=-1, keepdims=True) + EPSILON)


def norm_back(x, inverse, gain, grad):
    scaled = grad * gain
    along = jnp.mean(scaled * x, axis=-1, keepdims=True)
    d_x = inverse * scaled - x * (inverse * inverse * inverse * along)
    return d_x, jnp.sum(grad * (x * inverse), axis=0)


def body(
    block_in,
    memory,
    memory_len,
    cross_mask,
    buckets,
    bias_table,
    norm_self,
    w_query,
    w_key,
    w_value,
    w_out,
    norm_cross,
    cross_query,
    cross_key,
    cross_value,
    cross_out,
    norm_ffn,
    w_gate,
    w_up,
    w_down,
    grad_out,
):
    seq_count, length, model_width = block_in.shape
    assert seq_count == 1
    mem_rows = memory.shape[1]
    mem_total = cross_mask.shape[1]
    blocks = lax.axis_size("blk")
    my = lax.axis_index("blk")
    kv_width = w_key.shape[1]
    head_count = w_query.shape[1] // HEAD_DIM
    bucket_count = bias_table.shape[0]
    my_ref = my.reshape(1).astype(jnp.int32)

    x_parts = [block_in[0]] + trade([block_in[0]] * blocks, "blk", 1)

    own_heads = head_count // blocks
    own_q, own_kv = own_heads * HEAD_DIM, kv_width // blocks
    turned_qkv = [
        jnp.concatenate(
            [
                lax.dynamic_slice_in_dim(w, (my ^ j) * width, width, 1)
                for w, width in ((w_query, own_q), (w_key, own_kv), (w_value, own_kv))
            ],
            axis=1,
        )
        for j in range(blocks)
    ]
    out_turned = [lax.dynamic_slice_in_dim(w_out, (my ^ j) * own_q, own_q, 0) for j in range(blocks)]

    bucket_hot = (buckets[:, None] == jnp.arange(bucket_count)[None, :]).astype(F32)
    own_table = lax.dynamic_slice_in_dim(bias_table, my * own_heads, own_heads, 1)
    dist_bias = lax.dot_general(own_table, bucket_hot, (((0,), (1,)), ((), ())), precision=lax.Precision.HIGHEST)
    bias = jnp.concatenate([jnp.full((own_heads, length), NEGATIVE, F32), dist_bias], axis=1)

    mem_places = jnp.arange(mem_total)
    allowed = (mem_places == 0) | (mem_places < memory_len[0]) & (cross_mask[0] == 1)
    allow = allowed.astype(F32).reshape(blocks, mem_rows)[my ^ jnp.arange(blocks)].reshape(mem_total, 1)

    d_hidden = dot32(grad_out[0], w_down, NT)
    x_parts, mem_own, turned_qkv, out_turned, d_hidden, bias, allow, top_own = tie(
        x_parts, memory[0], turned_qkv, out_turned, d_hidden, bias, allow, grad_out[0]
    )
    top_all = lax.all_gather(top_own, "blk", axis=0, tiled=True)
    mem_all = jnp.concatenate([mem_own] + trade([mem_own] * blocks, "blk", 1), axis=0)
    self_all, qkv = norm_dot(x_parts, norm_self[None], turned_qkv[0])
    *own_mix, lse = self_forward(blocks, my_ref, qkv, bias)
    mem_key = dot32(mem_all, cross_key).astype(BF16)
    mem_value = dot32(mem_all, cross_value).astype(BF16)
    mix_got, mem_key, mem_value = tie(trade(own_mix, "blk", 1), mem_key, mem_value)
    mixes = [own_mix[0]] + mix_got
    after_self, cross_in, cross_q = add_norm(block_in[0], mixes, out_turned, norm_cross, cross_query)
    cross_mix, cross_lse = cross_forward(allow, cross_q, mem_key, mem_value)
    after_cross, ffn_in = add_norm(after_self, [cross_mix], [cross_out], norm_ffn)
    devices = blocks * lax.axis_size("dp")
    d, ff = model_width, w_gate.shape[1]
    share = 2 * ff // blocks
    fast = (
        blocks == 4
        and lax.axis_size("dp") == 8
        and d % (8 * devices) == 0
        and ff % (8 * devices) == 0
        and kv_width == SLAB
        and d % SLAB == 0
        and share % LANES == 0
    )
    gate = dot32(ffn_in, w_gate)
    up = dot32(ffn_in, w_up)
    (act, hidden_full), gated_back = jax.vjp(lambda g, u: (jax.nn.gelu(g, approximate=True), jax.nn.gelu(g, approximate=True) * u), gate, up)
    hidden = hidden_full.astype(BF16)

    ffn_grad = grad_out[0]
    gate_full, up_full = gated_back((jnp.zeros_like(act), d_hidden))
    gate_grad, up_grad = gate_full.astype(BF16), up_full.astype(BF16)
    if fast:
        order = exchange_order()
        turned = order ^ ((my * (devices // blocks)).astype(jnp.int32))
        small, large = d // devices, ff // devices
        d_slabs = d // SLAB
        top_all, ffn_late = tie(top_all, ffn_in)
        ffn_all = lax.all_gather(ffn_late, "blk", axis=0, tiled=True)
        both_grad = jnp.concatenate([gate_grad, up_grad], axis=1)
        shares = [lax.dynamic_slice_in_dim(both_grad, (my ^ j) * share, share, 1) for j in range(blocks)]
        shares, hidden = tie(shares, hidden)
        shares_near = trade(shares[:3], "blk", 1)
        hidden_parts = turn_chunks(my_ref, hidden, blocks, devices)
    else:
        dw_down = sum_rows(dot32(hidden, ffn_grad, TN).astype(BF16), 1)
        ffn_outs = (
            sum_rows(dot32(ffn_in, gate_grad, TN).astype(BF16), 0),
            sum_rows(dot32(ffn_in, up_grad, TN).astype(BF16), 1),
            dw_down,
        )
    tile = ff // 2 if ff % (2 * LANES) == 0 else ff
    grad_cross, cross_grad, d_gain_ffn, (mix_grad,) = norm_grad(
        ffn_grad, [gate_grad, up_grad], [w_gate, w_up], after_cross, norm_ffn, [cross_out], tile
    )
    block_out = (after_cross + dot32(hidden, w_down)).astype(BF16)
    if fast:
        total = 4 * d_slabs * small
        held = slabs(order, cross_mix, cross_grad, total, 0, total, None)
        mix_grad, shares_near, shares[3], hidden_parts, ffn_all, held, block_out = tie(
            mix_grad, shares_near, shares[3], hidden_parts, ffn_all, held, block_out
        )
        share_far = swap(shares[3], "blk", 3)
    cq_grad, mem_part = cross_backward(allow, cross_q, mem_key, mem_value, cross_lse, mix_grad)
    if fast:
        held = slabs(order, cross_in, cq_grad, total, d_slabs * small, total, held)
        held = slabs(order, mem_all, mem_part, total, 2 * d_slabs * small, 0, held)
        cq_grad, mem_part, share_far, held = tie(cq_grad, mem_part, share_far, held)
    grad_self, self_grad, d_gain_cross, grad_parts = norm_grad(
        grad_cross, [cq_grad], [cross_query], after_self, norm_cross, out_turned, d
    )
    grad_got = trade(grad_parts, "blk", 1)
    if fast:
        share_far, held, self_late = tie(share_far, held, self_grad)
        wide = pair_dot(my_ref, ffn_all, [shares[0]] + shares_near + [share_far])
        keep, send = slabs(turned, mixes, self_late, total, 3 * d_slabs * small, 0, held)
        grad_got, wide, keep, hidden_parts = tie(grad_got, wide, keep, hidden_parts)
        got = swap(send, "dp", 1)
        hidden_got = trade(hidden_parts, "blk", 1)
        wide = lax.psum_scatter(wide, "dp", scatter_dimension=0, tiled=True)
        cross = Halves(keep, got, [(0, total // 2)], [(total // 2, total)])
        cross.pack()
        grad_got, cross.out = tie(grad_got, cross.out)
        cross.hop((1, 2))
    qkv_parts, bias_grad = self_backward(blocks, my_ref, qkv, bias, own_mix, lse, [grad_parts[0]] + grad_got)
    d_table = lax.dot_general(bucket_hot, bias_grad[:, length:], (((0,), (1,)), ((), ())), precision=lax.Precision.HIGHEST)
    d_table = lax.dynamic_update_slice_in_dim(jnp.zeros_like(bias_table), d_table, my * own_heads, 1)
    if fast:
        qkv_parts, mem_part, cross.got = tie(qkv_parts, mem_part, cross.got)
        cross.arrive()
        cross.pack()
        qkv_parts, cross.out, hidden_got = tie(qkv_parts, cross.out, hidden_got)
        cross.hop((2, 1))
        own = own_q + 2 * own_kv
        keep, send, gain_part = slabs(order, self_all, qkv_parts, small, 0, 0, None, 2, own, turned_qkv[0])
        gain_part = gain_part[:, 0]
        view = (-1, blocks * small, own)
        got = swap(send, "dp", 1)
        sides = [(keep.reshape(view), cover((0, view[1]))), (got.reshape(view), cover((0, view[1])))]
        sides = totals(sides, [(0, cross.chunks, [(j * small, (j + 1) * small)]) for j in range(blocks)], 1)
        sides = [sides[0]] + trade(sides, "blk", 1)
        down = turned_dot(my_ref, [hidden_parts[0]] + hidden_got, top_all)
        gain_part, cross.got, sides, wide, down = tie(gain_part, cross.got, sides, wide, down)
        down = lax.psum_scatter(down, "dp", scatter_dimension=0, tiled=True)
        cross.arrive()
        cross.join([(side, cover((total + j * small, total + (j + 1) * small))) for j, side in enumerate(sides)], total + view[1])
        cross.pack(True)
        gain_part, cross.out, d_table, wide, mem_part = tie(gain_part, cross.out, d_table, wide, mem_part)
        cross.hop_deep(2)
        wides = [lax.dynamic_slice_in_dim(wide, (my ^ j) * small, small, 0) for j in range(blocks)]
        wides_got = trade(wides, "blk", 1)
    else:
        attn, gain_part = dot_gain(self_all, jnp.concatenate(qkv_parts, axis=0), turned_qkv[0])
        gain_part = gain_part[:, 0]
    d_gain_self = gain_part / norm_self
    lines = jnp.concatenate([d_gain_self, d_gain_cross, d_gain_ffn, d_table.reshape(-1)]).reshape(-1, LANES)
    mem_blocks = mem_part.reshape(2, blocks, mem_rows, kv_width)
    bit = blocks // 2
    while bit:
        mem_blocks = add16(mem_blocks[:, :bit], swap(mem_blocks[:, bit:], "blk", bit))
        bit //= 2
    mem_grad = mem_blocks[:, 0]
    if fast:
        lines = sum_axis(sum_axis(lines, "dp", 1), "blk", blocks // 2)
        cross.got, lines, mem_grad, wides_got, qkv_parts = tie(cross.got, lines, mem_grad, wides_got, qkv_parts)
        cross.arrive()
        cross.pack(True)
        lines, mem_grad, qkv_parts, cross.out = tie(lines, mem_grad, qkv_parts, cross.out)
        cross.hop_deep(4)
    qkv_got = trade(qkv_parts, "blk", 1)
    d_memory = dot32(mem_grad[0], cross_key, NT) + dot32(mem_grad[1], cross_value, NT)
    if fast:
        qkv_got, d_memory = tie(qkv_got, d_memory)
    d_block_in, _, _, _ = norm_grad(
        grad_self, [qkv_parts[0]] + qkv_got, turned_qkv, block_in[0], norm_self, [], own_q + 2 * own_kv
    )
    if fast:
        lines = sum_axis(lines, "dp", lax.axis_size("dp") // 2, 2).reshape(-1)
        dw_gate, dw_up = place(my_ref, [wides[0]] + wides_got)
        dw_down = down[0].astype(F32)
        d_block_in, cross.got, lines, dw_gate, dw_up, dw_down = tie(d_block_in, cross.got, lines, dw_gate, dw_up, dw_down)
        cross.arrive()
    else:
        lines = sum_axis(sum_axis(lines, "dp", lax.axis_size("dp") // 2), "blk", blocks // 2).reshape(-1)
    gain_self, gain_cross, gain_ffn = lines[:d], lines[d : 2 * d], lines[2 * d : 3 * d]
    table_sum = lines[3 * d :].reshape(bias_table.shape)
    if fast:
        shapes = [(small, d), (small, d), (small, kv_width), (small, kv_width), (small, d)]
        outs, row = [], 0
        for number, (_, width) in enumerate(shapes):
            for k in range(width // SLAB):
                outs.append((row, small, number, k * SLAB))
                row += small
        shapes += [(small, d), (small, kv_width), (small, kv_width)]
        dealt = [(j, row + j * small, small, ((5, own_q), (6, own_kv), (7, own_kv))) for j in range(blocks)]
        dw_co, dw_cq, dw_ck, dw_cv, dw_o, dw_q, dw_k, dw_v = finish(my_ref, cross.pieces, shapes, outs, dealt)
        ffn_outs = (dw_gate, dw_up, dw_down)
    else:
        dw_co = sum_rows(dot32(cross_mix, cross_grad, TN).astype(BF16), 0)
        dw_cq = sum_rows(dot32(cross_in, cq_grad, TN).astype(BF16), 1)
        dw_ck = sum_rows(dot32(mem_all, mem_part[0], TN).astype(BF16), 0)
        dw_cv = sum_rows(dot32(mem_all, mem_part[1], TN).astype(BF16), 1)
        dw_o = sum_rows(turn_rows(dot32(jnp.concatenate(mixes, axis=1), self_grad, TN).astype(BF16), own_q), 0)
        dw_q, dw_k, dw_v = [
            sum_rows(lax.dynamic_update_slice_in_dim(jnp.zeros((d, width), BF16), attn[:, low : low + width // blocks], my * (width // blocks), 1), 0)
            for width, low in ((blocks * own_q, 0), (kv_width, own_q), (kv_width, own_q + own_kv))
        ]
    return (
        block_out[None],
        d_block_in[None],
        d_memory[None],
        table_sum,
        gain_self,
        dw_q,
        dw_k,
        dw_v,
        dw_o,
        gain_cross,
        dw_cq,
        dw_ck,
        dw_cv,
        dw_co,
        gain_ffn,
        *ffn_outs,
    )


def solution(mesh):
    rows = P("dp", "blk", None)
    split = P(("dp", "blk"), None)
    whole = P()
    return jax.shard_map(
        body,
        mesh=mesh,
        in_specs=(rows, rows, P("dp"), P("dp", None)) + (whole,) * 16 + (rows,),
        out_specs=(rows, rows, rows, whole, whole)
        + (split,) * 4
        + (whole,)
        + (split,) * 4
        + (whole,)
        + (split,) * 3,
        check_vma=False,
    )
```

```python
import functools

import jax
import jax.numpy as jnp
from jax import lax
from jax.experimental import pallas as pl
from jax.experimental.pallas import tpu as pltpu
from jax.sharding import PartitionSpec as P

HEAD_DIM = 64
EPSILON = 1e-06
NEGATIVE = -1e30
SCALE = HEAD_DIM ** (-0.5)
LANES = 128
PAIR = 2 * HEAD_DIM
SLAB = 512
STEP_ELEMENTS = 768 * 1024
F32 = jnp.float32
BF16 = jnp.bfloat16
VMEM_SMALL = 28 * 1024 * 1024
VMEM_LARGE = 56 * 1024 * 1024

NT = (((1,), (1,)), ((), ()))
NN = (((1,), (0,)), ((), ()))
TN = (((0,), (0,)), ((), ()))


def dot32(a, b, dims=NN):
    return lax.dot_general(a, b, dims, preferred_element_type=F32)


def swap(x, axis, bit):
    return lax.ppermute(x, axis, [(i, i ^ bit) for i in range(lax.axis_size(axis))])


def trade(parts, axis, bit):
    return [swap(part, axis, k * bit) for k, part in enumerate(parts) if k]


def tie(*groups):
    return lax.optimization_barrier(groups)


def row_blocks(x, count):
    length = x.shape[0] // count
    return [x[k * length : (k + 1) * length] for k in range(count)]


def column_blocks(x, count):
    width = x.shape[1] // count
    return [x[:, k * width : (k + 1) * width] for k in range(count)]


def add16(a, b):
    return (a.astype(F32) + b.astype(F32)).astype(BF16)


def sum_axis(x, axis, last, bit=1):
    while bit <= last:
        x = x + swap(x, axis, bit)
        bit *= 2
    return x


def sum_rows(x, first_blk_bit):
    dp_bits = lax.axis_size("dp").bit_length() - 1
    blk_bits = lax.axis_size("blk").bit_length() - 1
    rest = [("dp", k) for k in reversed(range(dp_bits))] + [("blk", k) for k in reversed(range(blk_bits))]
    rows, width = x.shape
    x = x.reshape((2,) * len(rest) + (rows >> len(rest), width))
    order = [("dp", 0)]
    order += [("blk", (first_blk_bit + k) % blk_bits) for k in range(blk_bits)]
    order += [("dp", k) for k in range(1, dp_bits)]
    for axis, k in order:
        place = rest.index((axis, k))
        mine = (lax.axis_index(axis) >> k) & 1
        out = lax.dynamic_index_in_dim(x, 1 - mine, place, keepdims=False)
        keep = lax.dynamic_index_in_dim(x, mine, place, keepdims=False)
        got = swap(out, axis, 1 << k)
        rest.pop(place)
        x = keep.astype(F32) + got.astype(F32)
        if rest:
            x = x.astype(BF16)
    return x


def stacked(ref, kv):
    low = kv * PAIR
    return jnp.concatenate([ref[:, low : low + HEAD_DIM], ref[:, low + HEAD_DIM : low + PAIR]], axis=0)


def unstack(ref, kv, columns):
    length = columns.shape[1] // 2
    rows = columns.T
    low = kv * PAIR
    ref[:, low : low + HEAD_DIM] = rows[:length].astype(ref.dtype)
    ref[:, low + HEAD_DIM : low + PAIR] = rows[length:].astype(ref.dtype)


def spread_bias(bias_ref, tile_ref):
    heads, width = bias_ref.shape
    for h in range(heads):
        line = jnp.broadcast_to(bias_ref[h : h + 1, :], (LANES, width))
        tile_ref[h] = pltpu.roll(line, 0, 1, stride=1, stride_axis=0)


def bias_tile(tile_ref, kv, start, length):
    heads = []
    for g in range(2):
        parts = [
            tile_ref[2 * kv + g, :, pl.ds(pl.multiple_of(start - LANES * m, LANES), length)]
            for m in range(length // LANES)
        ]
        heads.append(jnp.concatenate(parts, axis=0))
    return jnp.concatenate(heads, axis=1)


def head_columns(kv_local, kv):
    return kv * PAIR, kv_local * PAIR + kv * HEAD_DIM, kv_local * (PAIR + HEAD_DIM) + kv * HEAD_DIM


def two_heads(ref, rows, low):
    return jnp.concatenate([ref[rows, low : low + HEAD_DIM], ref[rows, low + HEAD_DIM : low + PAIR]], axis=0)


def self_forward_kernel(blocks, kv_local, my_ref, qkv_ref, bias_ref, *refs):
    mix_refs, (lse_ref, tile_ref, top_ref, sum_ref, acc_ref) = refs[:blocks], refs[blocks:]
    a = pl.program_id(0)
    length = qkv_ref.shape[0] // blocks
    my = my_ref[0]
    mine = my ^ a

    @pl.when(a == 0)
    def _():
        spread_bias(bias_ref, tile_ref)

    rows = pl.ds(pl.multiple_of(a * length, length), length)
    top_ref[...] = jnp.full_like(top_ref, NEGATIVE)
    sum_ref[...] = jnp.zeros_like(sum_ref)
    acc_ref[...] = jnp.zeros_like(acc_ref)
    for b in range(blocks):
        source = my ^ b
        keys_at = slice(b * length, (b + 1) * length)

        @pl.when(source <= mine)
        def _(source=source, keys_at=keys_at):
            start = length + length * (mine - source)
            for kv in range(kv_local):
                q_at, k_at, v_at = head_columns(kv_local, kv)
                qq = two_heads(qkv_ref, rows, q_at)
                keys = qkv_ref[keys_at, k_at : k_at + HEAD_DIM]
                values = qkv_ref[keys_at, v_at : v_at + HEAD_DIM]
                scores = dot32(keys, qq, NT) * SCALE + bias_tile(tile_ref, kv, start, length)
                old = top_ref[kv]
                new = jnp.maximum(old, jnp.max(scores, axis=0, keepdims=True))
                weights = jnp.exp(scores - new)
                shrink = jnp.exp(old - new)
                top_ref[kv] = new
                sum_ref[kv] = sum_ref[kv] * shrink + jnp.sum(weights, axis=0, keepdims=True)
                acc_ref[kv] = acc_ref[kv] * shrink + dot32(values, weights.astype(BF16), TN)

    for kv in range(kv_local):
        lse_ref[0, kv] = top_ref[kv] + jnp.log(sum_ref[kv])
    for b, mix_ref in enumerate(mix_refs):

        @pl.when(a == b)
        def _(mix_ref=mix_ref):
            for kv in range(kv_local):
                unstack(mix_ref, kv, acc_ref[kv] / sum_ref[kv])


def self_backward_kernel(blocks, kv_local, my_ref, qkv_ref, bias_ref, lse_ref, *refs):
    mix_refs, grad_refs, out_refs = refs[:blocks], refs[blocks : 2 * blocks], refs[2 * blocks : 3 * blocks]
    dbias_ref, tile_ref, diag_ref, dq_ref, dk_ref, dv_ref, grad_ref, mix_ref = refs[3 * blocks :]
    a = pl.program_id(0)
    length = qkv_ref.shape[0] // blocks
    width = bias_ref.shape[1]
    my = my_ref[0]
    mine = my ^ a

    @pl.when(a == 0)
    def _():
        spread_bias(bias_ref, tile_ref)
        diag_ref[...] = jnp.zeros_like(diag_ref)
        dk_ref[...] = jnp.zeros_like(dk_ref)
        dv_ref[...] = jnp.zeros_like(dv_ref)

    rows = pl.ds(pl.multiple_of(a * length, length), length)
    every = slice(0, length)
    for b in range(blocks):

        @pl.when(a == b)
        def _(b=b):
            grad_ref[...] = grad_refs[b][...]
            mix_ref[...] = mix_refs[b][...]

    dq_ref[...] = jnp.zeros_like(dq_ref)
    deltas = []
    for kv in range(kv_local):
        both = two_heads(grad_ref, every, kv * PAIR).astype(F32) * two_heads(mix_ref, every, kv * PAIR).astype(F32)
        deltas.append(jnp.sum(both.T, axis=0, keepdims=True))
    for b in range(blocks):
        source = my ^ b
        keys_at = slice(b * length, (b + 1) * length)

        @pl.when(source <= mine)
        def _(source=source, keys_at=keys_at):
            start = length + length * (mine - source)
            for kv in range(kv_local):
                q_at, k_at, v_at = head_columns(kv_local, kv)
                qq = two_heads(qkv_ref, rows, q_at)
                dd = two_heads(grad_ref, every, q_at)
                keys = qkv_ref[keys_at, k_at : k_at + HEAD_DIM]
                values = qkv_ref[keys_at, v_at : v_at + HEAD_DIM]
                scores = dot32(keys, qq, NT) * SCALE + bias_tile(tile_ref, kv, start, length)
                probs = jnp.exp(scores - lse_ref[0, kv])
                dv_ref[kv, keys_at, :] += dot32(probs.astype(BF16), dd)
                change = dot32(values, dd, NT) - deltas[kv]
                ds = (probs * change).astype(BF16)
                dk_ref[kv, keys_at, :] += dot32(ds, qq)
                dq_ref[kv] += dot32(keys, ds, TN)
                ds = ds.astype(F32)
                for g in range(2):
                    for m in range(length // LANES):
                        where = pl.ds(pl.multiple_of(start - LANES * m, LANES), length)
                        diag_ref[2 * kv + g, :, where] += ds[m * LANES : (m + 1) * LANES, g * length : (g + 1) * length]

    for b in range(blocks):

        @pl.when(a == b)
        def _(out_ref=out_refs[b]):
            for kv in range(kv_local):
                back = (dq_ref[kv] * SCALE).T.astype(BF16)
                out_ref[:, kv * PAIR : kv * PAIR + HEAD_DIM] = back[:length]
                out_ref[:, kv * PAIR + HEAD_DIM : (kv + 1) * PAIR] = back[length:]

    @pl.when(a == blocks - 1)
    def _():
        for kv in range(kv_local):
            _, k_at, v_at = head_columns(kv_local, kv)
            for b, out_ref in enumerate(out_refs):
                keys_at = slice(b * length, (b + 1) * length)
                out_ref[:, k_at : k_at + HEAD_DIM] = (dk_ref[kv, keys_at, :] * SCALE).astype(BF16)
                out_ref[:, v_at : v_at + HEAD_DIM] = dv_ref[kv, keys_at, :].astype(BF16)
        for h in range(2 * kv_local):
            part = diag_ref[h]
            half = LANES // 2
            while half:
                part = part[:half] + pltpu.roll(part[half:], width - half, 1)
                half //= 2
            dbias_ref[h : h + 1, :] = part


def cross_forward_kernel(allow_ref, q_ref, k_ref, v_ref, mix_ref, lse_ref):
    allow = allow_ref[...] > 0
    for kv in range(2):
        low = kv * HEAD_DIM
        qq = stacked(q_ref, kv)
        scores = dot32(k_ref[:, low : low + HEAD_DIM], qq, NT) * SCALE
        scores = jnp.where(allow, scores, NEGATIVE)
        top = jnp.max(scores, axis=0, keepdims=True)
        raised = jnp.exp(scores - top)
        total = jnp.sum(raised, axis=0, keepdims=True)
        probs = (raised * (1.0 / total)).astype(BF16)
        unstack(mix_ref, kv, dot32(v_ref[:, low : low + HEAD_DIM], probs, TN))
        lse_ref[kv] = top + jnp.log(total)


def cross_backward_kernel(allow_ref, q_ref, k_ref, v_ref, lse_ref, grad_ref, dq_ref, dkv_ref):
    allow = allow_ref[...] > 0
    for kv in range(2):
        low = kv * HEAD_DIM
        qq = stacked(q_ref, kv)
        dd = stacked(grad_ref, kv)
        keys = k_ref[:, low : low + HEAD_DIM]
        scores = jnp.where(allow, dot32(keys, qq, NT) * SCALE, NEGATIVE)
        probs = jnp.exp(scores - lse_ref[kv])
        change = dot32(v_ref[:, low : low + HEAD_DIM], dd, NT)
        delta = jnp.sum(probs * change, axis=0, keepdims=True)
        ds = (probs * (change - delta)).astype(BF16)
        dkv_ref[1, :, low : low + HEAD_DIM] = dot32(probs.astype(BF16), dd).astype(BF16)
        dkv_ref[0, :, low : low + HEAD_DIM] = (dot32(ds, qq) * SCALE).astype(BF16)
        unstack(dq_ref, kv, dot32(keys, ds, TN) * SCALE)


TINY = pl.CostEstimate(flops=1, transcendentals=0, bytes_accessed=1)


def params(limit=VMEM_SMALL):
    return pltpu.CompilerParams(dimension_semantics=("arbitrary",), vmem_limit_bytes=limit)


def cost(length, keys, heads, passes, moved):
    return pl.CostEstimate(
        flops=2 * length * keys * heads * HEAD_DIM * passes,
        transcendentals=length * keys * heads,
        bytes_accessed=moved,
    )


def lane_block(rows, width):
    return pl.BlockSpec((rows, width), lambda i: (0, i))


def self_forward(blocks, my, qkv, bias):
    tokens, columns = qkv.shape
    length, kv_local, width = tokens // blocks, columns // (2 * PAIR), bias.shape[1]
    q_width = kv_local * PAIR
    return pl.pallas_call(
        functools.partial(self_forward_kernel, blocks, kv_local),
        grid=(blocks,),
        in_specs=[
            pl.BlockSpec(memory_space=pltpu.SMEM),
            pl.BlockSpec((tokens, columns), lambda i: (0, 0)),
            pl.BlockSpec(bias.shape, lambda i: (0, 0)),
        ],
        out_specs=[pl.BlockSpec((length, q_width), lambda i: (0, 0))] * blocks
        + [pl.BlockSpec((1, kv_local, 1, 2 * length), lambda i: (i, 0, 0, 0))],
        out_shape=[jax.ShapeDtypeStruct((length, q_width), BF16)] * blocks
        + [jax.ShapeDtypeStruct((blocks, kv_local, 1, 2 * length), F32)],
        scratch_shapes=[
            pltpu.VMEM((2 * kv_local, LANES, width), F32),
            pltpu.VMEM((kv_local, 1, 2 * length), F32),
            pltpu.VMEM((kv_local, 1, 2 * length), F32),
            pltpu.VMEM((kv_local, HEAD_DIM, 2 * length), F32),
        ],
        compiler_params=params(),
        cost_estimate=TINY,
        name="self_forward",
    )(my, qkv, bias)


def self_backward(blocks, my, qkv, bias, mixes, lse, grads):
    tokens, columns = qkv.shape
    length, kv_local, width = tokens // blocks, columns // (2 * PAIR), bias.shape[1]
    q_width = kv_local * PAIR
    lines = pl.BlockSpec(bias.shape, lambda i: (0, 0))
    *outs, d_bias = pl.pallas_call(
        functools.partial(self_backward_kernel, blocks, kv_local),
        grid=(blocks,),
        in_specs=[
            pl.BlockSpec(memory_space=pltpu.SMEM),
            pl.BlockSpec((tokens, columns), lambda i: (0, 0)),
            lines,
            pl.BlockSpec((1, kv_local, 1, 2 * length), lambda i: (i, 0, 0, 0)),
        ]
        + [pl.BlockSpec((length, q_width), lambda i: (0, 0))] * (2 * blocks),
        out_specs=[pl.BlockSpec((length, columns), lambda i: (0, 0))] * blocks + [lines],
        out_shape=[jax.ShapeDtypeStruct((length, columns), BF16)] * blocks + [jax.ShapeDtypeStruct(bias.shape, F32)],
        scratch_shapes=[
            pltpu.VMEM((2 * kv_local, LANES, width), F32),
            pltpu.VMEM((2 * kv_local, LANES, width), F32),
            pltpu.VMEM((kv_local, HEAD_DIM, 2 * length), F32),
            pltpu.VMEM((kv_local, tokens, HEAD_DIM), F32),
            pltpu.VMEM((kv_local, tokens, HEAD_DIM), F32),
            pltpu.VMEM((length, q_width), BF16),
            pltpu.VMEM((length, q_width), BF16),
        ],
        compiler_params=params(),
        cost_estimate=TINY,
        name="self_backward",
    )(my, qkv, bias, lse, *mixes, *grads)
    return outs, d_bias


def cross_forward(allow, q, k, v):
    length, keys, kv_heads = q.shape[0], k.shape[0], k.shape[1] // HEAD_DIM
    return pl.pallas_call(
        cross_forward_kernel,
        grid=(kv_heads // 2,),
        in_specs=[
            pl.BlockSpec((keys, 1), lambda i: (0, 0)),
            lane_block(length, 2 * PAIR),
            lane_block(keys, PAIR),
            lane_block(keys, PAIR),
        ],
        out_specs=[
            lane_block(length, 2 * PAIR),
            pl.BlockSpec((2, 1, 2 * length), lambda i: (i, 0, 0)),
        ],
        out_shape=[
            jax.ShapeDtypeStruct(q.shape, BF16),
            jax.ShapeDtypeStruct((kv_heads, 1, 2 * length), F32),
        ],
        compiler_params=params(),
        cost_estimate=TINY,
        name="cross_forward",
    )(allow, q, k, v)


def cross_backward(allow, q, k, v, lse, grad):
    length, keys, kv_heads = q.shape[0], k.shape[0], k.shape[1] // HEAD_DIM
    return pl.pallas_call(
        cross_backward_kernel,
        grid=(kv_heads // 2,),
        in_specs=[
            pl.BlockSpec((keys, 1), lambda i: (0, 0)),
            lane_block(length, 2 * PAIR),
            lane_block(keys, PAIR),
            lane_block(keys, PAIR),
            pl.BlockSpec((2, 1, 2 * length), lambda i: (i, 0, 0)),
            lane_block(length, 2 * PAIR),
        ],
        out_specs=[
            lane_block(length, 2 * PAIR),
            pl.BlockSpec((2, keys, PAIR), lambda i: (0, 0, i)),
        ],
        out_shape=[
            jax.ShapeDtypeStruct(q.shape, BF16),
            jax.ShapeDtypeStruct((2,) + k.shape, BF16),
        ],
        compiler_params=params(),
        cost_estimate=TINY,
        name="cross_backward",
    )(allow, q, k, v, lse, grad)


def slab_kernel(kind, later, x_count, g_count, gained, order_ref, *refs):
    xs, gs = refs[:x_count], refs[x_count : x_count + g_count]
    turned_ref, whole_ref = refs[-2:]
    keep_ref, send_ref = refs[-5:-3] if gained else refs[-4:-2]
    slab = pl.program_id(0)
    kind = jnp.where(slab < later, 0, 1) if kind is None else kind

    @pl.when(slab == 0)
    def _():
        low = 0
        for x in xs:
            turned_ref[low : low + x.shape[1], :] = x[...].T
            low += x.shape[1]

    chunks, rows, width = whole_ref.shape
    g = gs[0][...] if g_count == 1 else jnp.concatenate([ref[...] for ref in gs], axis=0)
    full = dot32(turned_ref[...], g)
    whole_ref[...] = full.reshape(chunks, rows, width)
    half = chunks // 2
    for c in range(half):
        keep_ref[c] = whole_ref[order_ref[kind, c]].astype(BF16)
        send_ref[c] = whole_ref[order_ref[kind, half + c]].astype(BF16)
    if gained:
        refs[-3][...] = jnp.sum(full * refs[x_count + g_count][...].astype(F32), axis=1, keepdims=True)


def slabs(order, x, g, total, at, later, buffers, kind=None, slab=SLAB, weight=None):
    xs = x if isinstance(x, list) else [x]
    tokens, features = xs[0].shape[0], sum(part.shape[1] for part in xs)
    chunks = order.shape[1]
    rows = features // chunks
    gs = g if isinstance(g, list) else [g]
    if len(gs) > 1:
        count, g_specs = 1, whole_blocks(gs)
    elif g.ndim == 3:
        count, g_specs = g.shape[0], [pl.BlockSpec((None, tokens, slab), lambda i: (i, 0, 0))]
    else:
        count, g_specs = g.shape[1] // slab, [pl.BlockSpec((tokens, slab), lambda i: (0, i))]
    assert at % rows == 0 and features % chunks == 0 and rows % 8 == 0
    out = pl.BlockSpec((chunks // 2, rows, slab), lambda i: (0, at // rows + i, 0))
    shapes = [jax.ShapeDtypeStruct((chunks // 2, total, slab), BF16)] * 2
    outs = [out, out]
    extra = [] if buffers is None else list(buffers)
    first = 1 + len(xs) + len(gs)
    weights = []
    if weight is not None:
        weights = [weight]
        shapes.append(jax.ShapeDtypeStruct((features, 1), F32))
        outs.append(pl.BlockSpec((features, 1), lambda i: (0, 0)))
    return pl.pallas_call(
        functools.partial(slab_kernel, kind, later, len(xs), len(gs), weight is not None),
        grid=(count,),
        in_specs=[pl.BlockSpec(memory_space=pltpu.SMEM)]
        + whole_blocks(xs)
        + g_specs
        + whole_blocks(weights)
        + [pl.BlockSpec(memory_space=pl.ANY)] * len(extra),
        out_specs=outs,
        out_shape=shapes,
        scratch_shapes=[pltpu.VMEM((features, tokens), BF16), pltpu.VMEM((chunks, rows, slab), F32)],
        input_output_aliases={first: 0, first + 1: 1} if extra else {},
        compiler_params=params(VMEM_LARGE),
        cost_estimate=TINY,
        name="slabs",
    )(order, *xs, *gs, *weights, *extra)


def cover(*ranges):
    held, row = [], 0
    for low, high in ranges:
        held.append((low, high, row))
        row += high - low
    return held


def add_range(sources, refs, low, high):
    total = None
    for number, segments in sources:
        for start, stop, row in segments:
            if start <= low and high <= stop:
                part = refs[number][:, row + low - start : row + high - start, :].astype(F32)
                total = part if total is None else total + part
    return total


def cut_points(pieces, low, high):
    marks = {low, high}
    for _, segments in pieces:
        marks |= {m for start, stop, _ in segments for m in (start, stop) if low < m < high}
    marks = sorted(marks)
    return list(zip(marks[:-1], marks[1:]))


def total_kernel(plan, *refs):
    inputs, results = refs[: -len(plan)], refs[-len(plan) :]
    for (sources, writes), result in zip(plan, results):
        for row, low, high in writes:
            result[:, row : row + high - low, :] = add_range(sources, inputs, low, high).astype(result.dtype)


def totals(pieces, groups, steps):
    plan, specs, arrays, shapes, outs = [], [], [], [], []
    width = pieces[0][0].shape[2]
    for first, count, ranges in groups:
        step = count // steps
        sources = []
        for array, segments in pieces:
            sources.append((len(arrays), segments))
            arrays.append(array)
            specs.append(pl.BlockSpec((step,) + array.shape[1:], lambda i, low=first // step: (low + i, 0, 0)))
        writes, rows = [], 0
        for low, high in ranges:
            for a, b in cut_points(pieces, low, high):
                writes.append((rows, a, b))
                rows += b - a
        plan.append((sources, writes))
        outs.append(pl.BlockSpec((step, rows, width), lambda i: (i, 0, 0)))
        shapes.append(jax.ShapeDtypeStruct((count, rows, width), BF16))
    return pl.pallas_call(
        functools.partial(total_kernel, plan),
        grid=(steps,),
        in_specs=specs,
        out_specs=outs,
        out_shape=shapes,
        compiler_params=params(VMEM_LARGE),
        cost_estimate=TINY,
        name="totals",
    )(*arrays)


def finish_kernel(sources, outs, dealt, my_ref, *refs):
    inputs, results = refs[: len(sources)], refs[len(sources) :]
    for row, rows, number, column in outs:
        results[number][:, column : column + SLAB] = add_range(sources, inputs, row, row + rows)[0]
    for j, row, rows, parts in dealt:
        block = add_range(sources, inputs, row, row + rows)[0]
        low = 0
        for number, width in parts:
            columns = pl.ds(pl.multiple_of((my_ref[0] ^ j) * width, LANES), width)
            results[number][:, columns] = block[:, low : low + width]
            low += width


def finish(my, pieces, shapes, outs, dealt):
    sources = [(number, segments) for number, (_, segments) in enumerate(pieces)]
    return pl.pallas_call(
        functools.partial(finish_kernel, sources, outs, dealt),
        grid=(1,),
        in_specs=[pl.BlockSpec(memory_space=pltpu.SMEM)]
        + [pl.BlockSpec((1,) + array.shape[1:], lambda i: (0, 0, 0)) for array, _ in pieces],
        out_specs=[pl.BlockSpec(shape, lambda i: (0, 0)) for shape in shapes],
        out_shape=[jax.ShapeDtypeStruct(shape, F32) for shape in shapes],
        compiler_params=params(VMEM_LARGE),
        cost_estimate=TINY,
        name="finish",
    )(my, *[array for array, _ in pieces])


def pair_dot_kernel(my_ref, x_ref, *refs):
    gs, result = refs[:-1], refs[-1]
    x = jnp.concatenate([x_ref[my_ref[0] ^ j] for j in range(len(gs))], axis=0)
    g = jnp.concatenate([ref[...] for ref in gs], axis=0)
    result[...] = dot32(x, g, TN).astype(BF16)


def whole_blocks(arrays):
    return [pl.BlockSpec(a.shape, lambda i, n=a.ndim: (0,) * n) for a in arrays]


def pair_dot(my, x, gs):
    features, width = x.shape[1], gs[0].shape[1]
    x = x.reshape(len(gs), -1, features)
    return pl.pallas_call(
        pair_dot_kernel,
        grid=(1,),
        in_specs=[pl.BlockSpec(memory_space=pltpu.SMEM)] + whole_blocks([x, *gs]),
        out_specs=pl.BlockSpec((features, width), lambda i: (0, 0)),
        out_shape=jax.ShapeDtypeStruct((features, width), BF16),
        compiler_params=params(),
        cost_estimate=TINY,
        name="pair_dot",
    )(my, x, *gs)


def dot_gain_kernel(x_ref, g_ref, w_ref, out_ref, gain_ref):
    full = dot32(x_ref[...], g_ref[...], TN)
    out_ref[...] = full.astype(BF16)
    gain_ref[...] = jnp.sum(full * w_ref[...].astype(F32), axis=1, keepdims=True)


def dot_gain(x, g, w):
    features, width = w.shape
    return pl.pallas_call(
        dot_gain_kernel,
        grid=(1,),
        in_specs=whole_blocks([x, g, w]),
        out_specs=[pl.BlockSpec((features, width), lambda i: (0, 0)), pl.BlockSpec((features, 1), lambda i: (0, 0))],
        out_shape=[jax.ShapeDtypeStruct((features, width), BF16), jax.ShapeDtypeStruct((features, 1), F32)],
        compiler_params=params(),
        cost_estimate=TINY,
        name="dot_gain",
    )(x, g, w)


def add_norm_kernel(count, has_next, *refs):
    xs, ws = refs[:count], refs[count : 2 * count]
    base_ref, gain_ref = refs[2 * count : 2 * count + 2]
    total = base_ref[...].astype(F32)
    for x, w in zip(xs, ws):
        total = total + dot32(x[...], w[...])
    normed = (total * inverse_rms(total) * gain_ref[...]).astype(BF16)
    if has_next:
        next_ref, total_ref, normed_ref, out_ref = refs[2 * count + 2 :]
        out_ref[...] = dot32(normed, next_ref[...]).astype(BF16)
    else:
        total_ref, normed_ref = refs[2 * count + 2 :]
    total_ref[...] = total
    normed_ref[...] = normed


def add_norm(base, xs, ws, gain, after=None):
    shapes = [jax.ShapeDtypeStruct(base.shape, F32), jax.ShapeDtypeStruct(base.shape, BF16)]
    inputs = [*xs, *ws, base, gain[None]]
    if after is not None:
        inputs.append(after)
        shapes.append(jax.ShapeDtypeStruct((base.shape[0], after.shape[1]), BF16))
    return pl.pallas_call(
        functools.partial(add_norm_kernel, len(xs), after is not None),
        grid=(1,),
        in_specs=whole_blocks(inputs),
        out_specs=whole_blocks(shapes),
        out_shape=shapes,
        compiler_params=params(),
        cost_estimate=TINY,
        name="add_norm",
    )(*inputs)


def norm_grad_kernel(count, nexts, *refs):
    gs, ws = refs[:count], refs[count : 2 * count]
    x_ref, gain_ref, base_ref = refs[2 * count : 2 * count + 3]
    after = refs[2 * count + 3 : 2 * count + 3 + nexts]
    grad_ref, low_ref, gain_grad_ref = refs[2 * count + 3 + nexts : 2 * count + 6 + nexts]
    outs, acc_ref = refs[2 * count + 6 + nexts : -1], refs[-1]
    step = pl.program_id(0)

    @pl.when(step == 0)
    def _():
        acc_ref[...] = jnp.zeros_like(acc_ref)

    part = None
    for g, w in zip(gs, ws):
        term = dot32(g[...], w[...], NT)
        part = term if part is None else part + term
    acc_ref[...] += part

    @pl.when(step == pl.num_programs(0) - 1)
    def _():
        total = acc_ref[...]
        x = x_ref[...].astype(F32)
        d_x, d_gain = norm_back(x, inverse_rms(x), gain_ref[...], total)
        grad = base_ref[...].astype(F32) + d_x
        low = grad.astype(BF16)
        grad_ref[...] = grad
        low_ref[...] = low
        gain_grad_ref[...] = d_gain[None]
        for w, out in zip(after, outs):
            out[...] = dot32(low, w[...], NT).astype(BF16)


def norm_grad(base, gs, ws, x, gain, after, tile):
    length, width = x.shape
    inner = gs[0].shape[1]
    fixed = [x, gain[None], base, *after]
    shapes = [
        jax.ShapeDtypeStruct(x.shape, F32),
        jax.ShapeDtypeStruct(x.shape, BF16),
        jax.ShapeDtypeStruct((1, width), F32),
    ] + [jax.ShapeDtypeStruct((length, w.shape[0]), BF16) for w in after]
    grad, low, d_gain, *outs = pl.pallas_call(
        functools.partial(norm_grad_kernel, len(gs), len(after)),
        grid=(inner // tile,),
        in_specs=[pl.BlockSpec((length, tile), lambda i: (0, i))] * len(gs)
        + [pl.BlockSpec((width, tile), lambda i: (0, i))] * len(ws)
        + whole_blocks(fixed),
        out_specs=whole_blocks(shapes),
        out_shape=shapes,
        scratch_shapes=[pltpu.VMEM((length, width), F32)],
        compiler_params=params(),
        cost_estimate=TINY,
        name="norm_grad",
    )(*gs, *ws, *fixed)
    return grad, low, d_gain[0], outs


def norm_dot_kernel(count, *refs):
    gain_ref, w_ref, normed_ref, out_ref = refs[count:]
    for k, ref in enumerate(refs[:count]):
        length = ref.shape[0]
        rows = slice(k * length, (k + 1) * length)
        x = ref[...].astype(F32)
        normed = (x * inverse_rms(x) * gain_ref[...]).astype(BF16)
        normed_ref[rows, :] = normed
        out_ref[rows, :] = dot32(normed, w_ref[...]).astype(BF16)


def norm_dot(xs, gain, w):
    rows = len(xs) * xs[0].shape[0]
    shapes = [(rows, w.shape[0]), (rows, w.shape[1])]
    return pl.pallas_call(
        functools.partial(norm_dot_kernel, len(xs)),
        grid=(1,),
        in_specs=whole_blocks([*xs, gain, w]),
        out_specs=[pl.BlockSpec(shape, lambda i: (0, 0)) for shape in shapes],
        out_shape=[jax.ShapeDtypeStruct(shape, BF16) for shape in shapes],
        compiler_params=params(),
        cost_estimate=TINY,
        name="norm_dot",
    )(*xs, gain, w)


def turn_kernel(my_ref, x_ref, *refs):
    results, chunk_ref = refs[:-1], refs[-1]
    count = len(results)
    chunk_ref[...] = x_ref[...].astype(F32).T.reshape(chunk_ref.shape)
    for j, result in enumerate(results):
        for k in range(result.shape[0]):
            result[k] = chunk_ref[k * count + (my_ref[0] ^ j)].astype(BF16)


def turn_chunks(my, x, blocks, devices):
    tokens, features = x.shape
    shape = (devices // blocks, features // devices, tokens)
    return pl.pallas_call(
        turn_kernel,
        grid=(1,),
        in_specs=[pl.BlockSpec(memory_space=pltpu.SMEM)] + whole_blocks([x]),
        out_specs=[pl.BlockSpec(shape, lambda i: (0, 0, 0))] * blocks,
        out_shape=[jax.ShapeDtypeStruct(shape, BF16)] * blocks,
        scratch_shapes=[pltpu.VMEM((devices, features // devices, tokens), F32)],
        compiler_params=params(),
        cost_estimate=TINY,
        name="turn_chunks",
    )(my, x)


def turned_dot_kernel(count, my_ref, *refs):
    xs, (g_ref, result) = refs[:count], refs[count:]
    chunks, rows, tokens = xs[0].shape
    total = None
    for j, ref in enumerate(xs):
        x = ref[...].astype(F32).reshape(chunks * rows, tokens).astype(BF16)
        term = dot32(x, g_ref[my_ref[0] ^ j])
        total = term if total is None else total + term
    result[...] = total.reshape(result.shape).astype(BF16)


def turned_dot(my, xs, g):
    chunks, rows, tokens = xs[0].shape
    width = g.shape[1]
    g = g.reshape(len(xs), tokens, width)
    return pl.pallas_call(
        functools.partial(turned_dot_kernel, len(xs)),
        grid=(1,),
        in_specs=[pl.BlockSpec(memory_space=pltpu.SMEM)] + whole_blocks([*xs, g]),
        out_specs=pl.BlockSpec((chunks, rows, width), lambda i: (0, 0, 0)),
        out_shape=jax.ShapeDtypeStruct((chunks, rows, width), BF16),
        compiler_params=params(),
        cost_estimate=TINY,
        name="turned_dot",
    )(my, *xs, g)


def place_kernel(my_ref, *refs):
    parts, results = refs[:-2], refs[-2:]
    per_half = len(parts) // 2
    share = parts[0].shape[1]
    for j, part in enumerate(parts):
        owner = my_ref[0] ^ j
        for number, result in enumerate(results):

            @pl.when(owner // per_half == number)
            def _(part=part, result=result, number=number, owner=owner):
                columns = pl.ds(pl.multiple_of((owner - number * per_half) * share, LANES), share)
                result[:, columns] = part[...].astype(F32)


def place(my, parts):
    shape = (parts[0].shape[0], len(parts) // 2 * parts[0].shape[1])
    return pl.pallas_call(
        place_kernel,
        grid=(1,),
        in_specs=[pl.BlockSpec(memory_space=pltpu.SMEM)] + whole_blocks(parts),
        out_specs=[pl.BlockSpec(shape, lambda i: (0, 0))] * 2,
        out_shape=[jax.ShapeDtypeStruct(shape, F32)] * 2,
        compiler_params=params(VMEM_LARGE),
        cost_estimate=TINY,
        name="place",
    )(my, *parts)


def exchange_order():
    dp, blk = lax.axis_size("dp"), lax.axis_size("blk")
    dp_bits, blk_bits = dp.bit_length() - 1, blk.bit_length() - 1
    mine = lax.axis_index("dp") * blk + lax.axis_index("blk")
    deep = list(range(blk_bits + 1, blk_bits + dp_bits))
    up, down = list(range(blk_bits)), list(reversed(range(blk_bits)))
    tables = []
    for order in (up + deep, down + deep, deep + down):
        order = [blk_bits] + order
        table = []
        for place in range(dp * blk):
            relative = 0
            for k, bit in enumerate(order):
                relative |= ((place >> (len(order) - 1 - k)) & 1) << bit
            table.append(relative)
        tables.append(table)
    return jnp.array(tables, jnp.int32) ^ mine.astype(jnp.int32)


class Halves:
    def __init__(self, keep, got, over_x, over_y):
        self.rows = [(0, keep.shape[1])]
        self.pieces = [(keep, cover(*self.rows)), (got, cover(*self.rows))]
        self.parts, self.chunks = (over_x, over_y), keep.shape[0]

    def pack(self, deep=False):
        half = self.chunks // 2
        parts = [self.rows] if deep else self.parts
        self.out = totals(self.pieces, [(half, half, part) for part in parts], 2 if half > 4 else 1)
        self.chunks = half

    def hop(self, bits):
        self.got = [swap(out, "blk", bit) for out, bit in zip(self.out, bits)]

    def join(self, pieces, end):
        self.pieces += pieces
        self.rows = [(0, end)]

    def hop_deep(self, bit):
        self.got = [swap(self.out[0], "dp", bit)]

    def arrive(self):
        parts = [self.rows] if len(self.got) == 1 else self.parts
        self.pieces += [(array, cover(*part)) for array, part in zip(self.got, parts)]


def turn_rows(x, rows):
    my = lax.axis_index("blk")
    return jnp.concatenate([lax.dynamic_slice_in_dim(x, (my ^ j) * rows, rows, 0) for j in range(lax.axis_size("blk"))], axis=0)


def inverse_rms(x):
    return lax.rsqrt(jnp.mean(x * x, axis=-1, keepdims=True) + EPSILON)


def norm_back(x, inverse, gain, grad):
    scaled = grad * gain
    along = jnp.mean(scaled * x, axis=-1, keepdims=True)
    d_x = inverse * scaled - x * (inverse * inverse * inverse * along)
    return d_x, jnp.sum(grad * (x * inverse), axis=0)


def body(
    block_in,
    memory,
    memory_len,
    cross_mask,
    buckets,
    bias_table,
    norm_self,
    w_query,
    w_key,
    w_value,
    w_out,
    norm_cross,
    cross_query,
    cross_key,
    cross_value,
    cross_out,
    norm_ffn,
    w_gate,
    w_up,
    w_down,
    grad_out,
):
    seq_count, length, model_width = block_in.shape
    assert seq_count == 1
    mem_rows = memory.shape[1]
    mem_total = cross_mask.shape[1]
    blocks = lax.axis_size("blk")
    my = lax.axis_index("blk")
    kv_width = w_key.shape[1]
    head_count = w_query.shape[1] // HEAD_DIM
    bucket_count = bias_table.shape[0]
    my_ref = my.reshape(1).astype(jnp.int32)

    x_parts = [block_in[0]] + trade([block_in[0]] * blocks, "blk", 1)

    own_heads = head_count // blocks
    own_q, own_kv = own_heads * HEAD_DIM, kv_width // blocks
    turned_qkv = [
        jnp.concatenate(
            [
                lax.dynamic_slice_in_dim(w, (my ^ j) * width, width, 1)
                for w, width in ((w_query, own_q), (w_key, own_kv), (w_value, own_kv))
            ],
            axis=1,
        )
        for j in range(blocks)
    ]
    out_turned = [lax.dynamic_slice_in_dim(w_out, (my ^ j) * own_q, own_q, 0) for j in range(blocks)]

    bucket_hot = (buckets[:, None] == jnp.arange(bucket_count)[None, :]).astype(F32)
    own_table = lax.dynamic_slice_in_dim(bias_table, my * own_heads, own_heads, 1)
    dist_bias = lax.dot_general(own_table, bucket_hot, (((0,), (1,)), ((), ())), precision=lax.Precision.HIGHEST)
    bias = jnp.concatenate([jnp.full((own_heads, length), NEGATIVE, F32), dist_bias], axis=1)

    mem_places = jnp.arange(mem_total)
    allowed = (mem_places == 0) | (mem_places < memory_len[0]) & (cross_mask[0] == 1)
    allow = allowed.astype(F32).reshape(blocks, mem_rows)[my ^ jnp.arange(blocks)].reshape(mem_total, 1)

    d_hidden = dot32(grad_out[0], w_down, NT)
    x_parts, mem_own, turned_qkv, out_turned, d_hidden, bias, allow, top_own = tie(
        x_parts, memory[0], turned_qkv, out_turned, d_hidden, bias, allow, grad_out[0]
    )
    top_all = lax.all_gather(top_own, "blk", axis=0, tiled=True)
    mem_all = jnp.concatenate([mem_own] + trade([mem_own] * blocks, "blk", 1), axis=0)
    self_all, qkv = norm_dot(x_parts, norm_self[None], turned_qkv[0])
    *own_mix, lse = self_forward(blocks, my_ref, qkv, bias)
    mem_key = dot32(mem_all, cross_key).astype(BF16)
    mem_value = dot32(mem_all, cross_value).astype(BF16)
    mix_got, mem_key, mem_value = tie(trade(own_mix, "blk", 1), mem_key, mem_value)
    mixes = [own_mix[0]] + mix_got
    after_self, cross_in, cross_q = add_norm(block_in[0], mixes, out_turned, norm_cross, cross_query)
    cross_mix, cross_lse = cross_forward(allow, cross_q, mem_key, mem_value)
    after_cross, ffn_in = add_norm(after_self, [cross_mix], [cross_out], norm_ffn)
    devices = blocks * lax.axis_size("dp")
    d, ff = model_width, w_gate.shape[1]
    share = 2 * ff // blocks
    fast = (
        blocks == 4
        and lax.axis_size("dp") == 8
        and d % (8 * devices) == 0
        and ff % (8 * devices) == 0
        and kv_width == SLAB
        and d % SLAB == 0
        and share % LANES == 0
    )
    gate = dot32(ffn_in, w_gate)
    up = dot32(ffn_in, w_up)
    (act, hidden_full), gated_back = jax.vjp(lambda g, u: (jax.nn.gelu(g, approximate=True), jax.nn.gelu(g, approximate=True) * u), gate, up)
    hidden = hidden_full.astype(BF16)

    ffn_grad = grad_out[0]
    gate_full, up_full = gated_back((jnp.zeros_like(act), d_hidden))
    gate_grad, up_grad = gate_full.astype(BF16), up_full.astype(BF16)
    if fast:
        order = exchange_order()
        turned = order ^ ((my * (devices // blocks)).astype(jnp.int32))
        small, large = d // devices, ff // devices
        d_slabs = d // SLAB
        top_all, ffn_late = tie(top_all, ffn_in)
        ffn_all = lax.all_gather(ffn_late, "blk", axis=0, tiled=True)
        both_grad = jnp.concatenate([gate_grad, up_grad], axis=1)
        shares = [lax.dynamic_slice_in_dim(both_grad, (my ^ j) * share, share, 1) for j in range(blocks)]
        shares, hidden = tie(shares, hidden)
        shares_near = trade(shares[:3], "blk", 1)
        hidden_parts = turn_chunks(my_ref, hidden, blocks, devices)
    else:
        dw_down = sum_rows(dot32(hidden, ffn_grad, TN).astype(BF16), 1)
        ffn_outs = (
            sum_rows(dot32(ffn_in, gate_grad, TN).astype(BF16), 0),
            sum_rows(dot32(ffn_in, up_grad, TN).astype(BF16), 1),
            dw_down,
        )
    tile = ff // 2 if ff % (2 * LANES) == 0 else ff
    grad_cross, cross_grad, d_gain_ffn, (mix_grad,) = norm_grad(
        ffn_grad, [gate_grad, up_grad], [w_gate, w_up], after_cross, norm_ffn, [cross_out], tile
    )
    block_out = (after_cross + dot32(hidden, w_down)).astype(BF16)
    if fast:
        total = 4 * d_slabs * small
        held = slabs(order, cross_mix, cross_grad, total, 0, total, None)
        mix_grad, shares_near, shares[3], hidden_parts, ffn_all, held, block_out = tie(
            mix_grad, shares_near, shares[3], hidden_parts, ffn_all, held, block_out
        )
        share_far = swap(shares[3], "blk", 3)
    cq_grad, mem_part = cross_backward(allow, cross_q, mem_key, mem_value, cross_lse, mix_grad)
    if fast:
        held = slabs(order, cross_in, cq_grad, total, d_slabs * small, total, held)
        held = slabs(order, mem_all, mem_part, total, 2 * d_slabs * small, 0, held)
        cq_grad, mem_part, share_far, held = tie(cq_grad, mem_part, share_far, held)
    grad_self, self_grad, d_gain_cross, grad_parts = norm_grad(
        grad_cross, [cq_grad], [cross_query], after_self, norm_cross, out_turned, d
    )
    grad_got = trade(grad_parts, "blk", 1)
    if fast:
        share_far, held, self_late = tie(share_far, held, self_grad)
        wide = pair_dot(my_ref, ffn_all, [shares[0]] + shares_near + [share_far])
        keep, send = slabs(turned, mixes, self_late, total, 3 * d_slabs * small, 0, held)
        grad_got, wide, keep, hidden_parts = tie(grad_got, wide, keep, hidden_parts)
        got = swap(send, "dp", 1)
        hidden_got = trade(hidden_parts, "blk", 1)
        wide = lax.psum_scatter(wide, "dp", scatter_dimension=0, tiled=True)
        cross = Halves(keep, got, [(0, total // 2)], [(total // 2, total)])
        cross.pack()
        grad_got, cross.out = tie(grad_got, cross.out)
        cross.hop((1, 2))
    qkv_parts, bias_grad = self_backward(blocks, my_ref, qkv, bias, own_mix, lse, [grad_parts[0]] + grad_got)
    d_table = lax.dot_general(bucket_hot, bias_grad[:, length:], (((0,), (1,)), ((), ())), precision=lax.Precision.HIGHEST)
    d_table = lax.dynamic_update_slice_in_dim(jnp.zeros_like(bias_table), d_table, my * own_heads, 1)
    if fast:
        qkv_parts, mem_part, cross.got = tie(qkv_parts, mem_part, cross.got)
        cross.arrive()
        cross.pack()
        qkv_parts, cross.out, hidden_got = tie(qkv_parts, cross.out, hidden_got)
        cross.hop((2, 1))
        own = own_q + 2 * own_kv
        keep, send, gain_part = slabs(order, self_all, qkv_parts, small, 0, 0, None, 2, own, turned_qkv[0])
        gain_part = gain_part[:, 0]
        view = (-1, blocks * small, own)
        got = swap(send, "dp", 1)
        sides = [(keep.reshape(view), cover((0, view[1]))), (got.reshape(view), cover((0, view[1])))]
        sides = totals(sides, [(0, cross.chunks, [(j * small, (j + 1) * small)]) for j in range(blocks)], 1)
        sides = [sides[0]] + trade(sides, "blk", 1)
        down = turned_dot(my_ref, [hidden_parts[0]] + hidden_got, top_all)
        gain_part, cross.got, sides, wide, down = tie(gain_part, cross.got, sides, wide, down)
        down = lax.psum_scatter(down, "dp", scatter_dimension=0, tiled=True)
        cross.arrive()
        cross.join([(side, cover((total + j * small, total + (j + 1) * small))) for j, side in enumerate(sides)], total + view[1])
        cross.pack(True)
        gain_part, cross.out, d_table, wide, mem_part = tie(gain_part, cross.out, d_table, wide, mem_part)
        cross.hop_deep(2)
        wides = [lax.dynamic_slice_in_dim(wide, (my ^ j) * small, small, 0) for j in range(blocks)]
        wides_got = trade(wides, "blk", 1)
    else:
        attn, gain_part = dot_gain(self_all, jnp.concatenate(qkv_parts, axis=0), turned_qkv[0])
        gain_part = gain_part[:, 0]
    d_gain_self = gain_part / norm_self
    lines = jnp.concatenate([d_gain_self, d_gain_cross, d_gain_ffn, d_table.reshape(-1)]).reshape(-1, LANES)
    mem_blocks = mem_part.reshape(2, blocks, mem_rows, kv_width)
    bit = blocks // 2
    while bit:
        mem_blocks = add16(mem_blocks[:, :bit], swap(mem_blocks[:, bit:], "blk", bit))
        bit //= 2
    mem_grad = mem_blocks[:, 0]
    if fast:
        lines = sum_axis(sum_axis(lines, "dp", 1), "blk", blocks // 2)
        cross.got, lines, mem_grad, wides_got, qkv_parts = tie(cross.got, lines, mem_grad, wides_got, qkv_parts)
        cross.arrive()
        cross.pack(True)
        lines, mem_grad, qkv_parts, cross.out = tie(lines, mem_grad, qkv_parts, cross.out)
        cross.hop_deep(4)
    qkv_got = trade(qkv_parts, "blk", 1)
    d_memory = dot32(mem_grad[0], cross_key, NT) + dot32(mem_grad[1], cross_value, NT)
    if fast:
        qkv_got, d_memory = tie(qkv_got, d_memory)
    d_block_in, _, _, _ = norm_grad(
        grad_self, [qkv_parts[0]] + qkv_got, turned_qkv, block_in[0], norm_self, [], own_q + 2 * own_kv
    )
    if fast:
        lines = sum_axis(lines, "dp", lax.axis_size("dp") // 2, 2).reshape(-1)
        dw_gate, dw_up = place(my_ref, [wides[0]] + wides_got)
        dw_down = down[0].astype(F32)
        d_block_in, cross.got, lines, dw_gate, dw_up, dw_down = tie(d_block_in, cross.got, lines, dw_gate, dw_up, dw_down)
        cross.arrive()
    else:
        lines = sum_axis(sum_axis(lines, "dp", lax.axis_size("dp") // 2), "blk", blocks // 2).reshape(-1)
    gain_self, gain_cross, gain_ffn = lines[:d], lines[d : 2 * d], lines[2 * d : 3 * d]
    table_sum = lines[3 * d :].reshape(bias_table.shape)
    if fast:
        shapes = [(small, d), (small, d), (small, kv_width), (small, kv_width), (small, d)]
        outs, row = [], 0
        for number, (_, width) in enumerate(shapes):
            for k in range(width // SLAB):
                outs.append((row, small, number, k * SLAB))
                row += small
        shapes += [(small, d), (small, kv_width), (small, kv_width)]
        dealt = [(j, row + j * small, small, ((5, own_q), (6, own_kv), (7, own_kv))) for j in range(blocks)]
        dw_co, dw_cq, dw_ck, dw_cv, dw_o, dw_q, dw_k, dw_v = finish(my_ref, cross.pieces, shapes, outs, dealt)
        ffn_outs = (dw_gate, dw_up, dw_down)
    else:
        dw_co = sum_rows(dot32(cross_mix, cross_grad, TN).astype(BF16), 0)
        dw_cq = sum_rows(dot32(cross_in, cq_grad, TN).astype(BF16), 1)
        dw_ck = sum_rows(dot32(mem_all, mem_part[0], TN).astype(BF16), 0)
        dw_cv = sum_rows(dot32(mem_all, mem_part[1], TN).astype(BF16), 1)
        dw_o = sum_rows(turn_rows(dot32(jnp.concatenate(mixes, axis=1), self_grad, TN).astype(BF16), own_q), 0)
        dw_q, dw_k, dw_v = [
            sum_rows(lax.dynamic_update_slice_in_dim(jnp.zeros((d, width), BF16), attn[:, low : low + width // blocks], my * (width // blocks), 1), 0)
            for width, low in ((blocks * own_q, 0), (kv_width, own_q), (kv_width, own_q + own_kv))
        ]
    return (
        block_out[None],
        d_block_in[None],
        d_memory[None],
        table_sum,
        gain_self,
        dw_q,
        dw_k,
        dw_v,
        dw_o,
        gain_cross,
        dw_cq,
        dw_ck,
        dw_cv,
        dw_co,
        gain_ffn,
        *ffn_outs,
    )


def solution(mesh):
    rows = P("dp", "blk", None)
    split = P(("dp", "blk"), None)
    whole = P()
    return jax.shard_map(
        body,
        mesh=mesh,
        in_specs=(rows, rows, P("dp"), P("dp", None)) + (whole,) * 16 + (rows,),
        out_specs=(rows, rows, rows, whole, whole)
        + (split,) * 4
        + (whole,)
        + (split,) * 4
        + (whole,)
        + (split,) * 3,
        check_vma=False,
    )
```

```python
import functools

import jax
import jax.numpy as jnp
from jax import lax
from jax.experimental import pallas as pl
from jax.experimental.pallas import tpu as pltpu
from jax.sharding import PartitionSpec as P

HEAD_DIM = 64
EPSILON = 1e-06
NEGATIVE = -1e30
SCALE = HEAD_DIM ** (-0.5)
LANES = 128
PAIR = 2 * HEAD_DIM
SLAB = 512
STEP_ELEMENTS = 768 * 1024
F32 = jnp.float32
BF16 = jnp.bfloat16
VMEM_SMALL = 28 * 1024 * 1024
VMEM_LARGE = 56 * 1024 * 1024

NT = (((1,), (1,)), ((), ()))
NN = (((1,), (0,)), ((), ()))
TN = (((0,), (0,)), ((), ()))


def dot32(a, b, dims=NN):
    return lax.dot_general(a, b, dims, preferred_element_type=F32)


def swap(x, axis, bit):
    return lax.ppermute(x, axis, [(i, i ^ bit) for i in range(lax.axis_size(axis))])


def trade(parts, axis, bit):
    return [swap(part, axis, k * bit) for k, part in enumerate(parts) if k]


def tie(*groups):
    return lax.optimization_barrier(groups)


def row_blocks(x, count):
    length = x.shape[0] // count
    return [x[k * length : (k + 1) * length] for k in range(count)]


def column_blocks(x, count):
    width = x.shape[1] // count
    return [x[:, k * width : (k + 1) * width] for k in range(count)]


def add16(a, b):
    return (a.astype(F32) + b.astype(F32)).astype(BF16)


def sum_axis(x, axis, last, bit=1):
    while bit <= last:
        x = x + swap(x, axis, bit)
        bit *= 2
    return x


def sum_rows(x, first_blk_bit):
    dp_bits = lax.axis_size("dp").bit_length() - 1
    blk_bits = lax.axis_size("blk").bit_length() - 1
    rest = [("dp", k) for k in reversed(range(dp_bits))] + [("blk", k) for k in reversed(range(blk_bits))]
    rows, width = x.shape
    x = x.reshape((2,) * len(rest) + (rows >> len(rest), width))
    order = [("dp", 0)]
    order += [("blk", (first_blk_bit + k) % blk_bits) for k in range(blk_bits)]
    order += [("dp", k) for k in range(1, dp_bits)]
    for axis, k in order:
        place = rest.index((axis, k))
        mine = (lax.axis_index(axis) >> k) & 1
        out = lax.dynamic_index_in_dim(x, 1 - mine, place, keepdims=False)
        keep = lax.dynamic_index_in_dim(x, mine, place, keepdims=False)
        got = swap(out, axis, 1 << k)
        rest.pop(place)
        x = keep.astype(F32) + got.astype(F32)
        if rest:
            x = x.astype(BF16)
    return x


def stacked(ref, kv):
    low = kv * PAIR
    return jnp.concatenate([ref[:, low : low + HEAD_DIM], ref[:, low + HEAD_DIM : low + PAIR]], axis=0)


def unstack(ref, kv, columns):
    length = columns.shape[1] // 2
    rows = columns.T
    low = kv * PAIR
    ref[:, low : low + HEAD_DIM] = rows[:length].astype(ref.dtype)
    ref[:, low + HEAD_DIM : low + PAIR] = rows[length:].astype(ref.dtype)


def spread_bias(bias_ref, tile_ref):
    heads, width = bias_ref.shape
    for h in range(heads):
        line = jnp.broadcast_to(bias_ref[h : h + 1, :], (LANES, width))
        tile_ref[h] = pltpu.roll(line, 0, 1, stride=1, stride_axis=0)


def bias_tile(tile_ref, kv, start, length):
    heads = []
    for g in range(2):
        parts = [
            tile_ref[2 * kv + g, :, pl.ds(pl.multiple_of(start - LANES * m, LANES), length)]
            for m in range(length // LANES)
        ]
        heads.append(jnp.concatenate(parts, axis=0))
    return jnp.concatenate(heads, axis=1)


def head_columns(kv_local, kv):
    return kv * PAIR, kv_local * PAIR + kv * HEAD_DIM, kv_local * (PAIR + HEAD_DIM) + kv * HEAD_DIM


def two_heads(ref, rows, low):
    return jnp.concatenate([ref[rows, low : low + HEAD_DIM], ref[rows, low + HEAD_DIM : low + PAIR]], axis=0)


def self_forward_kernel(blocks, kv_local, my_ref, qkv_ref, bias_ref, *refs):
    mix_refs, (lse_ref, tile_ref, top_ref, sum_ref, acc_ref) = refs[:blocks], refs[blocks:]
    a = pl.program_id(0)
    length = qkv_ref.shape[0] // blocks
    my = my_ref[0]
    mine = my ^ a

    @pl.when(a == 0)
    def _():
        spread_bias(bias_ref, tile_ref)

    rows = pl.ds(pl.multiple_of(a * length, length), length)
    top_ref[...] = jnp.full_like(top_ref, NEGATIVE)
    sum_ref[...] = jnp.zeros_like(sum_ref)
    acc_ref[...] = jnp.zeros_like(acc_ref)
    for b in range(blocks):
        source = my ^ b
        keys_at = slice(b * length, (b + 1) * length)

        @pl.when(source <= mine)
        def _(source=source, keys_at=keys_at):
            start = length + length * (mine - source)
            for kv in range(kv_local):
                q_at, k_at, v_at = head_columns(kv_local, kv)
                qq = two_heads(qkv_ref, rows, q_at)
                keys = qkv_ref[keys_at, k_at : k_at + HEAD_DIM]
                values = qkv_ref[keys_at, v_at : v_at + HEAD_DIM]
                scores = dot32(keys, qq, NT) * SCALE + bias_tile(tile_ref, kv, start, length)
                old = top_ref[kv]
                new = jnp.maximum(old, jnp.max(scores, axis=0, keepdims=True))
                weights = jnp.exp(scores - new)
                shrink = jnp.exp(old - new)
                top_ref[kv] = new
                sum_ref[kv] = sum_ref[kv] * shrink + jnp.sum(weights, axis=0, keepdims=True)
                acc_ref[kv] = acc_ref[kv] * shrink + dot32(values, weights.astype(BF16), TN)

    for kv in range(kv_local):
        lse_ref[0, kv] = top_ref[kv] + jnp.log(sum_ref[kv])
    for b, mix_ref in enumerate(mix_refs):

        @pl.when(a == b)
        def _(mix_ref=mix_ref):
            for kv in range(kv_local):
                unstack(mix_ref, kv, acc_ref[kv] / sum_ref[kv])


def self_backward_kernel(blocks, kv_local, my_ref, qkv_ref, bias_ref, lse_ref, *refs):
    mix_refs, grad_refs, out_refs = refs[:blocks], refs[blocks : 2 * blocks], refs[2 * blocks : 3 * blocks]
    dbias_ref, tile_ref, diag_ref, dq_ref, dk_ref, dv_ref, grad_ref, mix_ref = refs[3 * blocks :]
    a = pl.program_id(0)
    length = qkv_ref.shape[0] // blocks
    width = bias_ref.shape[1]
    my = my_ref[0]
    mine = my ^ a

    @pl.when(a == 0)
    def _():
        spread_bias(bias_ref, tile_ref)
        diag_ref[...] = jnp.zeros_like(diag_ref)
        dk_ref[...] = jnp.zeros_like(dk_ref)
        dv_ref[...] = jnp.zeros_like(dv_ref)

    rows = pl.ds(pl.multiple_of(a * length, length), length)
    every = slice(0, length)
    for b in range(blocks):

        @pl.when(a == b)
        def _(b=b):
            grad_ref[...] = grad_refs[b][...]
            mix_ref[...] = mix_refs[b][...]

    dq_ref[...] = jnp.zeros_like(dq_ref)
    deltas = []
    for kv in range(kv_local):
        both = two_heads(grad_ref, every, kv * PAIR).astype(F32) * two_heads(mix_ref, every, kv * PAIR).astype(F32)
        deltas.append(jnp.sum(both.T, axis=0, keepdims=True))
    for b in range(blocks):
        source = my ^ b
        keys_at = slice(b * length, (b + 1) * length)

        @pl.when(source <= mine)
        def _(source=source, keys_at=keys_at):
            start = length + length * (mine - source)
            for kv in range(kv_local):
                q_at, k_at, v_at = head_columns(kv_local, kv)
                qq = two_heads(qkv_ref, rows, q_at)
                dd = two_heads(grad_ref, every, q_at)
                keys = qkv_ref[keys_at, k_at : k_at + HEAD_DIM]
                values = qkv_ref[keys_at, v_at : v_at + HEAD_DIM]
                scores = dot32(keys, qq, NT) * SCALE + bias_tile(tile_ref, kv, start, length)
                probs = jnp.exp(scores - lse_ref[0, kv])
                dv_ref[kv, keys_at, :] += dot32(probs.astype(BF16), dd)
                change = dot32(values, dd, NT) - deltas[kv]
                ds = (probs * change).astype(BF16)
                dk_ref[kv, keys_at, :] += dot32(ds, qq)
                dq_ref[kv] += dot32(keys, ds, TN)
                ds = ds.astype(F32)
                for g in range(2):
                    for m in range(length // LANES):
                        where = pl.ds(pl.multiple_of(start - LANES * m, LANES), length)
                        diag_ref[2 * kv + g, :, where] += ds[m * LANES : (m + 1) * LANES, g * length : (g + 1) * length]

    for b in range(blocks):

        @pl.when(a == b)
        def _(out_ref=out_refs[b]):
            for kv in range(kv_local):
                back = (dq_ref[kv] * SCALE).T.astype(BF16)
                out_ref[:, kv * PAIR : kv * PAIR + HEAD_DIM] = back[:length]
                out_ref[:, kv * PAIR + HEAD_DIM : (kv + 1) * PAIR] = back[length:]

    @pl.when(a == blocks - 1)
    def _():
        for kv in range(kv_local):
            _, k_at, v_at = head_columns(kv_local, kv)
            for b, out_ref in enumerate(out_refs):
                keys_at = slice(b * length, (b + 1) * length)
                out_ref[:, k_at : k_at + HEAD_DIM] = (dk_ref[kv, keys_at, :] * SCALE).astype(BF16)
                out_ref[:, v_at : v_at + HEAD_DIM] = dv_ref[kv, keys_at, :].astype(BF16)
        for h in range(2 * kv_local):
            part = diag_ref[h]
            half = LANES // 2
            while half:
                part = part[:half] + pltpu.roll(part[half:], width - half, 1)
                half //= 2
            dbias_ref[h : h + 1, :] = part


def cross_forward_kernel(allow_ref, q_ref, k_ref, v_ref, mix_ref, lse_ref):
    allow = allow_ref[...] > 0
    for kv in range(2):
        low = kv * HEAD_DIM
        qq = stacked(q_ref, kv)
        scores = dot32(k_ref[:, low : low + HEAD_DIM], qq, NT) * SCALE
        scores = jnp.where(allow, scores, NEGATIVE)
        top = jnp.max(scores, axis=0, keepdims=True)
        raised = jnp.exp(scores - top)
        total = jnp.sum(raised, axis=0, keepdims=True)
        probs = (raised * (1.0 / total)).astype(BF16)
        unstack(mix_ref, kv, dot32(v_ref[:, low : low + HEAD_DIM], probs, TN))
        lse_ref[kv] = top + jnp.log(total)


def cross_backward_kernel(allow_ref, q_ref, k_ref, v_ref, lse_ref, grad_ref, dq_ref, dkv_ref):
    allow = allow_ref[...] > 0
    for kv in range(2):
        low = kv * HEAD_DIM
        qq = stacked(q_ref, kv)
        dd = stacked(grad_ref, kv)
        keys = k_ref[:, low : low + HEAD_DIM]
        scores = jnp.where(allow, dot32(keys, qq, NT) * SCALE, NEGATIVE)
        probs = jnp.exp(scores - lse_ref[kv])
        change = dot32(v_ref[:, low : low + HEAD_DIM], dd, NT)
        delta = jnp.sum(probs * change, axis=0, keepdims=True)
        ds = (probs * (change - delta)).astype(BF16)
        dkv_ref[1, :, low : low + HEAD_DIM] = dot32(probs.astype(BF16), dd).astype(BF16)
        dkv_ref[0, :, low : low + HEAD_DIM] = (dot32(ds, qq) * SCALE).astype(BF16)
        unstack(dq_ref, kv, dot32(keys, ds, TN) * SCALE)


TINY = pl.CostEstimate(flops=1, transcendentals=0, bytes_accessed=1)


def params(limit=VMEM_SMALL):
    return pltpu.CompilerParams(dimension_semantics=("arbitrary",), vmem_limit_bytes=limit)


def cost(length, keys, heads, passes, moved):
    return pl.CostEstimate(
        flops=2 * length * keys * heads * HEAD_DIM * passes,
        transcendentals=length * keys * heads,
        bytes_accessed=moved,
    )


def lane_block(rows, width):
    return pl.BlockSpec((rows, width), lambda i: (0, i))


def self_forward(blocks, my, qkv, bias):
    tokens, columns = qkv.shape
    length, kv_local, width = tokens // blocks, columns // (2 * PAIR), bias.shape[1]
    q_width = kv_local * PAIR
    return pl.pallas_call(
        functools.partial(self_forward_kernel, blocks, kv_local),
        grid=(blocks,),
        in_specs=[
            pl.BlockSpec(memory_space=pltpu.SMEM),
            pl.BlockSpec((tokens, columns), lambda i: (0, 0)),
            pl.BlockSpec(bias.shape, lambda i: (0, 0)),
        ],
        out_specs=[pl.BlockSpec((length, q_width), lambda i: (0, 0))] * blocks
        + [pl.BlockSpec((1, kv_local, 1, 2 * length), lambda i: (i, 0, 0, 0))],
        out_shape=[jax.ShapeDtypeStruct((length, q_width), BF16)] * blocks
        + [jax.ShapeDtypeStruct((blocks, kv_local, 1, 2 * length), F32)],
        scratch_shapes=[
            pltpu.VMEM((2 * kv_local, LANES, width), F32),
            pltpu.VMEM((kv_local, 1, 2 * length), F32),
            pltpu.VMEM((kv_local, 1, 2 * length), F32),
            pltpu.VMEM((kv_local, HEAD_DIM, 2 * length), F32),
        ],
        compiler_params=params(),
        cost_estimate=TINY,
        name="self_forward",
    )(my, qkv, bias)


def self_backward(blocks, my, qkv, bias, mixes, lse, grads):
    tokens, columns = qkv.shape
    length, kv_local, width = tokens // blocks, columns // (2 * PAIR), bias.shape[1]
    q_width = kv_local * PAIR
    lines = pl.BlockSpec(bias.shape, lambda i: (0, 0))
    *outs, d_bias = pl.pallas_call(
        functools.partial(self_backward_kernel, blocks, kv_local),
        grid=(blocks,),
        in_specs=[
            pl.BlockSpec(memory_space=pltpu.SMEM),
            pl.BlockSpec((tokens, columns), lambda i: (0, 0)),
            lines,
            pl.BlockSpec((1, kv_local, 1, 2 * length), lambda i: (i, 0, 0, 0)),
        ]
        + [pl.BlockSpec((length, q_width), lambda i: (0, 0))] * (2 * blocks),
        out_specs=[pl.BlockSpec((length, columns), lambda i: (0, 0))] * blocks + [lines],
        out_shape=[jax.ShapeDtypeStruct((length, columns), BF16)] * blocks + [jax.ShapeDtypeStruct(bias.shape, F32)],
        scratch_shapes=[
            pltpu.VMEM((2 * kv_local, LANES, width), F32),
            pltpu.VMEM((2 * kv_local, LANES, width), F32),
            pltpu.VMEM((kv_local, HEAD_DIM, 2 * length), F32),
            pltpu.VMEM((kv_local, tokens, HEAD_DIM), F32),
            pltpu.VMEM((kv_local, tokens, HEAD_DIM), F32),
            pltpu.VMEM((length, q_width), BF16),
            pltpu.VMEM((length, q_width), BF16),
        ],
        compiler_params=params(),
        cost_estimate=TINY,
        name="self_backward",
    )(my, qkv, bias, lse, *mixes, *grads)
    return outs, d_bias


def cross_forward(allow, q, k, v):
    length, keys, kv_heads = q.shape[0], k.shape[0], k.shape[1] // HEAD_DIM
    return pl.pallas_call(
        cross_forward_kernel,
        grid=(kv_heads // 2,),
        in_specs=[
            pl.BlockSpec((keys, 1), lambda i: (0, 0)),
            lane_block(length, 2 * PAIR),
            lane_block(keys, PAIR),
            lane_block(keys, PAIR),
        ],
        out_specs=[
            lane_block(length, 2 * PAIR),
            pl.BlockSpec((2, 1, 2 * length), lambda i: (i, 0, 0)),
        ],
        out_shape=[
            jax.ShapeDtypeStruct(q.shape, BF16),
            jax.ShapeDtypeStruct((kv_heads, 1, 2 * length), F32),
        ],
        compiler_params=params(),
        cost_estimate=TINY,
        name="cross_forward",
    )(allow, q, k, v)


def cross_backward(allow, q, k, v, lse, grad):
    length, keys, kv_heads = q.shape[0], k.shape[0], k.shape[1] // HEAD_DIM
    return pl.pallas_call(
        cross_backward_kernel,
        grid=(kv_heads // 2,),
        in_specs=[
            pl.BlockSpec((keys, 1), lambda i: (0, 0)),
            lane_block(length, 2 * PAIR),
            lane_block(keys, PAIR),
            lane_block(keys, PAIR),
            pl.BlockSpec((2, 1, 2 * length), lambda i: (i, 0, 0)),
            lane_block(length, 2 * PAIR),
        ],
        out_specs=[
            lane_block(length, 2 * PAIR),
            pl.BlockSpec((2, keys, PAIR), lambda i: (0, 0, i)),
        ],
        out_shape=[
            jax.ShapeDtypeStruct(q.shape, BF16),
            jax.ShapeDtypeStruct((2,) + k.shape, BF16),
        ],
        compiler_params=params(),
        cost_estimate=TINY,
        name="cross_backward",
    )(allow, q, k, v, lse, grad)


def slab_kernel(kind, later, x_count, g_count, gained, order_ref, *refs):
    xs, gs = refs[:x_count], refs[x_count : x_count + g_count]
    turned_ref, whole_ref = refs[-2:]
    keep_ref, send_ref = refs[-5:-3] if gained else refs[-4:-2]
    slab = pl.program_id(0)
    kind = jnp.where(slab < later, 0, 1) if kind is None else kind

    @pl.when(slab == 0)
    def _():
        low = 0
        for x in xs:
            turned_ref[low : low + x.shape[1], :] = x[...].T
            low += x.shape[1]

    chunks, rows, width = whole_ref.shape
    g = gs[0][...] if g_count == 1 else jnp.concatenate([ref[...] for ref in gs], axis=0)
    full = dot32(turned_ref[...], g)
    whole_ref[...] = full.reshape(chunks, rows, width)
    half = chunks // 2
    for c in range(half):
        keep_ref[c] = whole_ref[order_ref[kind, c]].astype(BF16)
        send_ref[c] = whole_ref[order_ref[kind, half + c]].astype(BF16)
    if gained:
        refs[-3][...] = jnp.sum(full * refs[x_count + g_count][...].astype(F32), axis=1, keepdims=True)


def slabs(order, x, g, total, at, later, buffers, kind=None, slab=SLAB, weight=None):
    xs = x if isinstance(x, list) else [x]
    tokens, features = xs[0].shape[0], sum(part.shape[1] for part in xs)
    chunks = order.shape[1]
    rows = features // chunks
    gs = g if isinstance(g, list) else [g]
    if len(gs) > 1:
        count, g_specs = 1, whole_blocks(gs)
    elif g.ndim == 3:
        count, g_specs = g.shape[0], [pl.BlockSpec((None, tokens, slab), lambda i: (i, 0, 0))]
    else:
        count, g_specs = g.shape[1] // slab, [pl.BlockSpec((tokens, slab), lambda i: (0, i))]
    assert at % rows == 0 and features % chunks == 0 and rows % 8 == 0
    out = pl.BlockSpec((chunks // 2, rows, slab), lambda i: (0, at // rows + i, 0))
    shapes = [jax.ShapeDtypeStruct((chunks // 2, total, slab), BF16)] * 2
    outs = [out, out]
    extra = [] if buffers is None else list(buffers)
    first = 1 + len(xs) + len(gs)
    weights = []
    if weight is not None:
        weights = [weight]
        shapes.append(jax.ShapeDtypeStruct((features, 1), F32))
        outs.append(pl.BlockSpec((features, 1), lambda i: (0, 0)))
    return pl.pallas_call(
        functools.partial(slab_kernel, kind, later, len(xs), len(gs), weight is not None),
        grid=(count,),
        in_specs=[pl.BlockSpec(memory_space=pltpu.SMEM)]
        + whole_blocks(xs)
        + g_specs
        + whole_blocks(weights)
        + [pl.BlockSpec(memory_space=pl.ANY)] * len(extra),
        out_specs=outs,
        out_shape=shapes,
        scratch_shapes=[pltpu.VMEM((features, tokens), BF16), pltpu.VMEM((chunks, rows, slab), F32)],
        input_output_aliases={first: 0, first + 1: 1} if extra else {},
        compiler_params=params(VMEM_LARGE),
        cost_estimate=TINY,
        name="slabs",
    )(order, *xs, *gs, *weights, *extra)


def cover(*ranges):
    held, row = [], 0
    for low, high in ranges:
        held.append((low, high, row))
        row += high - low
    return held


def add_range(sources, refs, low, high):
    total = None
    for number, segments in sources:
        for start, stop, row in segments:
            if start <= low and high <= stop:
                part = refs[number][:, row + low - start : row + high - start, :].astype(F32)
                total = part if total is None else total + part
    return total


def cut_points(pieces, low, high):
    marks = {low, high}
    for _, segments in pieces:
        marks |= {m for start, stop, _ in segments for m in (start, stop) if low < m < high}
    marks = sorted(marks)
    return list(zip(marks[:-1], marks[1:]))


def total_kernel(plan, *refs):
    inputs, results = refs[: -len(plan)], refs[-len(plan) :]
    for (sources, writes), result in zip(plan, results):
        for row, low, high in writes:
            result[:, row : row + high - low, :] = add_range(sources, inputs, low, high).astype(result.dtype)


def totals(pieces, groups, steps):
    plan, specs, arrays, shapes, outs = [], [], [], [], []
    width = pieces[0][0].shape[2]
    for first, count, ranges in groups:
        step = count // steps
        sources = []
        for array, segments in pieces:
            sources.append((len(arrays), segments))
            arrays.append(array)
            specs.append(pl.BlockSpec((step,) + array.shape[1:], lambda i, low=first // step: (low + i, 0, 0)))
        writes, rows = [], 0
        for low, high in ranges:
            for a, b in cut_points(pieces, low, high):
                writes.append((rows, a, b))
                rows += b - a
        plan.append((sources, writes))
        outs.append(pl.BlockSpec((step, rows, width), lambda i: (i, 0, 0)))
        shapes.append(jax.ShapeDtypeStruct((count, rows, width), BF16))
    return pl.pallas_call(
        functools.partial(total_kernel, plan),
        grid=(steps,),
        in_specs=specs,
        out_specs=outs,
        out_shape=shapes,
        compiler_params=params(VMEM_LARGE),
        cost_estimate=TINY,
        name="totals",
    )(*arrays)


def finish_kernel(sources, outs, dealt, my_ref, *refs):
    inputs, results = refs[: len(sources)], refs[len(sources) :]
    for row, rows, number, column in outs:
        results[number][:, column : column + SLAB] = add_range(sources, inputs, row, row + rows)[0]
    for j, row, rows, parts in dealt:
        block = add_range(sources, inputs, row, row + rows)[0]
        low = 0
        for number, width in parts:
            columns = pl.ds(pl.multiple_of((my_ref[0] ^ j) * width, LANES), width)
            results[number][:, columns] = block[:, low : low + width]
            low += width


def finish(my, pieces, shapes, outs, dealt):
    sources = [(number, segments) for number, (_, segments) in enumerate(pieces)]
    return pl.pallas_call(
        functools.partial(finish_kernel, sources, outs, dealt),
        grid=(1,),
        in_specs=[pl.BlockSpec(memory_space=pltpu.SMEM)]
        + [pl.BlockSpec((1,) + array.shape[1:], lambda i: (0, 0, 0)) for array, _ in pieces],
        out_specs=[pl.BlockSpec(shape, lambda i: (0, 0)) for shape in shapes],
        out_shape=[jax.ShapeDtypeStruct(shape, F32) for shape in shapes],
        compiler_params=params(VMEM_LARGE),
        cost_estimate=TINY,
        name="finish",
    )(my, *[array for array, _ in pieces])


def pair_dot_kernel(my_ref, x_ref, *refs):
    gs, result = refs[:-1], refs[-1]
    x = jnp.concatenate([x_ref[my_ref[0] ^ j] for j in range(len(gs))], axis=0)
    g = jnp.concatenate([ref[...] for ref in gs], axis=0)
    result[...] = dot32(x, g, TN).astype(BF16)


def whole_blocks(arrays):
    return [pl.BlockSpec(a.shape, lambda i, n=a.ndim: (0,) * n) for a in arrays]


def pair_dot(my, x, gs):
    features, width = x.shape[1], gs[0].shape[1]
    x = x.reshape(len(gs), -1, features)
    return pl.pallas_call(
        pair_dot_kernel,
        grid=(1,),
        in_specs=[pl.BlockSpec(memory_space=pltpu.SMEM)] + whole_blocks([x, *gs]),
        out_specs=pl.BlockSpec((features, width), lambda i: (0, 0)),
        out_shape=jax.ShapeDtypeStruct((features, width), BF16),
        compiler_params=params(),
        cost_estimate=TINY,
        name="pair_dot",
    )(my, x, *gs)


def dot_gain_kernel(x_ref, g_ref, w_ref, out_ref, gain_ref):
    full = dot32(x_ref[...], g_ref[...], TN)
    out_ref[...] = full.astype(BF16)
    gain_ref[...] = jnp.sum(full * w_ref[...].astype(F32), axis=1, keepdims=True)


def dot_gain(x, g, w):
    features, width = w.shape
    return pl.pallas_call(
        dot_gain_kernel,
        grid=(1,),
        in_specs=whole_blocks([x, g, w]),
        out_specs=[pl.BlockSpec((features, width), lambda i: (0, 0)), pl.BlockSpec((features, 1), lambda i: (0, 0))],
        out_shape=[jax.ShapeDtypeStruct((features, width), BF16), jax.ShapeDtypeStruct((features, 1), F32)],
        compiler_params=params(),
        cost_estimate=TINY,
        name="dot_gain",
    )(x, g, w)


def add_norm_kernel(count, has_next, *refs):
    xs, ws = refs[:count], refs[count : 2 * count]
    base_ref, gain_ref = refs[2 * count : 2 * count + 2]
    total = base_ref[...].astype(F32)
    for x, w in zip(xs, ws):
        total = total + dot32(x[...], w[...])
    normed = (total * inverse_rms(total) * gain_ref[...]).astype(BF16)
    if has_next:
        next_ref, total_ref, normed_ref, out_ref = refs[2 * count + 2 :]
        out_ref[...] = dot32(normed, next_ref[...]).astype(BF16)
    else:
        total_ref, normed_ref = refs[2 * count + 2 :]
    total_ref[...] = total
    normed_ref[...] = normed


def add_norm(base, xs, ws, gain, after=None):
    shapes = [jax.ShapeDtypeStruct(base.shape, F32), jax.ShapeDtypeStruct(base.shape, BF16)]
    inputs = [*xs, *ws, base, gain[None]]
    if after is not None:
        inputs.append(after)
        shapes.append(jax.ShapeDtypeStruct((base.shape[0], after.shape[1]), BF16))
    return pl.pallas_call(
        functools.partial(add_norm_kernel, len(xs), after is not None),
        grid=(1,),
        in_specs=whole_blocks(inputs),
        out_specs=whole_blocks(shapes),
        out_shape=shapes,
        compiler_params=params(),
        cost_estimate=TINY,
        name="add_norm",
    )(*inputs)


def norm_grad_kernel(count, nexts, *refs):
    gs, ws = refs[:count], refs[count : 2 * count]
    x_ref, gain_ref, base_ref = refs[2 * count : 2 * count + 3]
    after = refs[2 * count + 3 : 2 * count + 3 + nexts]
    grad_ref, low_ref, gain_grad_ref = refs[2 * count + 3 + nexts : 2 * count + 6 + nexts]
    outs, acc_ref = refs[2 * count + 6 + nexts : -1], refs[-1]
    step = pl.program_id(0)

    @pl.when(step == 0)
    def _():
        acc_ref[...] = jnp.zeros_like(acc_ref)

    part = None
    for g, w in zip(gs, ws):
        term = dot32(g[...], w[...], NT)
        part = term if part is None else part + term
    acc_ref[...] += part

    @pl.when(step == pl.num_programs(0) - 1)
    def _():
        total = acc_ref[...]
        x = x_ref[...].astype(F32)
        d_x, d_gain = norm_back(x, inverse_rms(x), gain_ref[...], total)
        grad = base_ref[...].astype(F32) + d_x
        low = grad.astype(BF16)
        grad_ref[...] = grad
        low_ref[...] = low
        gain_grad_ref[...] = d_gain[None]
        for w, out in zip(after, outs):
            out[...] = dot32(low, w[...], NT).astype(BF16)


def norm_grad(base, gs, ws, x, gain, after, tile):
    length, width = x.shape
    inner = gs[0].shape[1]
    fixed = [x, gain[None], base, *after]
    shapes = [
        jax.ShapeDtypeStruct(x.shape, F32),
        jax.ShapeDtypeStruct(x.shape, BF16),
        jax.ShapeDtypeStruct((1, width), F32),
    ] + [jax.ShapeDtypeStruct((length, w.shape[0]), BF16) for w in after]
    grad, low, d_gain, *outs = pl.pallas_call(
        functools.partial(norm_grad_kernel, len(gs), len(after)),
        grid=(inner // tile,),
        in_specs=[pl.BlockSpec((length, tile), lambda i: (0, i))] * len(gs)
        + [pl.BlockSpec((width, tile), lambda i: (0, i))] * len(ws)
        + whole_blocks(fixed),
        out_specs=whole_blocks(shapes),
        out_shape=shapes,
        scratch_shapes=[pltpu.VMEM((length, width), F32)],
        compiler_params=params(),
        cost_estimate=TINY,
        name="norm_grad",
    )(*gs, *ws, *fixed)
    return grad, low, d_gain[0], outs


def norm_dot_kernel(count, *refs):
    gain_ref, w_ref, normed_ref, out_ref = refs[count:]
    for k, ref in enumerate(refs[:count]):
        length = ref.shape[0]
        rows = slice(k * length, (k + 1) * length)
        x = ref[...].astype(F32)
        normed = (x * inverse_rms(x) * gain_ref[...]).astype(BF16)
        normed_ref[rows, :] = normed
        out_ref[rows, :] = dot32(normed, w_ref[...]).astype(BF16)


def norm_dot(xs, gain, w):
    rows = len(xs) * xs[0].shape[0]
    shapes = [(rows, w.shape[0]), (rows, w.shape[1])]
    return pl.pallas_call(
        functools.partial(norm_dot_kernel, len(xs)),
        grid=(1,),
        in_specs=whole_blocks([*xs, gain, w]),
        out_specs=[pl.BlockSpec(shape, lambda i: (0, 0)) for shape in shapes],
        out_shape=[jax.ShapeDtypeStruct(shape, BF16) for shape in shapes],
        compiler_params=params(),
        cost_estimate=TINY,
        name="norm_dot",
    )(*xs, gain, w)


def turn_kernel(my_ref, x_ref, *refs):
    results, chunk_ref = refs[:-1], refs[-1]
    count = len(results)
    chunk_ref[...] = x_ref[...].astype(F32).T.reshape(chunk_ref.shape)
    for j, result in enumerate(results):
        for k in range(result.shape[0]):
            result[k] = chunk_ref[k * count + (my_ref[0] ^ j)].astype(BF16)


def turn_chunks(my, x, blocks, devices):
    tokens, features = x.shape
    shape = (devices // blocks, features // devices, tokens)
    return pl.pallas_call(
        turn_kernel,
        grid=(1,),
        in_specs=[pl.BlockSpec(memory_space=pltpu.SMEM)] + whole_blocks([x]),
        out_specs=[pl.BlockSpec(shape, lambda i: (0, 0, 0))] * blocks,
        out_shape=[jax.ShapeDtypeStruct(shape, BF16)] * blocks,
        scratch_shapes=[pltpu.VMEM((devices, features // devices, tokens), F32)],
        compiler_params=params(),
        cost_estimate=TINY,
        name="turn_chunks",
    )(my, x)


def turned_dot_kernel(count, my_ref, *refs):
    xs, (g_ref, result) = refs[:count], refs[count:]
    chunks, rows, tokens = xs[0].shape
    total = None
    for j, ref in enumerate(xs):
        x = ref[...].astype(F32).reshape(chunks * rows, tokens).astype(BF16)
        term = dot32(x, g_ref[my_ref[0] ^ j])
        total = term if total is None else total + term
    result[...] = total.reshape(result.shape).astype(BF16)


def turned_dot(my, xs, g):
    chunks, rows, tokens = xs[0].shape
    width = g.shape[1]
    g = g.reshape(len(xs), tokens, width)
    return pl.pallas_call(
        functools.partial(turned_dot_kernel, len(xs)),
        grid=(1,),
        in_specs=[pl.BlockSpec(memory_space=pltpu.SMEM)] + whole_blocks([*xs, g]),
        out_specs=pl.BlockSpec((chunks, rows, width), lambda i: (0, 0, 0)),
        out_shape=jax.ShapeDtypeStruct((chunks, rows, width), BF16),
        compiler_params=params(),
        cost_estimate=TINY,
        name="turned_dot",
    )(my, *xs, g)


def place_kernel(my_ref, *refs):
    parts, results = refs[:-2], refs[-2:]
    per_half = len(parts) // 2
    share = parts[0].shape[1]
    for j, part in enumerate(parts):
        owner = my_ref[0] ^ j
        for number, result in enumerate(results):

            @pl.when(owner // per_half == number)
            def _(part=part, result=result, number=number, owner=owner):
                columns = pl.ds(pl.multiple_of((owner - number * per_half) * share, LANES), share)
                result[:, columns] = part[...].astype(F32)


def place(my, parts):
    shape = (parts[0].shape[0], len(parts) // 2 * parts[0].shape[1])
    return pl.pallas_call(
        place_kernel,
        grid=(1,),
        in_specs=[pl.BlockSpec(memory_space=pltpu.SMEM)] + whole_blocks(parts),
        out_specs=[pl.BlockSpec(shape, lambda i: (0, 0))] * 2,
        out_shape=[jax.ShapeDtypeStruct(shape, F32)] * 2,
        compiler_params=params(VMEM_LARGE),
        cost_estimate=TINY,
        name="place",
    )(my, *parts)


def exchange_order():
    dp, blk = lax.axis_size("dp"), lax.axis_size("blk")
    dp_bits, blk_bits = dp.bit_length() - 1, blk.bit_length() - 1
    mine = lax.axis_index("dp") * blk + lax.axis_index("blk")
    deep = list(range(blk_bits + 1, blk_bits + dp_bits))
    up, down = list(range(blk_bits)), list(reversed(range(blk_bits)))
    tables = []
    for order in (up + deep, down + deep, deep + down):
        order = [blk_bits] + order
        table = []
        for place in range(dp * blk):
            relative = 0
            for k, bit in enumerate(order):
                relative |= ((place >> (len(order) - 1 - k)) & 1) << bit
            table.append(relative)
        tables.append(table)
    return jnp.array(tables, jnp.int32) ^ mine.astype(jnp.int32)


class Halves:
    def __init__(self, keep, got, over_x, over_y):
        self.rows = [(0, keep.shape[1])]
        self.pieces = [(keep, cover(*self.rows)), (got, cover(*self.rows))]
        self.parts, self.chunks = (over_x, over_y), keep.shape[0]

    def pack(self, deep=False):
        half = self.chunks // 2
        parts = [self.rows] if deep else self.parts
        self.out = totals(self.pieces, [(half, half, part) for part in parts], 2 if half > 4 else 1)
        self.chunks = half

    def hop(self, bits):
        self.got = [swap(out, "blk", bit) for out, bit in zip(self.out, bits)]

    def join(self, pieces, end):
        self.pieces += pieces
        self.rows = [(0, end)]

    def hop_deep(self, bit):
        self.got = [swap(self.out[0], "dp", bit)]

    def arrive(self):
        parts = [self.rows] if len(self.got) == 1 else self.parts
        self.pieces += [(array, cover(*part)) for array, part in zip(self.got, parts)]


def turn_rows(x, rows):
    my = lax.axis_index("blk")
    return jnp.concatenate([lax.dynamic_slice_in_dim(x, (my ^ j) * rows, rows, 0) for j in range(lax.axis_size("blk"))], axis=0)


def inverse_rms(x):
    return lax.rsqrt(jnp.mean(x * x, axis=-1, keepdims=True) + EPSILON)


def norm_back(x, inverse, gain, grad):
    scaled = grad * gain
    along = jnp.mean(scaled * x, axis=-1, keepdims=True)
    d_x = inverse * scaled - x * (inverse * inverse * inverse * along)
    return d_x, jnp.sum(grad * (x * inverse), axis=0)


def body(
    block_in,
    memory,
    memory_len,
    cross_mask,
    buckets,
    bias_table,
    norm_self,
    w_query,
    w_key,
    w_value,
    w_out,
    norm_cross,
    cross_query,
    cross_key,
    cross_value,
    cross_out,
    norm_ffn,
    w_gate,
    w_up,
    w_down,
    grad_out,
):
    seq_count, length, model_width = block_in.shape
    assert seq_count == 1
    mem_rows = memory.shape[1]
    mem_total = cross_mask.shape[1]
    blocks = lax.axis_size("blk")
    my = lax.axis_index("blk")
    kv_width = w_key.shape[1]
    head_count = w_query.shape[1] // HEAD_DIM
    bucket_count = bias_table.shape[0]
    my_ref = my.reshape(1).astype(jnp.int32)

    x_parts = [block_in[0]] + trade([block_in[0]] * blocks, "blk", 1)

    own_heads = head_count // blocks
    own_q, own_kv = own_heads * HEAD_DIM, kv_width // blocks
    turned_qkv = [
        jnp.concatenate(
            [
                lax.dynamic_slice_in_dim(w, (my ^ j) * width, width, 1)
                for w, width in ((w_query, own_q), (w_key, own_kv), (w_value, own_kv))
            ],
            axis=1,
        )
        for j in range(blocks)
    ]
    out_turned = [lax.dynamic_slice_in_dim(w_out, (my ^ j) * own_q, own_q, 0) for j in range(blocks)]

    bucket_hot = (buckets[:, None] == jnp.arange(bucket_count)[None, :]).astype(F32)
    own_table = lax.dynamic_slice_in_dim(bias_table, my * own_heads, own_heads, 1)
    dist_bias = lax.dot_general(own_table, bucket_hot, (((0,), (1,)), ((), ())), precision=lax.Precision.HIGHEST)
    bias = jnp.concatenate([jnp.full((own_heads, length), NEGATIVE, F32), dist_bias], axis=1)

    mem_places = jnp.arange(mem_total)
    allowed = (mem_places == 0) | (mem_places < memory_len[0]) & (cross_mask[0] == 1)
    allow = allowed.astype(F32).reshape(blocks, mem_rows)[my ^ jnp.arange(blocks)].reshape(mem_total, 1)

    d_hidden = dot32(grad_out[0], w_down, NT)
    x_parts, mem_own, turned_qkv, out_turned, d_hidden, bias, allow, top_own = tie(
        x_parts, memory[0], turned_qkv, out_turned, d_hidden, bias, allow, grad_out[0]
    )
    top_all = lax.all_gather(top_own, "blk", axis=0, tiled=True)
    mem_all = jnp.concatenate([mem_own] + trade([mem_own] * blocks, "blk", 1), axis=0)
    self_all, qkv = norm_dot(x_parts, norm_self[None], turned_qkv[0])
    *own_mix, lse = self_forward(blocks, my_ref, qkv, bias)
    mem_key = dot32(mem_all, cross_key).astype(BF16)
    mem_value = dot32(mem_all, cross_value).astype(BF16)
    mix_got, mem_key, mem_value = tie(trade(own_mix, "blk", 1), mem_key, mem_value)
    mixes = [own_mix[0]] + mix_got
    after_self, cross_in, cross_q = add_norm(block_in[0], mixes, out_turned, norm_cross, cross_query)
    cross_mix, cross_lse = cross_forward(allow, cross_q, mem_key, mem_value)
    after_cross, ffn_in = add_norm(after_self, [cross_mix], [cross_out], norm_ffn)
    devices = blocks * lax.axis_size("dp")
    d, ff = model_width, w_gate.shape[1]
    share = 2 * ff // blocks
    fast = (
        blocks == 4
        and lax.axis_size("dp") == 8
        and d % (8 * devices) == 0
        and ff % (8 * devices) == 0
        and kv_width == SLAB
        and d % SLAB == 0
        and share % LANES == 0
    )
    gate = dot32(ffn_in, w_gate)
    up = dot32(ffn_in, w_up)
    (act, hidden_full), gated_back = jax.vjp(lambda g, u: (jax.nn.gelu(g, approximate=True), jax.nn.gelu(g, approximate=True) * u), gate, up)
    hidden = hidden_full.astype(BF16)

    ffn_grad = grad_out[0]
    gate_full, up_full = gated_back((jnp.zeros_like(act), d_hidden))
    gate_grad, up_grad = gate_full.astype(BF16), up_full.astype(BF16)
    if fast:
        order = exchange_order()
        turned = order ^ ((my * (devices // blocks)).astype(jnp.int32))
        small, large = d // devices, ff // devices
        d_slabs = d // SLAB
        top_all, ffn_late = tie(top_all, ffn_in)
        ffn_all = lax.all_gather(ffn_late, "blk", axis=0, tiled=True)
        both_grad = jnp.concatenate([gate_grad, up_grad], axis=1)
        shares = [lax.dynamic_slice_in_dim(both_grad, (my ^ j) * share, share, 1) for j in range(blocks)]
        shares, hidden = tie(shares, hidden)
        shares_near = trade(shares[:3], "blk", 1)
        hidden_parts = turn_chunks(my_ref, hidden, blocks, devices)
    else:
        dw_down = sum_rows(dot32(hidden, ffn_grad, TN).astype(BF16), 1)
        ffn_outs = (
            sum_rows(dot32(ffn_in, gate_grad, TN).astype(BF16), 0),
            sum_rows(dot32(ffn_in, up_grad, TN).astype(BF16), 1),
            dw_down,
        )
    tile = ff // 2 if ff % (2 * LANES) == 0 else ff
    grad_cross, cross_grad, d_gain_ffn, (mix_grad,) = norm_grad(
        ffn_grad, [gate_grad, up_grad], [w_gate, w_up], after_cross, norm_ffn, [cross_out], tile
    )
    block_out = (after_cross + dot32(hidden, w_down)).astype(BF16)
    if fast:
        total = 4 * d_slabs * small
        held = slabs(order, cross_mix, cross_grad, total, 0, total, None)
        mix_grad, shares_near, shares[3], hidden_parts, ffn_all, held, block_out = tie(
            mix_grad, shares_near, shares[3], hidden_parts, ffn_all, held, block_out
        )
        share_far = swap(shares[3], "blk", 3)
    cq_grad, mem_part = cross_backward(allow, cross_q, mem_key, mem_value, cross_lse, mix_grad)
    if fast:
        held = slabs(order, cross_in, cq_grad, total, d_slabs * small, total, held)
        held = slabs(order, mem_all, mem_part, total, 2 * d_slabs * small, 0, held)
        cq_grad, mem_part, share_far, held = tie(cq_grad, mem_part, share_far, held)
    grad_self, self_grad, d_gain_cross, grad_parts = norm_grad(
        grad_cross, [cq_grad], [cross_query], after_self, norm_cross, out_turned, d
    )
    grad_got = trade(grad_parts, "blk", 1)
    if fast:
        share_far, held, self_late = tie(share_far, held, self_grad)
        wide = pair_dot(my_ref, ffn_all, [shares[0]] + shares_near + [share_far])
        keep, send = slabs(turned, mixes, self_late, total, 3 * d_slabs * small, 0, held)
        got = swap(send, "dp", 1)
        grad_got, wide, keep, hidden_parts, got = tie(grad_got, wide, keep, hidden_parts, got)
        hidden_got = trade(hidden_parts, "blk", 1)
        wide = lax.psum_scatter(wide, "dp", scatter_dimension=0, tiled=True)
        cross = Halves(keep, got, [(0, total // 2)], [(total // 2, total)])
        cross.pack()
        grad_got, cross.out = tie(grad_got, cross.out)
        cross.hop((1, 2))
    qkv_parts, bias_grad = self_backward(blocks, my_ref, qkv, bias, own_mix, lse, [grad_parts[0]] + grad_got)
    d_table = lax.dot_general(bucket_hot, bias_grad[:, length:], (((0,), (1,)), ((), ())), precision=lax.Precision.HIGHEST)
    d_table = lax.dynamic_update_slice_in_dim(jnp.zeros_like(bias_table), d_table, my * own_heads, 1)
    if fast:
        qkv_parts, mem_part, cross.got = tie(qkv_parts, mem_part, cross.got)
        cross.arrive()
        cross.pack()
        qkv_parts, cross.out, hidden_got, wide = tie(qkv_parts, cross.out, hidden_got, wide)
        cross.hop((2, 1))
        down = turned_dot(my_ref, [hidden_parts[0]] + hidden_got, top_all)
        qkv_parts, down = tie(qkv_parts, down)
        down = lax.psum_scatter(down, "dp", scatter_dimension=0, tiled=True)
        own = own_q + 2 * own_kv
        keep, send, gain_part = slabs(order, self_all, qkv_parts, small, 0, 0, None, 2, own, turned_qkv[0])
        gain_part = gain_part[:, 0]
        view = (-1, blocks * small, own)
        got = swap(send, "dp", 1)
        sides = [(keep.reshape(view), cover((0, view[1]))), (got.reshape(view), cover((0, view[1])))]
        sides = totals(sides, [(0, cross.chunks, [(j * small, (j + 1) * small)]) for j in range(blocks)], 1)
        sides = [sides[0]] + trade(sides, "blk", 1)
        gain_part, cross.got, sides = tie(gain_part, cross.got, sides)
        cross.arrive()
        cross.join([(side, cover((total + j * small, total + (j + 1) * small))) for j, side in enumerate(sides)], total + view[1])
        cross.pack(True)
        gain_part, cross.out, d_table, wide, mem_part = tie(gain_part, cross.out, d_table, wide, mem_part)
        cross.hop_deep(2)
        wides = [lax.dynamic_slice_in_dim(wide, (my ^ j) * small, small, 0) for j in range(blocks)]
        wides_got = trade(wides, "blk", 1)
    else:
        attn, gain_part = dot_gain(self_all, jnp.concatenate(qkv_parts, axis=0), turned_qkv[0])
        gain_part = gain_part[:, 0]
    d_gain_self = gain_part / norm_self
    lines = jnp.concatenate([d_gain_self, d_gain_cross, d_gain_ffn, d_table.reshape(-1)]).reshape(-1, LANES)
    mem_blocks = mem_part.reshape(2, blocks, mem_rows, kv_width)
    bit = blocks // 2
    while bit:
        mem_blocks = add16(mem_blocks[:, :bit], swap(mem_blocks[:, bit:], "blk", bit))
        bit //= 2
    mem_grad = mem_blocks[:, 0]
    if fast:
        lines = sum_axis(sum_axis(lines, "dp", 1), "blk", blocks // 2)
        cross.got, lines, mem_grad, wides_got, qkv_parts = tie(cross.got, lines, mem_grad, wides_got, qkv_parts)
        cross.arrive()
        cross.pack(True)
        lines, mem_grad, qkv_parts, cross.out = tie(lines, mem_grad, qkv_parts, cross.out)
        cross.hop_deep(4)
    qkv_got = trade(qkv_parts, "blk", 1)
    d_memory = dot32(mem_grad[0], cross_key, NT) + dot32(mem_grad[1], cross_value, NT)
    if fast:
        qkv_got, d_memory = tie(qkv_got, d_memory)
    d_block_in, _, _, _ = norm_grad(
        grad_self, [qkv_parts[0]] + qkv_got, turned_qkv, block_in[0], norm_self, [], own_q + 2 * own_kv
    )
    if fast:
        lines = sum_axis(lines, "dp", lax.axis_size("dp") // 2, 2).reshape(-1)
        dw_gate, dw_up = place(my_ref, [wides[0]] + wides_got)
        dw_down = down[0].astype(F32)
        d_block_in, cross.got, lines, dw_gate, dw_up, dw_down = tie(d_block_in, cross.got, lines, dw_gate, dw_up, dw_down)
        cross.arrive()
    else:
        lines = sum_axis(sum_axis(lines, "dp", lax.axis_size("dp") // 2), "blk", blocks // 2).reshape(-1)
    gain_self, gain_cross, gain_ffn = lines[:d], lines[d : 2 * d], lines[2 * d : 3 * d]
    table_sum = lines[3 * d :].reshape(bias_table.shape)
    if fast:
        shapes = [(small, d), (small, d), (small, kv_width), (small, kv_width), (small, d)]
        outs, row = [], 0
        for number, (_, width) in enumerate(shapes):
            for k in range(width // SLAB):
                outs.append((row, small, number, k * SLAB))
                row += small
        shapes += [(small, d), (small, kv_width), (small, kv_width)]
        dealt = [(j, row + j * small, small, ((5, own_q), (6, own_kv), (7, own_kv))) for j in range(blocks)]
        dw_co, dw_cq, dw_ck, dw_cv, dw_o, dw_q, dw_k, dw_v = finish(my_ref, cross.pieces, shapes, outs, dealt)
        ffn_outs = (dw_gate, dw_up, dw_down)
    else:
        dw_co = sum_rows(dot32(cross_mix, cross_grad, TN).astype(BF16), 0)
        dw_cq = sum_rows(dot32(cross_in, cq_grad, TN).astype(BF16), 1)
        dw_ck = sum_rows(dot32(mem_all, mem_part[0], TN).astype(BF16), 0)
        dw_cv = sum_rows(dot32(mem_all, mem_part[1], TN).astype(BF16), 1)
        dw_o = sum_rows(turn_rows(dot32(jnp.concatenate(mixes, axis=1), self_grad, TN).astype(BF16), own_q), 0)
        dw_q, dw_k, dw_v = [
            sum_rows(lax.dynamic_update_slice_in_dim(jnp.zeros((d, width), BF16), attn[:, low : low + width // blocks], my * (width // blocks), 1), 0)
            for width, low in ((blocks * own_q, 0), (kv_width, own_q), (kv_width, own_q + own_kv))
        ]
    return (
        block_out[None],
        d_block_in[None],
        d_memory[None],
        table_sum,
        gain_self,
        dw_q,
        dw_k,
        dw_v,
        dw_o,
        gain_cross,
        dw_cq,
        dw_ck,
        dw_cv,
        dw_co,
        gain_ffn,
        *ffn_outs,
    )


def solution(mesh):
    rows = P("dp", "blk", None)
    split = P(("dp", "blk"), None)
    whole = P()
    return jax.shard_map(
        body,
        mesh=mesh,
        in_specs=(rows, rows, P("dp"), P("dp", None)) + (whole,) * 16 + (rows,),
        out_specs=(rows, rows, rows, whole, whole)
        + (split,) * 4
        + (whole,)
        + (split,) * 4
        + (whole,)
        + (split,) * 3,
        check_vma=False,
    )
```
